128 devices in a mesh: curve: 32 (over x, y, core), slab: 4 (over z).
Axes of the slice: x: 4, y: 4, z: 4, core: 2. Of those that a mesh axis runs over, the one named last changes fastest.
Arguments:
- start_state: float32 [135, 16384], P(None, ('curve', 'slab')), may hold values from -6 to 6
- right_side: float32 [135, 16384], P(None, ('curve', 'slab')), may hold values from -6 to 6
- block_inverse: float32 [135, 135, 16384], P(None, None, ('curve', 'slab')), as said below
- lifted_flux_jacobian: float32 [6, 135, 45], replicated, may hold values from -0.875 to 0.875
- face_weight: float32 [6, 16384], P(None, ('curve', 'slab')), may hold values from 0.1 to 0.4
- dep_level: int32 [16384], P(('curve', 'slab')), may hold values from 0 to 7
- face_link: int32 [6, 16384], P(None, ('curve', 'slab')), may hold values from -1 to 127, as said below
- send_list: int32 [8, 65536], P(None, ('curve', 'slab')), may hold values from 0 to 768, as said below
- recv_list: int32 [8, 65536], P(None, ('curve', 'slab')), may hold values from 0 to 768, as said below
Outputs:
- forward_state: float32 [135, 16384], P(None, ('curve', 'slab'))
- swept_state: float32 [135, 16384], P(None, ('curve', 'slab'))
The draws below stay inside these ranges and needn't reach their ends.
Inputs may be any that keep to these rules, and one draw needn't show every extreme that they name: `block_inverse`: A dense 135 x 135 matrix for each element. `face_link`: for face d of element k of a device, the index on the same device of the element across that face, or -1 where that element lies on another device or outside the domain; links are mutual. `send_list`: A device's shard holds, for each level, 4 slots for each destination device in order; an entry d * 128 + k names face d of the device's local element k, and 768 marks an empty slot. Non-empty slots go only to devices whose curve index differs from the sender's by at most one. In every draw some device fills all 4 slots to one destination at every level. `recv_list`: A device's shard holds, for each level, 4 slots for each source device in order; slot j from source t names the face index at which t's slot j toward this device arrives, empty (768) exactly where that send slot is empty. Over all levels no face appears twice in one device's shard. Non-empty slots come only from devices whose curve index differs by at most one.
All inputs are finite; a program needn't handle non-finite values.
Results may differ from the reference program's by a relative error of at most 0.0003.
Values sent between devices are 32-bit elements; how exact they have to be, the bound alone decides.
A program may use at most 64 MiB of HBM per device.

```python
import math
import jax
import jax.numpy as jnp
from jax import lax

VARS = 5
LEVELS = 8
LA = 4
LC = 4
BLOCK = 135
TRACE = 45
EL = 128
CAP = 4
ELEMENTS = 16384
N_CURVE = 32
N_SLAB = 4
DEVICES = 128


def layout(key):
    base = jax.random.fold_in(key, 7)
    shifts = jax.random.randint(jax.random.fold_in(base, 1), (DEVICES, LA, LC), 0, LEVELS).astype(jnp.int32)
    turn_start = jax.random.randint(jax.random.fold_in(base, 2), (1,), 0, N_SLAB).astype(jnp.int32)
    turns = ((jnp.arange(N_CURVE, dtype=jnp.int32) + turn_start) % N_SLAB).astype(jnp.int32)
    scores = jax.random.randint(jax.random.fold_in(base, 3), (DEVICES, EL), 0, 1 << 18).astype(jnp.int32) * EL + jnp.arange(EL, dtype=jnp.int32)[None, :]
    places = jnp.argsort(scores, axis=1).astype(jnp.int32)
    canon = jnp.arange(EL, dtype=jnp.int32)
    coord_b = canon % LEVELS
    coord_a = canon // LEVELS % LA
    coord_c = canon // (LEVELS * LA)
    owners = jnp.arange(DEVICES, dtype=jnp.int32)[:, None]
    levels = jnp.zeros((DEVICES, EL), jnp.int32).at[owners, places].set((coord_b[None, :] + shifts[:, coord_a, coord_c]) % LEVELS)
    coords = (coord_a, coord_b, coord_c)
    extents = (LA, LEVELS, LC)
    strides = (LEVELS, 1, LEVELS * LA)
    link_rows = []
    for face in range(6):
        axis_id = face // 2
        step_dir = 2 * (face % 2) - 1
        moved = coords[axis_id] + step_dir
        inside = (moved >= 0) & (moved < extents[axis_id])
        partner = jnp.clip(canon + step_dir * strides[axis_id], 0, EL - 1)
        target = jnp.where(inside[None, :], places[:, partner], -1).astype(jnp.int32)
        link_rows.append(jnp.full((DEVICES, EL), -1, jnp.int32).at[owners, places].set(target))
    links = jnp.stack(link_rows)
    curve_of = owners[:, 0] // N_SLAB
    slab_of = owners[:, 0] % N_SLAB
    sends = jnp.full((DEVICES, LEVELS, DEVICES * CAP), 6 * EL, jnp.int32)
    recvs = jnp.full((DEVICES, LEVELS, DEVICES * CAP), 6 * EL, jnp.int32)
    source = owners[:, :, None]
    level_axis = jnp.arange(LEVELS, dtype=jnp.int32)[None, :, None]

    def connect(sends, recvs, valid, targets, span, send_a, send_c, recv_a, recv_c, face_send, face_recv):
        slot_indices = jnp.arange(span, dtype=jnp.int32)[None, None, :]
        along_b = (level_axis - shifts[source, send_a[None, None, :], send_c[None, None, :]]) % LEVELS
        sender = places[source, (send_c * LA + send_a)[None, None, :] * LEVELS + along_b]
        dest = jnp.where(valid, targets, DEVICES).astype(jnp.int32)[:, None, None]
        receiver = places[jnp.minimum(dest, DEVICES - 1), (recv_c * LA + recv_a)[None, None, :] * LEVELS + along_b]
        sends = sends.at[source, level_axis, dest * CAP + slot_indices].set(face_send * EL + sender, mode='drop')
        recvs = recvs.at[dest, level_axis, source * CAP + slot_indices].set(face_recv * EL + receiver, mode='drop')
        return (sends, recvs)
    row_a = jnp.arange(LA, dtype=jnp.int32)
    row_c = jnp.arange(LC, dtype=jnp.int32)
    up_curve = (curve_of + 1) * N_SLAB + (slab_of + turns[curve_of]) % N_SLAB
    sends, recvs = connect(sends, recvs, curve_of < N_CURVE - 1, up_curve, LA, row_a, jnp.full((LA,), LC - 1, jnp.int32), row_a, jnp.zeros((LA,), jnp.int32), 5, 4)
    down_curve = (curve_of - 1) * N_SLAB + (slab_of - turns[jnp.maximum(curve_of - 1, 0)]) % N_SLAB
    sends, recvs = connect(sends, recvs, curve_of > 0, down_curve, LA, row_a, jnp.zeros((LA,), jnp.int32), row_a, jnp.full((LA,), LC - 1, jnp.int32), 4, 5)
    sends, recvs = connect(sends, recvs, slab_of < N_SLAB - 1, owners[:, 0] + 1, LC, jnp.full((LC,), LA - 1, jnp.int32), row_c, jnp.zeros((LC,), jnp.int32), row_c, 1, 0)
    sends, recvs = connect(sends, recvs, slab_of > 0, owners[:, 0] - 1, LC, jnp.zeros((LC,), jnp.int32), row_c, jnp.full((LC,), LA - 1, jnp.int32), row_c, 0, 1)
    return (levels, links, sends, recvs)


def draw_block_inverse(key, part):
    base = jax.random.fold_in(key, 21)
    diagonal = jnp.exp(jax.random.uniform(jax.random.fold_in(base, 1), (BLOCK, ELEMENTS), jnp.float32, jnp.log(0.5), jnp.log(1.5)))
    spread = jnp.clip(jax.random.normal(jax.random.fold_in(base, 2), (BLOCK, BLOCK, ELEMENTS), jnp.float32), -4.0, 4.0) * (0.5 / BLOCK ** 0.5)
    eye = jnp.eye(BLOCK, dtype=jnp.float32)[:, :, None]
    return spread + eye * diagonal[:, None, :]


def draw_dep_level(key, part):
    return layout(key)[0].reshape(ELEMENTS)


def draw_face_link(key, part):
    return layout(key)[1].reshape(6, ELEMENTS)


def draw_send_list(key, part):
    return layout(key)[2].transpose(1, 0, 2).reshape(LEVELS, DEVICES * DEVICES * CAP)


def draw_recv_list(key, part):
    return layout(key)[3].transpose(1, 0, 2).reshape(LEVELS, DEVICES * DEVICES * CAP)


def level_of(stream_key, extent, shards, least, high):
    gain = 1.0
    for axis_at, blocks in shards:
        draws = jax.random.uniform(jax.random.fold_in(jax.random.fold_in(stream_key, 6), axis_at), (blocks,), jnp.float32, least / len(shards), high / len(shards))
        gain = gain * jnp.repeat(jnp.exp(draws), extent[axis_at] // blocks).reshape((-1,) + (1,) * (len(extent) - 1 - axis_at))
    return gain


def bell_draw(rng, extent, scale, limit, cuts=(), kind=jnp.bfloat16):
    level = level_of(rng, extent, cuts, -0.22, 0.18) if cuts else 1.0
    values = jax.random.normal(rng, extent, jnp.float32) * scale * level
    return jnp.minimum(jnp.maximum(values, -limit), limit).astype(kind)


def setup_inputs(seed: int = 0) -> dict:
    key_of = jax.random.split(jax.random.key(seed), 10)
    return {
        "start_state": bell_draw(key_of[0], (BLOCK, ELEMENTS), 1.0, 6.0, ((1, 128),), jnp.float32),
        "right_side": bell_draw(key_of[1], (BLOCK, ELEMENTS), 1.0, 6.0, ((1, 128),), jnp.float32),
        "block_inverse": draw_block_inverse(jax.random.fold_in(key_of[9], 71), 0),
        "lifted_flux_jacobian": bell_draw(key_of[3], (6, BLOCK, TRACE), TRACE ** -0.5, 0.875, (), jnp.float32),
        "face_weight": jnp.clip(jnp.exp(math.log(0.4) - 1.3862944 * jax.random.uniform(key_of[4], (6, ELEMENTS), jnp.float32) ** level_of(key_of[4], (6, ELEMENTS), ((1, 128),), -0.2, 0.2)), 0.1, 0.4),
        "dep_level": draw_dep_level(jax.random.fold_in(key_of[9], 71), 0),
        "face_link": draw_face_link(jax.random.fold_in(key_of[9], 71), 0),
        "send_list": draw_send_list(jax.random.fold_in(key_of[9], 71), 0),
        "recv_list": draw_recv_list(jax.random.fold_in(key_of[9], 71), 0),
    }


REVERSE_FACE = (1, 0, 3, 2, 5, 4)


def face_table(values):
    columns = values.shape[-1]
    cube = values.reshape(VARS, 3, 3, 3, columns)
    faces = [cube[:, 0], cube[:, 2], cube[:, :, 0], cube[:, :, 2], cube[:, :, :, 0], cube[:, :, :, 2]]
    joined = jnp.concatenate([piece.reshape(TRACE, columns) for piece in faces], axis=1)
    return jnp.concatenate([joined, jnp.zeros((TRACE, 1), joined.dtype)], axis=1)


def neighbor_index(links):
    columns = links.shape[1]
    offsets = jnp.array(REVERSE_FACE, jnp.int32)[:, None] * columns
    return jnp.where(links >= 0, links + offsets, 6 * columns).astype(jnp.int32).reshape(6 * columns)


def inflow(traces, ghosts, where_from, lifted_flux_jacobian, coupling_weights):
    columns = coupling_weights.shape[1]
    gathered = (traces[:, where_from] + ghosts[:, :6 * columns]).reshape(TRACE, 6, columns)
    weighted_traces = gathered * coupling_weights[None]
    return jnp.einsum("vuh,hvw->uw", lifted_flux_jacobian, weighted_traces, precision=lax.Precision.HIGHEST)


def to_devices(values):
    return values.reshape(BLOCK, DEVICES, EL).transpose(1, 0, 2)


def from_devices(stacked):
    return stacked.transpose(1, 0, 2).reshape(BLOCK, DEVICES * EL)


def deliver_traces(ghosts, traces, sends, recvs, width):
    packed = jax.vmap(lambda one_table, one_send: one_table[:, one_send])(traces, sends)
    packed = packed.reshape(DEVICES, TRACE, DEVICES, width).transpose(2, 1, 0, 3).reshape(DEVICES, TRACE, DEVICES * width)
    return jax.vmap(lambda one_ghost, one_recv, arrived: one_ghost.at[:, one_recv].set(arrived))(ghosts, recvs, packed)


def reference(start_state, right_side, block_inverse, lifted_flux_jacobian, face_weight, dep_level, face_link, send_list, recv_list):
    sends = send_list.reshape(LEVELS, DEVICES, DEVICES * CAP)
    recvs = recv_list.reshape(LEVELS, DEVICES, DEVICES * CAP)
    where_from = jax.vmap(neighbor_index)(face_link.reshape(6, DEVICES, EL).transpose(1, 0, 2))
    coupling_weights = face_weight.reshape(6, DEVICES, EL).transpose(1, 0, 2)
    all_send = sends.reshape(LEVELS, DEVICES, DEVICES, CAP).transpose(1, 2, 0, 3).reshape(DEVICES, DEVICES * LEVELS * CAP)
    all_recv = recvs.reshape(LEVELS, DEVICES, DEVICES, CAP).transpose(1, 2, 0, 3).reshape(DEVICES, DEVICES * LEVELS * CAP)
    ghosts = jnp.zeros((DEVICES, TRACE, 6 * EL + 1), jnp.float32)
    traces = jax.vmap(face_table)(to_devices(start_state))
    ghosts = deliver_traces(ghosts, traces, all_send, all_recv, LEVELS * CAP)

    def advance(current, ghosts, traces, level_now):
        flows = jax.vmap(lambda one_table, one_ghost, one_index, one_weight: inflow(one_table, one_ghost, one_index, lifted_flux_jacobian, one_weight))(traces, ghosts, where_from, coupling_weights)
        update = jnp.einsum("ije,je->ie", block_inverse, right_side - from_devices(flows), precision=lax.Precision.HIGHEST)
        return jnp.where(dep_level[None] == level_now, update, current)

    current = start_state
    for level_now in range(LEVELS):
        current = advance(current, ghosts, traces, level_now)
        traces = jax.vmap(face_table)(to_devices(current))
        ghosts = deliver_traces(ghosts, traces, sends[level_now], recvs[level_now], CAP)
    forward_state = current
    for level_now in range(LEVELS - 1, -1, -1):
        current = advance(current, ghosts, traces, level_now)
        if level_now > 0:
            traces = jax.vmap(face_table)(to_devices(current))
            ghosts = deliver_traces(ghosts, traces, sends[level_now], recvs[level_now], CAP)
    return forward_state, current
```

```python
import functools

import jax
import jax.numpy as jnp
from jax import lax
from jax.experimental import pallas as pl
from jax.experimental.pallas import tpu as pltpu
from jax.sharding import PartitionSpec as P

VARS = 5
TRACE = 45
BLOCK = 135
EL = 128
LEVELS = 8
CAP = 4
PAD = 64
GROUPS = 12
ROWS = 8 * GROUPS
MESH = pl.DeviceIdType.MESH
F32 = jnp.float32
BF16 = jnp.bfloat16


def split(x):
    hi = x.astype(BF16)
    lo = (x - hi.astype(F32)).astype(BF16)
    return hi, lo


def dot(a, b):
    return lax.dot_general(a, b, (((1,), (0,)), ((), ())), preferred_element_type=F32)


def dot_t(a, b):
    return lax.dot_general(a, b, (((1,), (1,)), ((), ())), preferred_element_type=F32)


def kernel(
    start_ref,
    right_ref,
    inverse_hbm,
    jac_ref,
    weight_ref,
    level_ref,
    link_ref,
    send_ref,
    recv_ref,
    forward_ref,
    swept_ref,
    inverse,
    state,
    table,
    solve_in,
    base,
    update,
    jac,
    jac3,
    links,
    picks,
    drops,
    factors,
    flows,
    index,
    out_buf,
    in_buf,
    first_out,
    first_in,
    inverse_sem,
    send_sem,
    recv_sem,
    first_send_sem,
    first_recv_sem,
):
    curves = lax.axis_size("curve")
    slabs = lax.axis_size("slab")
    my_curve = lax.axis_index("curve")
    my_slab = lax.axis_index("slab")
    own_group = slabs + my_slab

    pull = pltpu.make_async_copy(inverse_hbm, inverse, inverse_sem)
    pull.start()
    in_buf[...] = jnp.zeros_like(in_buf)
    first_in[...] = jnp.zeros_like(first_in)

    def each_peer(act):
        @pl.when(my_curve > 0)
        def _():
            for z in range(slabs):
                act(-1, z)

        @pl.when(my_curve < curves - 1)
        def _():
            for z in range(slabs):
                act(1, z)

        for shift in range(1, slabs):
            act(0, lax.rem(my_slab + shift, slabs))

    barrier = pltpu.get_barrier_semaphore()
    each_peer(
        lambda step, z: pl.semaphore_signal(
            barrier, inc=1, device_id=(my_curve + step, z), device_id_type=MESH
        )
    )

    lane = lax.broadcasted_iota(jnp.int32, (ROWS, EL), 1)

    def to_rows(list_ref):
        shift = lax.rem((curves + 1 - my_curve) * (slabs * CAP), curves * slabs * CAP)
        near = pltpu.roll(list_ref[...], shift, 1)[:, :EL]
        tall = jnp.concatenate([near] * 16, axis=0).T
        index[...] = jnp.full_like(index, 6 * EL)
        for group in range(GROUPS):
            index[8 * group : 8 * group + CAP, :] = tall[CAP * group : CAP * (group + 1), :]

    table[...] = jnp.zeros_like(table)

    def fill_table():
        for side in range(2):
            for q in range(9):
                table[side, pl.ds(q, VARS, stride=9), :] = state[
                    pl.ds(18 * side + q, VARS, stride=27), :
                ]
            for q in range(3):
                table[2 + side, pl.ds(q, 15, stride=3), :] = state[
                    pl.ds(6 * side + q, 15, stride=9), :
                ]
            table[4 + side, :TRACE, :] = state[pl.ds(2 * side, TRACE, stride=3), :]

    state[...] = start_ref[...]
    fill_table()
    to_rows(send_ref)
    for level in range(LEVELS):
        column = index[:, level : level + 1]
        for face in range(6):
            picks[level, :, EL * face : EL * (face + 1)] = (
                jnp.where(column == lane + EL * face, 1.0, 0.0).astype(BF16)
            )

    def packed(level):
        hi, lo = split(jnp.concatenate([table[face] for face in range(6)], axis=1))
        both = jnp.concatenate([hi, lo], axis=1)
        twice = jnp.concatenate([both, both], axis=0)
        pick = picks[level]
        return dot_t(jnp.concatenate([pick, pick], axis=1), twice)

    for level in range(LEVELS):
        first_out[level] = packed(level).reshape(GROUPS, 8, EL)

    @pl.when(jnp.logical_and(my_curve > 0, my_curve < curves - 1))
    def _():
        pl.semaphore_wait(barrier, 3 * slabs - 1)

    @pl.when(jnp.logical_or(my_curve == 0, my_curve == curves - 1))
    def _():
        pl.semaphore_wait(barrier, 2 * slabs - 1)

    def first_copy(step, z):
        return pltpu.make_async_remote_copy(
            src_ref=first_out.at[:, (1 + step) * slabs + z],
            dst_ref=first_in.at[:, (1 - step) * slabs + my_slab],
            send_sem=first_send_sem.at[(1 + step) * slabs + z],
            recv_sem=first_recv_sem.at[(1 - step) * slabs + my_slab],
            device_id=(my_curve + step, z),
            device_id_type=MESH,
        )

    def first_arrival(step, z):
        group = (1 + step) * slabs + z
        return pltpu.make_async_remote_copy(
            src_ref=first_out.at[:, group],
            dst_ref=first_in.at[:, group],
            send_sem=first_send_sem.at[group],
            recv_sem=first_recv_sem.at[group],
            device_id=(my_curve + step, z),
            device_id_type=MESH,
        )

    def copy(slot, step, z):
        return pltpu.make_async_remote_copy(
            src_ref=out_buf.at[slot, (1 + step) * slabs + z],
            dst_ref=in_buf.at[slot, (1 - step) * slabs + my_slab],
            send_sem=send_sem.at[slot, (1 + step) * slabs + z],
            recv_sem=recv_sem.at[slot, (1 - step) * slabs + my_slab],
            device_id=(my_curve + step, z),
            device_id_type=MESH,
        )

    def arrival(slot, step, z):
        group = (1 + step) * slabs + z
        return pltpu.make_async_remote_copy(
            src_ref=out_buf.at[slot, group],
            dst_ref=in_buf.at[slot, group],
            send_sem=send_sem.at[slot, group],
            recv_sem=recv_sem.at[slot, group],
            device_id=(my_curve + step, z),
            device_id_type=MESH,
        )

    each_peer(lambda step, z: first_copy(step, z).start())
    first_in[:, own_group] = first_out[:, own_group]

    jac[...] = jnp.zeros_like(jac)
    for face in range(6):
        jac[:, PAD * face : PAD * face + TRACE] = jac_ref[face]
    jac_hi, jac_lo = split(jac[...])
    width = 6 * PAD
    jac3[:, :width] = jac_hi
    jac3[:, width : 2 * width] = jac_lo
    jac3[:, 2 * width :] = jac_hi

    row = lax.broadcasted_iota(jnp.int32, (EL, EL), 0)
    for face in range(6):
        one = jnp.where(link_ref[face : face + 1, :] == row, 1.0, 0.0).astype(BF16)
        links[face, :EL, :] = one
        links[face, EL:, :] = one

    to_rows(recv_ref)
    face_lane = lax.broadcasted_iota(jnp.int32, (ROWS, width), 1) // PAD
    for level in range(LEVELS):
        column = index[:, level : level + 1]
        hit = jnp.zeros((ROWS, EL), F32)
        gain = jnp.zeros((ROWS, EL), F32)
        for face in range(6):
            mine = column == lane + EL * face
            hit = jnp.where(mine, 1.0, hit)
            gain = jnp.where(mine, weight_ref[face : face + 1, :], gain)
        one = hit.astype(BF16)
        drops[level, :ROWS, :] = one
        drops[level, ROWS:, :] = one
        scale = jnp.sum(gain, axis=1, keepdims=True)
        factors[level] = jnp.where(column // EL == face_lane, scale, 0.0)

    def local_flow():
        parts_hi = []
        parts_lo = []
        for face in range(6):
            other = face + 1 - 2 * (face % 2)
            hi, lo = split(table[other])
            moved = dot(jnp.concatenate([hi, lo], axis=1), links[face])
            hi, lo = split(moved * weight_ref[face : face + 1, :])
            parts_hi.append(hi)
            parts_lo.append(lo)
        hi = jnp.concatenate(parts_hi, axis=0)
        lo = jnp.concatenate(parts_lo, axis=0)
        return dot(jac3[...], jnp.concatenate([hi, hi, lo], axis=0))

    def ghost_flow(level, block):
        thrice = jnp.concatenate([block] * 3, axis=1) * factors[level]
        hi, lo = split(thrice)
        spread = dot_t(jac3[...], jnp.concatenate([hi, hi, lo], axis=1))
        hi, lo = split(spread)
        return dot(jnp.concatenate([hi, lo], axis=1), drops[level])

    local = local_flow()
    each_peer(lambda step, z: first_arrival(step, z).wait_recv())
    known = right_ref[...] - local
    for level in range(LEVELS):
        flow = ghost_flow(level, first_in[level].reshape(ROWS, EL))
        flows[level] = flow
        known = known - flow
    solve_in[...] = known
    pull.wait()

    chunk = 9

    def advance(level):
        vector = solve_in[...]

        def rows(at, carry):
            for k in range(chunk):
                i = at * chunk + k
                update[pl.ds(i, 1), :] = jnp.sum(inverse[i] * vector, axis=0, keepdims=True)
            return carry

        lax.fori_loop(0, BLOCK // chunk, rows, 0)
        state[...] = jnp.where(level_ref[...] == level, update[...], state[...])

    def level_step(step, carry):
        level = jnp.where(step < LEVELS, step, 2 * LEVELS - 1 - step)
        slot = lax.rem(step, 2)
        advance(level)

        @pl.when(step >= 2)
        def _():
            each_peer(lambda s, z: arrival(slot, s, z).wait_send())

        fill_table()
        out_buf[slot] = packed(level).reshape(GROUPS, 8, EL)
        each_peer(lambda s, z: copy(slot, s, z).start())
        in_buf[slot, own_group] = out_buf[slot, own_group]

        @pl.when(step == LEVELS - 1)
        def _():
            forward_ref[...] = state[...]

        known = right_ref[...] - local_flow()
        for other in range(LEVELS):
            known = known - jnp.where(level == other, 0.0, flows[other])
        base[...] = known
        each_peer(lambda s, z: arrival(slot, s, z).wait_recv())
        flow = ghost_flow(level, in_buf[slot].reshape(ROWS, EL))
        flows[level] = flow
        solve_in[...] = base[...] - flow
        return carry

    lax.fori_loop(0, 2 * LEVELS - 1, level_step, 0)
    advance(0)
    swept_ref[...] = state[...]
    each_peer(lambda s, z: first_arrival(s, z).wait_send())
    for slot in range(2):
        each_peer(lambda s, z: arrival(slot, s, z).wait_send())


def body(
    start_state,
    right_side,
    block_inverse,
    lifted_flux_jacobian,
    face_weight,
    dep_level,
    face_link,
    send_list,
    recv_list,
):
    vmem = pl.BlockSpec(memory_space=pltpu.VMEM)
    out = jax.ShapeDtypeStruct((BLOCK, EL), F32)
    width = 6 * PAD
    return pl.pallas_call(
        kernel,
        out_shape=(out, out),
        in_specs=[vmem, vmem, pl.BlockSpec(memory_space=pl.ANY)] + [vmem] * 6,
        out_specs=(vmem, vmem),
        scratch_shapes=[
            pltpu.VMEM((BLOCK, BLOCK, EL), F32),
            pltpu.VMEM((BLOCK, EL), F32),
            pltpu.VMEM((6, PAD, EL), F32),
            pltpu.VMEM((BLOCK, EL), F32),
            pltpu.VMEM((BLOCK, EL), F32),
            pltpu.VMEM((BLOCK, EL), F32),
            pltpu.VMEM((BLOCK, width), F32),
            pltpu.VMEM((BLOCK, 3 * width), BF16),
            pltpu.VMEM((6, 2 * EL, EL), BF16),
            pltpu.VMEM((LEVELS, ROWS, 6 * EL), BF16),
            pltpu.VMEM((LEVELS, 2 * ROWS, EL), BF16),
            pltpu.VMEM((LEVELS, ROWS, width), F32),
            pltpu.VMEM((LEVELS, BLOCK, EL), F32),
            pltpu.VMEM((ROWS, EL), jnp.int32),
            pltpu.VMEM((2, GROUPS, 8, EL), F32),
            pltpu.VMEM((2, GROUPS, 8, EL), F32),
            pltpu.VMEM((LEVELS, GROUPS, 8, EL), F32),
            pltpu.VMEM((LEVELS, GROUPS, 8, EL), F32),
            pltpu.SemaphoreType.DMA,
            pltpu.SemaphoreType.DMA((2, GROUPS)),
            pltpu.SemaphoreType.DMA((2, GROUPS)),
            pltpu.SemaphoreType.DMA((GROUPS,)),
            pltpu.SemaphoreType.DMA((GROUPS,)),
        ],
        compiler_params=pltpu.CompilerParams(
            collective_id=0, has_side_effects=True, vmem_limit_bytes=60 << 20
        ),
    )(
        start_state,
        right_side,
        block_inverse,
        lifted_flux_jacobian,
        face_weight,
        dep_level.reshape(1, EL),
        face_link,
        send_list,
        recv_list,
    )


def solution(mesh):
    return jax.shard_map(
        body,
        mesh=mesh,
        in_specs=(
            P(None, ("curve", "slab")),
            P(None, ("curve", "slab")),
            P(None, None, ("curve", "slab")),
            P(),
            P(None, ("curve", "slab")),
            P(("curve", "slab")),
            P(None, ("curve", "slab")),
            P(None, ("curve", "slab")),
            P(None, ("curve", "slab")),
        ),
        out_specs=(P(None, ("curve", "slab")), P(None, ("curve", "slab"))),
        check_vma=False,
    )
```

```python
import functools

import jax
import jax.numpy as jnp
from jax import lax
from jax.experimental import pallas as pl
from jax.experimental.pallas import tpu as pltpu
from jax.sharding import PartitionSpec as P

VARS = 5
TRACE = 45
BLOCK = 135
EL = 128
LEVELS = 8
CAP = 4
PAD = 64
GROUPS = 12
ROWS = 8 * GROUPS
FAR = 32
MESH = pl.DeviceIdType.MESH
F32 = jnp.float32
BF16 = jnp.bfloat16


def split(x):
    hi = x.astype(BF16)
    lo = (x - hi.astype(F32)).astype(BF16)
    return hi, lo


def dot(a, b):
    return lax.dot_general(a, b, (((1,), (0,)), ((), ())), preferred_element_type=F32)


def dot_t(a, b):
    return lax.dot_general(a, b, (((1,), (1,)), ((), ())), preferred_element_type=F32)


def kernel(
    start_ref,
    right_ref,
    inverse_hbm,
    jac_ref,
    weight_ref,
    level_ref,
    link_ref,
    send_ref,
    recv_ref,
    forward_ref,
    swept_ref,
    inverse,
    state,
    table,
    solve_in,
    base,
    update,
    jac,
    jac3,
    links,
    picks,
    drops,
    far_drops,
    far_lane,
    far_spread,
    chosen,
    partial,
    factors,
    flows,
    index,
    out_buf,
    in_buf,
    first_out,
    first_in,
    inverse_sem,
    send_sem,
    recv_sem,
    first_send_sem,
    first_recv_sem,
):
    curves = lax.axis_size("curve")
    slabs = lax.axis_size("slab")
    my_curve = lax.axis_index("curve")
    my_slab = lax.axis_index("slab")
    odd = lax.rem(my_curve, 2)
    far_curve = my_curve + 2 * odd - 1
    pair_curve = my_curve + 1 - 2 * odd
    has_far = jnp.logical_and(far_curve >= 0, far_curve < curves)
    kind_curve = (far_curve, my_curve, pair_curve)
    far, own, pair = range(3)
    own_group = own * slabs + my_slab

    pull = pltpu.make_async_copy(inverse_hbm, inverse, inverse_sem)
    pull.start()
    in_buf[...] = jnp.zeros_like(in_buf)
    first_in[...] = jnp.zeros_like(first_in)

    def each_far(act):
        @pl.when(has_far)
        def _():
            for shift in (2, 1, 3, 0):
                act(far, lax.rem(my_slab + shift, slabs))

    def each_near(act):
        for shift in (2, 1, 3):
            act(own, lax.rem(my_slab + shift, slabs))
            act(pair, lax.rem(my_slab + shift, slabs))
        act(pair, my_slab)

    def each_peer(act):
        each_far(act)
        each_near(act)

    barrier = pltpu.get_barrier_semaphore()
    each_peer(
        lambda kind, z: pl.semaphore_signal(
            barrier, inc=1, device_id=(kind_curve[kind], z), device_id_type=MESH
        )
    )

    lane = lax.broadcasted_iota(jnp.int32, (ROWS, EL), 1)

    def to_rows(list_ref):
        shift = lax.rem((curves + 1 - my_curve) * (slabs * CAP), curves * slabs * CAP)
        near = pltpu.roll(list_ref[...], shift, 1)[:, :EL]
        tall = jnp.concatenate([near] * 16, axis=0).T
        step = slabs * CAP
        low, mid, high = (tall[step * k : step * (k + 1), :] for k in range(3))
        ordered = (jnp.where(odd == 1, high, low), mid, jnp.where(odd == 1, low, high))
        for group in range(GROUPS):
            at = CAP * (group % slabs)
            four = ordered[group // slabs][at : at + CAP, :]
            index[8 * group : 8 * group + CAP, :] = four
            index[8 * group + CAP : 8 * group + 8, :] = four

    table[...] = jnp.zeros_like(table)

    def fill_table():
        for side in range(2):
            for q in range(9):
                table[side, pl.ds(q, VARS, stride=9), :] = state[
                    pl.ds(18 * side + q, VARS, stride=27), :
                ]
            for q in range(3):
                table[2 + side, pl.ds(q, 15, stride=3), :] = state[
                    pl.ds(6 * side + q, 15, stride=9), :
                ]
            table[4 + side, :TRACE, :] = state[pl.ds(2 * side, TRACE, stride=3), :]

    state[...] = start_ref[...]
    fill_table()
    to_rows(send_ref)
    for level in range(LEVELS):
        column = index[:, level : level + 1]
        for face in range(6):
            picks[level, :, EL * face : EL * (face + 1)] = (
                jnp.where(column == lane + EL * face, 1.0, 0.0).astype(BF16)
            )

    def packed(level):
        hi, lo = split(jnp.concatenate([table[face] for face in range(6)], axis=1))
        both = jnp.concatenate([hi, lo], axis=1)
        twice = jnp.concatenate([both, both], axis=0)
        pick = picks[level]
        return dot_t(jnp.concatenate([pick, pick], axis=1), twice)

    for level in range(LEVELS):
        first_out[level] = packed(level).reshape(GROUPS, 8, EL)

    @pl.when(has_far)
    def _():
        pl.semaphore_wait(barrier, 3 * slabs - 1)

    @pl.when(jnp.logical_not(has_far))
    def _():
        pl.semaphore_wait(barrier, 2 * slabs - 1)

    def first_copy(kind, z):
        return pltpu.make_async_remote_copy(
            src_ref=first_out.at[:, kind * slabs + z],
            dst_ref=first_in.at[:, kind * slabs + my_slab],
            send_sem=first_send_sem.at[kind * slabs + z],
            recv_sem=first_recv_sem.at[kind * slabs + my_slab],
            device_id=(kind_curve[kind], z),
            device_id_type=MESH,
        )

    def first_arrival(kind, z):
        group = kind * slabs + z
        return pltpu.make_async_remote_copy(
            src_ref=first_out.at[:, group],
            dst_ref=first_in.at[:, group],
            send_sem=first_send_sem.at[group],
            recv_sem=first_recv_sem.at[group],
            device_id=(kind_curve[kind], z),
            device_id_type=MESH,
        )

    def copy(slot, kind, z):
        return pltpu.make_async_remote_copy(
            src_ref=out_buf.at[slot, kind * slabs + z],
            dst_ref=in_buf.at[slot, kind * slabs + my_slab],
            send_sem=send_sem.at[slot, kind * slabs + z],
            recv_sem=recv_sem.at[slot, kind * slabs + my_slab],
            device_id=(kind_curve[kind], z),
            device_id_type=MESH,
        )

    def arrival(slot, kind, z):
        group = kind * slabs + z
        return pltpu.make_async_remote_copy(
            src_ref=out_buf.at[slot, group],
            dst_ref=in_buf.at[slot, group],
            send_sem=send_sem.at[slot, group],
            recv_sem=recv_sem.at[slot, group],
            device_id=(kind_curve[kind], z),
            device_id_type=MESH,
        )

    each_peer(lambda kind, z: first_copy(kind, z).start())
    first_in[:, own_group] = first_out[:, own_group]

    jac[...] = jnp.zeros_like(jac)
    for face in range(6):
        jac[PAD * face : PAD * face + TRACE, :BLOCK] = jac_ref[face]
    width = 6 * PAD
    jac_hi, jac_lo = split(jac[...].T[:BLOCK])
    jac3[:, :width] = jac_hi
    jac3[:, width : 2 * width] = jac_lo
    jac3[:, 2 * width :] = jac_hi

    row = lax.broadcasted_iota(jnp.int32, (EL, EL), 0)
    for face in range(6):
        one = jnp.where(link_ref[face : face + 1, :] == row, 1.0, 0.0).astype(BF16)
        links[face, :EL, :] = one
        links[face, EL:, :] = one

    to_rows(recv_ref)
    face_lane = lax.broadcasted_iota(jnp.int32, (ROWS, width), 1) // PAD
    first_half = lax.broadcasted_iota(jnp.int32, (ROWS, EL), 0) % 8 < CAP
    for level in range(LEVELS):
        column = index[:, level : level + 1]
        hit = jnp.zeros((ROWS, EL), F32)
        gain = jnp.zeros((ROWS, EL), F32)
        for face in range(6):
            mine = column == lane + EL * face
            hit = jnp.where(mine, 1.0, hit)
            gain = jnp.where(mine, weight_ref[face : face + 1, :], gain)
        drops[level] = jnp.where(first_half, hit, 0.0).astype(BF16)
        far_drops[level] = jnp.concatenate([hit[:FAR].astype(BF16)] * 4, axis=0)
        scale = jnp.sum(gain, axis=1, keepdims=True)
        factors[level] = jnp.where(column // EL == face_lane, scale, 0.0)
    far_lane[...] = (jnp.concatenate([index[:FAR, :]] * 4, axis=0).T)[:8] % EL

    def local_flow():
        parts_hi = []
        parts_lo = []
        for face in range(6):
            other = face + 1 - 2 * (face % 2)
            hi, lo = split(table[other])
            moved = dot(jnp.concatenate([hi, lo], axis=1), links[face])
            hi, lo = split(moved * weight_ref[face : face + 1, :])
            parts_hi.append(hi)
            parts_lo.append(lo)
        hi = jnp.concatenate(parts_hi, axis=0)
        lo = jnp.concatenate(parts_lo, axis=0)
        return dot(jac3[...], jnp.concatenate([hi, hi, lo], axis=0))

    def scattered(values, where_to):
        hi, lo = split(values)
        return dot(
            jnp.concatenate([hi, lo], axis=1), jnp.concatenate([where_to, where_to], axis=0)
        )

    def spread(block, factor, repeat):
        hi, lo = split(jnp.concatenate([block] * 3, axis=1) * factor)
        thrice = jnp.concatenate([hi, hi, lo], axis=1)
        return dot_t(jac3[...], jnp.concatenate([thrice] * repeat, axis=0))

    local = local_flow()
    each_peer(lambda kind, z: first_arrival(kind, z).wait_recv())
    known = right_ref[...] - local
    for level in range(LEVELS):
        flow = scattered(
            spread(first_in[level].reshape(ROWS, EL), factors[level], 1), drops[level]
        )
        flows[level] = flow
        known = known - flow
    solve_in[...] = known
    pull.wait()

    chunk = 27

    def multiply():
        vector = solve_in[...]

        def rows(at, carry):
            for k in range(chunk):
                i = at * chunk + k
                update[pl.ds(i, 1), :] = jnp.sum(inverse[i] * vector, axis=0, keepdims=True)
            return carry

        lax.fori_loop(0, BLOCK // chunk, rows, 0)

    lanes8 = lax.broadcasted_iota(jnp.int32, (8, EL), 1)
    part_of = (lanes8 // 32) * 2 + (lanes8 // 4) % 2
    tail = lax.broadcasted_iota(jnp.int32, (8, EL), 0) < BLOCK - 128

    def choose(level):
        where_from = jnp.broadcast_to(far_lane[pl.ds(level, 1), :], (8, EL))

        def rows_one(i, carry):
            for half in range(2):
                got = None
                for part in range(8):
                    at = 64 * half + 8 * part
                    moved = jnp.take_along_axis(inverse[i, at : at + 8, :], where_from, axis=1)
                    got = moved if got is None else jnp.where(part_of == part, moved, got)
                chosen[i, 8 * half : 8 * half + 8, :] = got
            last = jnp.concatenate(
                [inverse[i, 128:BLOCK, :], jnp.zeros((136 - BLOCK, EL), F32)], axis=0
            )
            chosen[i, 16:24, :] = jnp.where(
                tail, jnp.take_along_axis(last, where_from, axis=1), 0.0
            )
            return carry

        def rows(at, carry):
            for k in range(27):
                rows_one(at * 27 + k, carry)
            return carry

        lax.fori_loop(0, BLOCK // 27, rows, 0)

    def fold(values):
        pieces = []
        for half in range(2):
            got = None
            for part in range(8):
                at = 64 * half + 8 * part
                piece = values[at : at + 8]
                got = piece if got is None else jnp.where(part_of == part, piece, got)
            pieces.append(got)
        last = jnp.concatenate([values[128:BLOCK], jnp.zeros((136 - BLOCK, EL), F32)], axis=0)
        pieces.append(jnp.where(part_of == 0, last, 0.0))
        return jnp.concatenate(pieces, axis=0)

    def level_of(step):
        return jnp.where(step < LEVELS, step, 2 * LEVELS - 1 - step)

    def far_multiply(vector):
        def rows(at, carry):
            for k in range(chunk):
                i = at * chunk + k
                partial[pl.ds(i, 1), :] = jnp.sum(chosen[i] * vector, axis=0, keepdims=True)
            return carry

        lax.fori_loop(0, BLOCK // chunk, rows, 0)

    multiply()
    state[...] = jnp.where(level_ref[...] == 0, update[...], state[...])

    def level_step(step, carry):
        level = level_of(step)
        slot = lax.rem(step, 2)

        @pl.when(step >= 2)
        def _():
            each_peer(lambda s, z: arrival(slot, s, z).wait_send())

        fill_table()
        out_buf[slot] = packed(level).reshape(GROUPS, 8, EL)
        each_peer(lambda s, z: copy(slot, s, z).start())
        in_buf[slot, own_group] = out_buf[slot, own_group]

        @pl.when(step == LEVELS - 1)
        def _():
            forward_ref[...] = state[...]

        @pl.when(step > 0)
        def _():
            before = level_of(step - 1)
            flows[before] = flows[before] + scattered(
                jnp.where(part_of[:1] == 0, far_spread[...], 0.0), far_drops[before]
            )

        known = right_ref[...] - local_flow()
        for other in range(LEVELS):
            known = known - jnp.where(level == other, 0.0, flows[other])
        base[...] = known
        choose(level)
        each_near(lambda s, z: arrival(slot, s, z).wait_recv())
        block = in_buf[slot, slabs:].reshape(ROWS - FAR, EL)
        flow = scattered(spread(block, factors[level, FAR:], 1), drops[level, FAR:])
        flows[level] = flow
        solve_in[...] = base[...] - flow
        multiply()
        each_far(lambda s, z: arrival(slot, s, z).wait_recv())
        block = in_buf[slot, :slabs].reshape(FAR, EL)
        far_values = spread(block, factors[level, :FAR], 4)
        far_spread[...] = far_values
        far_multiply(fold(far_values))
        fresh = update[...] - scattered(partial[...], far_drops[level])
        state[...] = jnp.where(level_ref[...] == level_of(step + 1), fresh, state[...])
        return carry

    lax.fori_loop(0, 2 * LEVELS - 1, level_step, 0)
    swept_ref[...] = state[...]
    each_peer(lambda s, z: first_arrival(s, z).wait_send())
    for slot in range(2):
        each_peer(lambda s, z: arrival(slot, s, z).wait_send())


def body(
    start_state,
    right_side,
    block_inverse,
    lifted_flux_jacobian,
    face_weight,
    dep_level,
    face_link,
    send_list,
    recv_list,
):
    vmem = pl.BlockSpec(memory_space=pltpu.VMEM)
    out = jax.ShapeDtypeStruct((BLOCK, EL), F32)
    width = 6 * PAD
    return pl.pallas_call(
        kernel,
        out_shape=(out, out),
        in_specs=[vmem, vmem, pl.BlockSpec(memory_space=pl.ANY)] + [vmem] * 6,
        out_specs=(vmem, vmem),
        scratch_shapes=[
            pltpu.VMEM((BLOCK, BLOCK, EL), F32),
            pltpu.VMEM((BLOCK, EL), F32),
            pltpu.VMEM((6, PAD, EL), F32),
            pltpu.VMEM((BLOCK, EL), F32),
            pltpu.VMEM((BLOCK, EL), F32),
            pltpu.VMEM((BLOCK, EL), F32),
            pltpu.VMEM((width, 256), F32),
            pltpu.VMEM((BLOCK, 3 * width), BF16),
            pltpu.VMEM((6, 2 * EL, EL), BF16),
            pltpu.VMEM((LEVELS, ROWS, 6 * EL), BF16),
            pltpu.VMEM((LEVELS, ROWS, EL), BF16),
            pltpu.VMEM((LEVELS, EL, EL), BF16),
            pltpu.VMEM((8, EL), jnp.int32),
            pltpu.VMEM((BLOCK, EL), F32),
            pltpu.VMEM((BLOCK, 24, EL), F32),
            pltpu.VMEM((BLOCK, EL), F32),
            pltpu.VMEM((LEVELS, ROWS, width), F32),
            pltpu.VMEM((LEVELS, BLOCK, EL), F32),
            pltpu.VMEM((ROWS, EL), jnp.int32),
            pltpu.VMEM((2, GROUPS, 8, EL), F32),
            pltpu.VMEM((2, GROUPS, 8, EL), F32),
            pltpu.VMEM((LEVELS, GROUPS, 8, EL), F32),
            pltpu.VMEM((LEVELS, GROUPS, 8, EL), F32),
            pltpu.SemaphoreType.DMA,
            pltpu.SemaphoreType.DMA((2, GROUPS)),
            pltpu.SemaphoreType.DMA((2, GROUPS)),
            pltpu.SemaphoreType.DMA((GROUPS,)),
            pltpu.SemaphoreType.DMA((GROUPS,)),
        ],
        compiler_params=pltpu.CompilerParams(
            collective_id=0, has_side_effects=True, vmem_limit_bytes=60 << 20
        ),
    )(
        start_state,
        right_side,
        block_inverse,
        lifted_flux_jacobian.swapaxes(1, 2),
        face_weight,
        dep_level.reshape(1, EL),
        face_link,
        send_list,
        recv_list,
    )


def solution(mesh):
    return jax.shard_map(
        body,
        mesh=mesh,
        in_specs=(
            P(None, ("curve", "slab")),
            P(None, ("curve", "slab")),
            P(None, None, ("curve", "slab")),
            P(),
            P(None, ("curve", "slab")),
            P(("curve", "slab")),
            P(None, ("curve", "slab")),
            P(None, ("curve", "slab")),
            P(None, ("curve", "slab")),
        ),
        out_specs=(P(None, ("curve", "slab")), P(None, ("curve", "slab"))),
        check_vma=False,
    )
```

```python
import functools

import jax
import jax.numpy as jnp
from jax import lax
from jax.experimental import pallas as pl
from jax.experimental.pallas import tpu as pltpu
from jax.sharding import PartitionSpec as P

VARS = 5
TRACE = 45
BLOCK = 135
EL = 128
LEVELS = 8
CAP = 4
PAD = 64
GROUPS = 12
ROWS = 8 * GROUPS
FAR = 32
MESH = pl.DeviceIdType.MESH
F32 = jnp.float32
BF16 = jnp.bfloat16


def split(x):
    hi = x.astype(BF16)
    lo = (x - hi.astype(F32)).astype(BF16)
    return hi, lo


def dot(a, b):
    return lax.dot_general(a, b, (((1,), (0,)), ((), ())), preferred_element_type=F32)


def dot_t(a, b):
    return lax.dot_general(a, b, (((1,), (1,)), ((), ())), preferred_element_type=F32)


def kernel(
    start_hbm,
    right_hbm,
    inverse_hbm,
    jac_hbm,
    weight_hbm,
    level_hbm,
    link_hbm,
    send_hbm,
    recv_hbm,
    forward_ref,
    swept_ref,
    right_ref,
    jac_ref,
    weight_ref,
    level_ref,
    link_ref,
    send_ref,
    recv_ref,
    inverse,
    state,
    table,
    solve_in,
    update,
    jac,
    jac3,
    links,
    picks,
    drops,
    far_drops,
    far_lane,
    near_flow,
    far_spread,
    far_chosen,
    far_part,
    factors,
    flows,
    others,
    index,
    out_buf,
    in_buf,
    first_out,
    first_in,
    input_sems,
    send_sem,
    recv_sem,
    first_send_sem,
    first_recv_sem,
):
    curves = lax.axis_size("curve")
    slabs = lax.axis_size("slab")
    my_curve = lax.axis_index("curve")
    my_slab = lax.axis_index("slab")
    odd = lax.rem(my_curve, 2)
    far_curve = my_curve + 2 * odd - 1
    pair_curve = my_curve + 1 - 2 * odd
    has_far = jnp.logical_and(far_curve >= 0, far_curve < curves)
    kind_curve = (far_curve, my_curve, pair_curve)
    far, own, pair = range(3)
    own_group = own * slabs + my_slab

    pulls = [
        pltpu.make_async_copy(source, target, input_sems.at[at])
        for at, (source, target) in enumerate(
            (
                (start_hbm, state),
                (send_hbm, send_ref),
                (recv_hbm, recv_ref),
                (jac_hbm, jac_ref),
                (weight_hbm, weight_ref),
                (link_hbm, link_ref),
                (right_hbm, right_ref),
                (level_hbm, level_ref),
                (inverse_hbm, inverse),
            )
        )
    ]
    for pull in pulls:
        pull.start()

    @pl.when(jnp.logical_not(has_far))
    def _():
        in_buf[:, :slabs] = jnp.zeros((2, slabs, 8, EL), F32)
        first_in[:, :slabs] = jnp.zeros((LEVELS, slabs, 8, EL), F32)

    def each_far(act):
        @pl.when(has_far)
        def _():
            for shift in (2, 1, 3, 0):
                act(far, lax.rem(my_slab + shift, slabs))

    def each_near(act):
        for shift in (2, 1, 3):
            act(own, lax.rem(my_slab + shift, slabs))
            act(pair, lax.rem(my_slab + shift, slabs))
        act(pair, my_slab)

    def each_peer(act):
        each_far(act)
        each_near(act)

    barrier = pltpu.get_barrier_semaphore()
    each_peer(
        lambda kind, z: pl.semaphore_signal(
            barrier, inc=1, device_id=(kind_curve[kind], z), device_id_type=MESH
        )
    )

    lane = lax.broadcasted_iota(jnp.int32, (ROWS, EL), 1)

    def to_rows(list_ref):
        shift = lax.rem((curves + 1 - my_curve) * (slabs * CAP), curves * slabs * CAP)
        near = pltpu.roll(list_ref[...], shift, 1)[:, :EL]
        tall = jnp.concatenate([near] * 16, axis=0).T
        step = slabs * CAP
        low, mid, high = (tall[step * k : step * (k + 1), :] for k in range(3))
        ordered = (jnp.where(odd == 1, high, low), mid, jnp.where(odd == 1, low, high))
        for group in range(GROUPS):
            at = CAP * (group % slabs)
            four = ordered[group // slabs][at : at + CAP, :]
            index[8 * group : 8 * group + CAP, :] = four
            index[8 * group + CAP : 8 * group + 8, :] = four

    table[...] = jnp.zeros_like(table)

    def fill_table():
        for side in range(2):
            for q in range(9):
                table[side, pl.ds(q, VARS, stride=9), :] = state[
                    pl.ds(18 * side + q, VARS, stride=27), :
                ]
            for q in range(3):
                table[2 + side, pl.ds(q, 15, stride=3), :] = state[
                    pl.ds(6 * side + q, 15, stride=9), :
                ]
            table[4 + side, :TRACE, :] = state[pl.ds(2 * side, TRACE, stride=3), :]

    for pull in pulls[:2]:
        pull.wait()
    fill_table()
    to_rows(send_ref)
    for level in range(LEVELS):
        column = index[:, level : level + 1]
        for face in range(6):
            picks[level, :, EL * face : EL * (face + 1)] = (
                jnp.where(column == lane + EL * face, 1.0, 0.0).astype(BF16)
            )

    def packed(level):
        hi, lo = split(jnp.concatenate([table[face] for face in range(6)], axis=1))
        both = jnp.concatenate([hi, lo], axis=1)
        twice = jnp.concatenate([both, both], axis=0)
        pick = picks[level]
        return dot_t(jnp.concatenate([pick, pick], axis=1), twice)

    for level in range(LEVELS):
        first_out[level] = packed(level).reshape(GROUPS, 8, EL)

    @pl.when(has_far)
    def _():
        pl.semaphore_wait(barrier, 3 * slabs - 1)

    @pl.when(jnp.logical_not(has_far))
    def _():
        pl.semaphore_wait(barrier, 2 * slabs - 1)

    def first_copy(kind, z):
        return pltpu.make_async_remote_copy(
            src_ref=first_out.at[:, kind * slabs + z],
            dst_ref=first_in.at[:, kind * slabs + my_slab],
            send_sem=first_send_sem.at[kind * slabs + z],
            recv_sem=first_recv_sem.at[kind * slabs + my_slab],
            device_id=(kind_curve[kind], z),
            device_id_type=MESH,
        )

    def first_arrival(kind, z):
        group = kind * slabs + z
        return pltpu.make_async_remote_copy(
            src_ref=first_out.at[:, group],
            dst_ref=first_in.at[:, group],
            send_sem=first_send_sem.at[group],
            recv_sem=first_recv_sem.at[group],
            device_id=(kind_curve[kind], z),
            device_id_type=MESH,
        )

    def copy(slot, kind, z):
        return pltpu.make_async_remote_copy(
            src_ref=out_buf.at[slot, kind * slabs + z],
            dst_ref=in_buf.at[slot, kind * slabs + my_slab],
            send_sem=send_sem.at[slot, kind * slabs + z],
            recv_sem=recv_sem.at[slot, kind * slabs + my_slab],
            device_id=(kind_curve[kind], z),
            device_id_type=MESH,
        )

    def arrival(slot, kind, z):
        group = kind * slabs + z
        return pltpu.make_async_remote_copy(
            src_ref=out_buf.at[slot, group],
            dst_ref=in_buf.at[slot, group],
            send_sem=send_sem.at[slot, group],
            recv_sem=recv_sem.at[slot, group],
            device_id=(kind_curve[kind], z),
            device_id_type=MESH,
        )

    each_peer(lambda kind, z: first_copy(kind, z).start())
    first_in[:, own_group] = first_out[:, own_group]

    for pull in pulls[2:8]:
        pull.wait()
    jac[...] = jnp.zeros_like(jac)
    for face in range(6):
        jac[PAD * face : PAD * face + TRACE, :BLOCK] = jac_ref[face]
    width = 6 * PAD
    jac_hi, jac_lo = split(jac[...].T[:BLOCK])
    jac3[:, :width] = jac_hi
    jac3[:, width : 2 * width] = jac_lo
    jac3[:, 2 * width :] = jac_hi

    row = lax.broadcasted_iota(jnp.int32, (EL, EL), 0)
    for face in range(6):
        one = jnp.where(link_ref[face : face + 1, :] == row, 1.0, 0.0).astype(BF16)
        links[face, :EL, :] = one
        links[face, EL:, :] = one

    to_rows(recv_ref)
    face_lane = lax.broadcasted_iota(jnp.int32, (ROWS, width), 1) // PAD
    first_half = lax.broadcasted_iota(jnp.int32, (ROWS, EL), 0) % 8 < CAP
    for level in range(LEVELS):
        column = index[:, level : level + 1]
        hit = jnp.zeros((ROWS, EL), F32)
        gain = jnp.zeros((ROWS, EL), F32)
        for face in range(6):
            mine = column == lane + EL * face
            hit = jnp.where(mine, 1.0, hit)
            gain = jnp.where(mine, weight_ref[face : face + 1, :], gain)
        drops[level] = jnp.where(first_half, hit, 0.0).astype(BF16)
        far_drops[level] = jnp.concatenate([hit[:FAR].astype(BF16)] * 4, axis=0)
        scale = jnp.sum(gain, axis=1, keepdims=True)
        factors[level] = jnp.where(column // EL == face_lane, scale, 0.0)
    far_lane[...] = (jnp.concatenate([index[:FAR, :]] * 4, axis=0).T)[:8] % EL

    def local_flow():
        parts_hi = []
        parts_lo = []
        for face in range(6):
            other = face + 1 - 2 * (face % 2)
            hi, lo = split(table[other])
            moved = dot(jnp.concatenate([hi, lo], axis=1), links[face])
            hi, lo = split(moved * weight_ref[face : face + 1, :])
            parts_hi.append(hi)
            parts_lo.append(lo)
        hi = jnp.concatenate(parts_hi, axis=0)
        lo = jnp.concatenate(parts_lo, axis=0)
        return dot(jac3[...], jnp.concatenate([hi, hi, lo], axis=0))

    def scattered(values, where_to):
        hi, lo = split(values)
        return dot(
            jnp.concatenate([hi, lo], axis=1), jnp.concatenate([where_to, where_to], axis=0)
        )

    def spread(block, factor, repeat):
        hi, lo = split(jnp.concatenate([block] * 3, axis=1) * factor)
        thrice = jnp.concatenate([hi, hi, lo], axis=1)
        return dot_t(jac3[...], jnp.concatenate([thrice] * repeat, axis=0))

    def first_flow(low, high):
        count = LEVELS * (high - low) * 8
        block = first_in[:, low:high].reshape(count, EL)
        values = spread(block, factors[:, 8 * low : 8 * high].reshape(count, width), 1)
        return scattered(values, drops[:, 8 * low : 8 * high].reshape(count, EL))

    known = right_ref[...] - local_flow()
    each_near(lambda kind, z: first_arrival(kind, z).wait_recv())
    ghost = first_flow(slabs, GROUPS)
    each_far(lambda kind, z: first_arrival(kind, z).wait_recv())
    ghost = ghost + first_flow(0, slabs)
    others[...] = ghost
    solve_in[...] = known - ghost
    pulls[8].wait()

    chunk = 27

    def multiply():
        vector = solve_in[...]

        def rows(at, carry):
            for k in range(chunk):
                i = at * chunk + k
                update[pl.ds(i, 1), :] = jnp.sum(inverse[i] * vector, axis=0, keepdims=True)
            return carry

        lax.fori_loop(0, BLOCK // chunk, rows, 0)

    lanes8 = lax.broadcasted_iota(jnp.int32, (8, EL), 1)
    second = (lanes8 // 4) % 2
    far_place = (lanes8 // 32) * 2 + second
    tail = lax.broadcasted_iota(jnp.int32, (8, EL), 0) < BLOCK - 128

    def merged(pieces, place):
        got = pieces[0]
        for part in range(1, len(pieces)):
            got = jnp.where(place == part, pieces[part], got)
        return got

    def tail_of(values):
        return jnp.concatenate([values, jnp.zeros((136 - BLOCK, EL), F32)], axis=0)

    def choose(level):
        far_from = jnp.broadcast_to(far_lane[pl.ds(level, 1), :], (8, EL))

        def row_of(i, target, where_from, place, parts):
            for m in range(16 // parts):
                pieces = [
                    jnp.take_along_axis(
                        inverse[i, 8 * (m * parts + part) : 8 * (m * parts + part + 1), :],
                        where_from,
                        axis=1,
                    )
                    for part in range(parts)
                ]
                target[i, 8 * m : 8 * m + 8, :] = merged(pieces, place)
            last = jnp.take_along_axis(tail_of(inverse[i, 128:BLOCK, :]), where_from, axis=1)
            at = 128 // parts
            target[i, at : at + 8, :] = jnp.where(tail, last, 0.0)

        def far_rows(at, carry):
            for k in range(chunk):
                row_of(at * chunk + k, far_chosen, far_from, far_place, 8)
            return carry

        lax.fori_loop(0, BLOCK // chunk, far_rows, 0)

    def fold(values, place, parts):
        pieces = []
        for m in range(16 // parts):
            at = 8 * parts * m
            pieces.append(
                merged([values[at + 8 * p : at + 8 * p + 8] for p in range(parts)], place)
            )
        pieces.append(jnp.where(place == 0, tail_of(values[128:BLOCK]), 0.0))
        return jnp.concatenate(pieces, axis=0)

    def part_multiply(chosen, vector, target):
        def rows(at, carry):
            for k in range(chunk):
                i = at * chunk + k
                target[pl.ds(i, 1), :] = jnp.sum(chosen[i] * vector, axis=0, keepdims=True)
            return carry

        lax.fori_loop(0, BLOCK // chunk, rows, 0)

    def level_of(step):
        return jnp.where(step < LEVELS, step, 2 * LEVELS - 1 - step)

    multiply()
    state[...] = jnp.where(level_ref[...] == 0, update[...], state[...])

    def level_step(step, carry):
        level = level_of(step)
        slot = lax.rem(step, 2)

        @pl.when(step >= 2)
        def _():
            each_peer(lambda s, z: arrival(slot, s, z).wait_send())

        fill_table()
        out_buf[slot] = packed(level).reshape(GROUPS, 8, EL)
        each_peer(lambda s, z: copy(slot, s, z).start())
        in_buf[slot, own_group] = out_buf[slot, own_group]

        @pl.when(step == LEVELS - 1)
        def _():
            forward_ref[...] = state[...]

        @pl.when(step > 0)
        def _():
            before = level_of(step - 1)
            flow = near_flow[...] + scattered(
                jnp.where(far_place[:1] == 0, far_spread[...], 0.0), far_drops[before]
            )
            flows[before] = flow
            others[...] = others[...] + flow

        @pl.when(step < LEVELS)
        def _():
            block = first_in[level].reshape(ROWS, EL)
            flows[level] = scattered(spread(block, factors[level], 1), drops[level])

        rest = others[...] - flows[level]
        others[...] = rest
        solve_in[...] = right_ref[...] - local_flow() - rest
        choose(level)
        each_near(lambda s, z: arrival(slot, s, z).wait_recv())
        block = in_buf[slot, slabs:].reshape(ROWS - FAR, EL)
        flow = scattered(spread(block, factors[level, FAR:], 1), drops[level, FAR:])
        near_flow[...] = flow
        solve_in[...] = solve_in[...] - flow
        multiply()
        each_far(lambda s, z: arrival(slot, s, z).wait_recv())
        block = in_buf[slot, :slabs].reshape(FAR, EL)
        values = spread(block, factors[level, :FAR], 4)
        far_spread[...] = values
        part_multiply(far_chosen, fold(values, far_place, 8), far_part)
        fresh = update[...] - scattered(far_part[...], far_drops[level])
        state[...] = jnp.where(level_ref[...] == level_of(step + 1), fresh, state[...])
        return carry

    lax.fori_loop(0, 2 * LEVELS - 1, level_step, 0)
    swept_ref[...] = state[...]
    each_peer(lambda s, z: first_arrival(s, z).wait_send())
    for slot in range(2):
        each_peer(lambda s, z: arrival(slot, s, z).wait_send())


def hand_on(first_ref, second_ref, first_out, second_out, sems):
    copies = (
        pltpu.make_async_copy(first_ref, first_out, sems.at[0]),
        pltpu.make_async_copy(second_ref, second_out, sems.at[1]),
    )
    for one in copies:
        one.start()
    for one in copies:
        one.wait()


def body(
    start_state,
    right_side,
    block_inverse,
    lifted_flux_jacobian,
    face_weight,
    dep_level,
    face_link,
    send_list,
    recv_list,
):
    vmem = pl.BlockSpec(memory_space=pltpu.VMEM)
    out = jax.ShapeDtypeStruct((BLOCK, EL), F32)
    width = 6 * PAD
    lists = send_list.shape[1]
    hbm = pl.BlockSpec(memory_space=pl.ANY)
    first, second = pl.pallas_call(
        kernel,
        out_shape=(out, out),
        in_specs=[hbm] * 9,
        out_specs=(vmem, vmem),
        scratch_shapes=[
            pltpu.VMEM((BLOCK, EL), F32),
            pltpu.VMEM((6, TRACE, BLOCK), F32),
            pltpu.VMEM((6, EL), F32),
            pltpu.VMEM((1, EL), jnp.int32),
            pltpu.VMEM((6, EL), jnp.int32),
            pltpu.VMEM((LEVELS, lists), jnp.int32),
            pltpu.VMEM((LEVELS, lists), jnp.int32),
            pltpu.VMEM((BLOCK, BLOCK, EL), F32),
            pltpu.VMEM((BLOCK, EL), F32),
            pltpu.VMEM((6, PAD, EL), F32),
            pltpu.VMEM((BLOCK, EL), F32),
            pltpu.VMEM((BLOCK, EL), F32),
            pltpu.VMEM((width, 256), F32),
            pltpu.VMEM((BLOCK, 3 * width), BF16),
            pltpu.VMEM((6, 2 * EL, EL), BF16),
            pltpu.VMEM((LEVELS, ROWS, 6 * EL), BF16),
            pltpu.VMEM((LEVELS, ROWS, EL), BF16),
            pltpu.VMEM((LEVELS, EL, EL), BF16),
            pltpu.VMEM((8, EL), jnp.int32),
            pltpu.VMEM((BLOCK, EL), F32),
            pltpu.VMEM((BLOCK, EL), F32),
            pltpu.VMEM((BLOCK, 24, EL), F32),
            pltpu.VMEM((BLOCK, EL), F32),
            pltpu.VMEM((LEVELS, ROWS, width), F32),
            pltpu.VMEM((LEVELS, BLOCK, EL), F32),
            pltpu.VMEM((BLOCK, EL), F32),
            pltpu.VMEM((ROWS, EL), jnp.int32),
            pltpu.VMEM((2, GROUPS, 8, EL), F32),
            pltpu.VMEM((2, GROUPS, 8, EL), F32),
            pltpu.VMEM((LEVELS, GROUPS, 8, EL), F32),
            pltpu.VMEM((LEVELS, GROUPS, 8, EL), F32),
            pltpu.SemaphoreType.DMA((9,)),
            pltpu.SemaphoreType.DMA((2, GROUPS)),
            pltpu.SemaphoreType.DMA((2, GROUPS)),
            pltpu.SemaphoreType.DMA((GROUPS,)),
            pltpu.SemaphoreType.DMA((GROUPS,)),
        ],
        compiler_params=pltpu.CompilerParams(
            collective_id=0, has_side_effects=True, vmem_limit_bytes=60 << 20
        ),
    )(
        start_state,
        right_side,
        block_inverse,
        lifted_flux_jacobian.swapaxes(1, 2),
        face_weight,
        dep_level.reshape(1, EL),
        face_link,
        send_list,
        recv_list,
    )
    return pl.pallas_call(
        hand_on,
        out_shape=(out, out),
        in_specs=[vmem, vmem],
        out_specs=(hbm, hbm),
        scratch_shapes=[pltpu.SemaphoreType.DMA((2,))],
    )(first, second)


def solution(mesh):
    return jax.shard_map(
        body,
        mesh=mesh,
        in_specs=(
            P(None, ("curve", "slab")),
            P(None, ("curve", "slab")),
            P(None, None, ("curve", "slab")),
            P(),
            P(None, ("curve", "slab")),
            P(("curve", "slab")),
            P(None, ("curve", "slab")),
            P(None, ("curve", "slab")),
            P(None, ("curve", "slab")),
        ),
        out_specs=(P(None, ("curve", "slab")), P(None, ("curve", "slab"))),
        check_vma=False,
    )
```

```python
import functools

import jax
import jax.numpy as jnp
from jax import lax
from jax.experimental import pallas as pl
from jax.experimental.pallas import tpu as pltpu
from jax.sharding import PartitionSpec as P

VARS = 5
TRACE = 45
BLOCK = 135
EL = 128
LEVELS = 8
CAP = 4
PAD = 64
GROUPS = 12
ROWS = 8 * GROUPS
FAR, OWN, PAIR = range(3)
LATE = ((FAR, 2), (FAR, 1), (FAR, 3), (FAR, 0), (OWN, 2), (PAIR, 2))
EARLY = ((OWN, 1), (OWN, 3), (PAIR, 1), (PAIR, 3), (PAIR, 0), (OWN, 0))
PLACES = {key: at for at, key in enumerate(LATE + EARLY)}
HALF = 8 * len(LATE)
MESH = pl.DeviceIdType.MESH
F32 = jnp.float32
BF16 = jnp.bfloat16


def split(x):
    hi = x.astype(BF16)
    lo = (x - hi.astype(F32)).astype(BF16)
    return hi, lo


def dot(a, b):
    return lax.dot_general(a, b, (((1,), (0,)), ((), ())), preferred_element_type=F32)


def dot_t(a, b):
    return lax.dot_general(a, b, (((1,), (1,)), ((), ())), preferred_element_type=F32)


def kernel(
    start_hbm,
    right_hbm,
    inverse_hbm,
    jac_hbm,
    weight_hbm,
    level_hbm,
    link_hbm,
    send_hbm,
    recv_hbm,
    forward_ref,
    swept_ref,
    right_ref,
    jac_ref,
    weight_ref,
    level_ref,
    link_ref,
    send_ref,
    recv_ref,
    inverse,
    state,
    table,
    solve_in,
    update,
    jac,
    jac3,
    links,
    picks,
    drops,
    late_drops,
    late_lane,
    early_flow,
    late_spread,
    late_chosen,
    late_part,
    factors,
    total,
    index,
    out_buf,
    in_buf,
    first_out,
    first_in,
    input_sems,
    send_sem,
    recv_sem,
    first_send_sem,
    first_recv_sem,
):
    curves = lax.axis_size("curve")
    slabs = lax.axis_size("slab")
    my_curve = lax.axis_index("curve")
    my_slab = lax.axis_index("slab")
    odd = lax.rem(my_curve, 2)
    far_curve = my_curve + 2 * odd - 1
    pair_curve = my_curve + 1 - 2 * odd
    has_far = jnp.logical_and(far_curve >= 0, far_curve < curves)
    kind_curve = (far_curve, my_curve, pair_curve)
    here = PLACES[OWN, 0]

    pulls = [
        pltpu.make_async_copy(source, target, input_sems.at[at])
        for at, (source, target) in enumerate(
            (
                (start_hbm, state),
                (send_hbm, send_ref),
                (recv_hbm, recv_ref),
                (jac_hbm, jac_ref),
                (weight_hbm, weight_ref),
                (link_hbm, link_ref),
                (right_hbm, right_ref),
                (level_hbm, level_ref),
                (inverse_hbm, inverse),
            )
        )
    ]
    for pull in pulls:
        pull.start()

    @pl.when(jnp.logical_not(has_far))
    def _():
        in_buf[:, :4] = jnp.zeros((2, 4, 8, EL), F32)
        first_in[:, :4] = jnp.zeros((LEVELS, 4, 8, EL), F32)

    def each_late(act):
        @pl.when(has_far)
        def _():
            for kind, shift in LATE[:4]:
                act(kind, shift)

        for kind, shift in LATE[4:]:
            act(kind, shift)

    def each_early(act):
        for kind, shift in EARLY[:-1]:
            act(kind, shift)

    def each_peer(act):
        each_late(act)
        each_early(act)

    def device(kind, shift):
        return (kind_curve[kind], lax.rem(my_slab + shift, slabs))

    barrier = pltpu.get_barrier_semaphore()
    each_peer(
        lambda kind, shift: pl.semaphore_signal(
            barrier, inc=1, device_id=device(kind, shift), device_id_type=MESH
        )
    )

    lane = lax.broadcasted_iota(jnp.int32, (ROWS, EL), 1)

    def to_rows(list_ref):
        shift = lax.rem((curves + 1 - my_curve) * (slabs * CAP), curves * slabs * CAP)
        near = pltpu.roll(list_ref[...], shift, 1)[:, :EL]
        tall = jnp.concatenate([near] * 16, axis=0).T
        step = slabs * CAP
        low, mid, high = (tall[step * k : step * (k + 1), :] for k in range(3))
        ordered = (jnp.where(odd == 1, high, low), mid, jnp.where(odd == 1, low, high))
        for kind in range(3):
            block = ordered[kind]
            turned = block
            for z in range(1, slabs):
                other = jnp.concatenate([block[CAP * z :], block[: CAP * z]], axis=0)
                turned = jnp.where(my_slab == z, other, turned)
            for shift in range(slabs):
                group = PLACES[kind, shift]
                four = turned[CAP * shift : CAP * (shift + 1), :]
                index[8 * group : 8 * group + CAP, :] = four
                index[8 * group + CAP : 8 * group + 8, :] = four

    table[...] = jnp.zeros_like(table)

    def fill_table():
        for side in range(2):
            for q in range(9):
                table[side, pl.ds(q, VARS, stride=9), :] = state[
                    pl.ds(18 * side + q, VARS, stride=27), :
                ]
            for q in range(3):
                table[2 + side, pl.ds(q, 15, stride=3), :] = state[
                    pl.ds(6 * side + q, 15, stride=9), :
                ]
            table[4 + side, :TRACE, :] = state[pl.ds(2 * side, TRACE, stride=3), :]

    for pull in pulls[:2]:
        pull.wait()
    fill_table()
    to_rows(send_ref)
    for level in range(LEVELS):
        column = index[:, level : level + 1]
        for face in range(6):
            picks[level, :, EL * face : EL * (face + 1)] = (
                jnp.where(column == lane + EL * face, 1.0, 0.0).astype(BF16)
            )

    def packed(level):
        hi, lo = split(jnp.concatenate([table[face] for face in range(6)], axis=1))
        both = jnp.concatenate([hi, lo], axis=1)
        twice = jnp.concatenate([both, both], axis=0)
        pick = picks[level]
        return dot_t(jnp.concatenate([pick, pick], axis=1), twice)

    for level in range(LEVELS):
        first_out[level] = packed(level).reshape(GROUPS, 8, EL)

    @pl.when(has_far)
    def _():
        pl.semaphore_wait(barrier, 3 * slabs - 1)

    @pl.when(jnp.logical_not(has_far))
    def _():
        pl.semaphore_wait(barrier, 2 * slabs - 1)

    def first_copy(kind, shift):
        source = PLACES[kind, shift]
        target = PLACES[kind, (4 - shift) % 4]
        return pltpu.make_async_remote_copy(
            src_ref=first_out.at[:, source],
            dst_ref=first_in.at[:, target],
            send_sem=first_send_sem.at[source],
            recv_sem=first_recv_sem.at[target],
            device_id=device(kind, shift),
            device_id_type=MESH,
        )

    def first_arrival(kind, shift):
        place = PLACES[kind, shift]
        return pltpu.make_async_remote_copy(
            src_ref=first_out.at[:, place],
            dst_ref=first_in.at[:, place],
            send_sem=first_send_sem.at[place],
            recv_sem=first_recv_sem.at[place],
            device_id=device(kind, shift),
            device_id_type=MESH,
        )

    def copy(slot, kind, shift):
        source = PLACES[kind, shift]
        target = PLACES[kind, (4 - shift) % 4]
        return pltpu.make_async_remote_copy(
            src_ref=out_buf.at[slot, source],
            dst_ref=in_buf.at[slot, target],
            send_sem=send_sem.at[slot, source],
            recv_sem=recv_sem.at[slot, target],
            device_id=device(kind, shift),
            device_id_type=MESH,
        )

    def arrival(slot, kind, shift):
        place = PLACES[kind, shift]
        return pltpu.make_async_remote_copy(
            src_ref=out_buf.at[slot, place],
            dst_ref=in_buf.at[slot, place],
            send_sem=send_sem.at[slot, place],
            recv_sem=recv_sem.at[slot, place],
            device_id=device(kind, shift),
            device_id_type=MESH,
        )

    each_peer(lambda kind, shift: first_copy(kind, shift).start())
    first_in[:, here] = first_out[:, here]

    for pull in pulls[2:8]:
        pull.wait()
    jac[...] = jnp.zeros_like(jac)
    for face in range(6):
        jac[PAD * face : PAD * face + TRACE, :BLOCK] = jac_ref[face]
    width = 6 * PAD
    jac_hi, jac_lo = split(jac[...].T[:BLOCK])
    jac3[:, :width] = jac_hi
    jac3[:, width : 2 * width] = jac_lo
    jac3[:, 2 * width :] = jac_hi

    row = lax.broadcasted_iota(jnp.int32, (EL, EL), 0)
    for face in range(6):
        one = jnp.where(link_ref[face : face + 1, :] == row, 1.0, 0.0).astype(BF16)
        links[face, :EL, :] = one
        links[face, EL:, :] = one

    def tiled(rows):
        low = lax.broadcasted_iota(jnp.int32, (8, rows.shape[1]), 0) < CAP
        mixed = [
            jnp.where(low, rows[16 * k : 16 * k + 8], rows[16 * k + 8 : 16 * k + 16])
            for k in range(3)
        ]
        return jnp.concatenate([rows, rows, *mixed, jnp.zeros_like(mixed[0])], axis=0)

    to_rows(recv_ref)
    face_lane = lax.broadcasted_iota(jnp.int32, (ROWS, width), 1) // PAD
    first_half = lax.broadcasted_iota(jnp.int32, (ROWS, EL), 0) % 8 < CAP
    for level in range(LEVELS):
        column = index[:, level : level + 1]
        hit = jnp.zeros((ROWS, EL), F32)
        gain = jnp.zeros((ROWS, EL), F32)
        for face in range(6):
            mine = column == lane + EL * face
            hit = jnp.where(mine, 1.0, hit)
            gain = jnp.where(mine, weight_ref[face : face + 1, :], gain)
        drops[level] = jnp.where(first_half, hit, 0.0).astype(BF16)
        late_drops[level] = tiled(hit[:HALF]).astype(BF16)
        scale = jnp.sum(gain, axis=1, keepdims=True)
        factors[level] = jnp.where(column // EL == face_lane, scale, 0.0)
    late_lane[...] = (tiled(index[:HALF, :]).T)[:8] % EL

    def local_flow():
        parts_hi = []
        parts_lo = []
        for face in range(6):
            other = face + 1 - 2 * (face % 2)
            hi, lo = split(table[other])
            moved = dot(jnp.concatenate([hi, lo], axis=1), links[face])
            hi, lo = split(moved * weight_ref[face : face + 1, :])
            parts_hi.append(hi)
            parts_lo.append(lo)
        hi = jnp.concatenate(parts_hi, axis=0)
        lo = jnp.concatenate(parts_lo, axis=0)
        return dot(jac3[...], jnp.concatenate([hi, hi, lo], axis=0))

    def scattered(values, where_to):
        hi, lo = split(values)
        return dot(
            jnp.concatenate([hi, lo], axis=1), jnp.concatenate([where_to, where_to], axis=0)
        )

    def spread(block, factor, tile=lambda rows: rows):
        hi, lo = split(tile(jnp.concatenate([block] * 3, axis=1) * factor))
        return dot_t(jac3[...], jnp.concatenate([hi, hi, lo], axis=1))

    def first_flow(low, high):
        count = LEVELS * (high - low) * 8
        block = first_in[:, low:high].reshape(count, EL)
        values = spread(block, factors[:, 8 * low : 8 * high].reshape(count, width))
        return scattered(values, drops[:, 8 * low : 8 * high].reshape(count, EL))

    known = right_ref[...] - local_flow()
    each_early(lambda kind, shift: first_arrival(kind, shift).wait_recv())
    ghost = first_flow(len(LATE), GROUPS)
    each_late(lambda kind, shift: first_arrival(kind, shift).wait_recv())
    ghost = ghost + first_flow(0, len(LATE))
    total[...] = ghost
    solve_in[...] = known - ghost
    each_peer(lambda kind, shift: first_arrival(kind, shift).wait_send())
    pulls[8].wait()

    chunk = 27

    def multiply():
        vector = solve_in[...]

        def rows(at, carry):
            for k in range(chunk):
                i = at * chunk + k
                update[pl.ds(i, 1), :] = jnp.sum(inverse[i] * vector, axis=0, keepdims=True)
            return carry

        lax.fori_loop(0, BLOCK // chunk, rows, 0)

    lanes8 = lax.broadcasted_iota(jnp.int32, (8, EL), 1)
    tile_at = lanes8 // 8
    second = (lanes8 // 4) % 2
    place_of = jnp.where(tile_at < 12, 2 * (tile_at // 6) + second, jnp.where(tile_at < 15, 4, 7))
    def merged(pieces, place):
        got = pieces[0]
        for part in range(1, len(pieces)):
            got = jnp.where(place == part, pieces[part], got)
        return got

    def tail_of(values):
        return jnp.concatenate([values, jnp.zeros((136 - BLOCK, EL), F32)], axis=0)

    def choose(level):
        where_from = jnp.broadcast_to(late_lane[pl.ds(level, 1), :], (8, EL))

        def moved(values):
            return jnp.take_along_axis(values, where_from, axis=1)

        def rows(at, carry):
            for k in range(chunk):
                i = at * chunk + k
                for m in range(3):
                    late_chosen[i, 8 * m : 8 * m + 8, :] = merged(
                        [
                            moved(inverse[i, 8 * b : 8 * b + 8, :])
                            for b in range(5 * m, 5 * m + 5)
                        ],
                        place_of,
                    )
                late_chosen[i, 24:32, :] = merged(
                    [moved(inverse[i, 120:128, :]), moved(tail_of(inverse[i, 128:BLOCK, :]))],
                    place_of,
                )
            return carry

        lax.fori_loop(0, BLOCK // chunk, rows, 0)

    def fold(values):
        pieces = [
            merged([values[8 * b : 8 * b + 8] for b in range(5 * m, 5 * m + 5)], place_of)
            for m in range(3)
        ]
        last = merged([values[120:128], tail_of(values[128:BLOCK])], place_of)
        pieces.append(jnp.where(place_of < 2, last, 0.0))
        return jnp.concatenate(pieces, axis=0)

    def part_multiply(chosen, vector, target):
        def rows(at, carry):
            for k in range(chunk):
                i = at * chunk + k
                target[pl.ds(i, 1), :] = jnp.sum(chosen[i] * vector, axis=0, keepdims=True)
            return carry

        lax.fori_loop(0, BLOCK // chunk, rows, 0)

    def level_of(step):
        return jnp.where(step < LEVELS, step, 2 * LEVELS - 1 - step)

    multiply()
    state[...] = jnp.where(level_ref[...] == 0, update[...], state[...])

    def level_step(step, carry):
        level = level_of(step)
        slot = lax.rem(step, 2)

        @pl.when(step >= 2)
        def _():
            each_peer(lambda kind, shift: arrival(slot, kind, shift).wait_send())

        fill_table()
        fresh = packed(level).reshape(GROUPS, 8, EL)
        out_buf[slot] = fresh - first_out[level]
        each_peer(lambda kind, shift: copy(slot, kind, shift).start())
        first_out[level] = fresh
        in_buf[slot, here] = out_buf[slot, here]

        @pl.when(step == LEVELS - 1)
        def _():
            forward_ref[...] = state[...]

        @pl.when(step > 0)
        def _():
            before = level_of(step - 1)
            once = jnp.where(place_of[:1] == 0, late_spread[...], 0.0)
            total[...] = total[...] + early_flow[...] + scattered(once, late_drops[before])

        solve_in[...] = right_ref[...] - local_flow() - total[...]
        choose(level)
        each_early(lambda kind, shift: arrival(slot, kind, shift).wait_recv())
        block = in_buf[slot, len(LATE) :].reshape(HALF, EL)
        flow = scattered(spread(block, factors[level, HALF:]), drops[level, HALF:])
        early_flow[...] = flow
        solve_in[...] = solve_in[...] - flow
        multiply()
        each_late(lambda kind, shift: arrival(slot, kind, shift).wait_recv())
        block = in_buf[slot, : len(LATE)].reshape(HALF, EL)
        values = spread(block, factors[level, :HALF], tiled)
        late_spread[...] = values
        part_multiply(late_chosen, fold(values), late_part)
        fresh = update[...] - scattered(late_part[...], late_drops[level])
        state[...] = jnp.where(level_ref[...] == level_of(step + 1), fresh, state[...])
        return carry

    lax.fori_loop(0, 2 * LEVELS - 1, level_step, 0)
    swept_ref[...] = state[...]
    for slot in range(2):
        each_peer(lambda kind, shift: arrival(slot, kind, shift).wait_send())


def hand_on(first_ref, second_ref, first_out, second_out, sems):
    copies = (
        pltpu.make_async_copy(first_ref, first_out, sems.at[0]),
        pltpu.make_async_copy(second_ref, second_out, sems.at[1]),
    )
    for one in copies:
        one.start()
    for one in copies:
        one.wait()


def body(
    start_state,
    right_side,
    block_inverse,
    lifted_flux_jacobian,
    face_weight,
    dep_level,
    face_link,
    send_list,
    recv_list,
):
    vmem = pl.BlockSpec(memory_space=pltpu.VMEM)
    out = jax.ShapeDtypeStruct((BLOCK, EL), F32)
    width = 6 * PAD
    lists = send_list.shape[1]
    hbm = pl.BlockSpec(memory_space=pl.ANY)
    first, second = pl.pallas_call(
        kernel,
        out_shape=(out, out),
        in_specs=[hbm] * 9,
        out_specs=(vmem, vmem),
        scratch_shapes=[
            pltpu.VMEM((BLOCK, EL), F32),
            pltpu.VMEM((6, TRACE, BLOCK), F32),
            pltpu.VMEM((6, EL), F32),
            pltpu.VMEM((1, EL), jnp.int32),
            pltpu.VMEM((6, EL), jnp.int32),
            pltpu.VMEM((LEVELS, lists), jnp.int32),
            pltpu.VMEM((LEVELS, lists), jnp.int32),
            pltpu.VMEM((BLOCK, BLOCK, EL), F32),
            pltpu.VMEM((BLOCK, EL), F32),
            pltpu.VMEM((6, PAD, EL), F32),
            pltpu.VMEM((BLOCK, EL), F32),
            pltpu.VMEM((BLOCK, EL), F32),
            pltpu.VMEM((width, 256), F32),
            pltpu.VMEM((BLOCK, 3 * width), BF16),
            pltpu.VMEM((6, 2 * EL, EL), BF16),
            pltpu.VMEM((LEVELS, ROWS, 6 * EL), BF16),
            pltpu.VMEM((LEVELS, ROWS, EL), BF16),
            pltpu.VMEM((LEVELS, EL, EL), BF16),
            pltpu.VMEM((8, EL), jnp.int32),
            pltpu.VMEM((BLOCK, EL), F32),
            pltpu.VMEM((BLOCK, EL), F32),
            pltpu.VMEM((BLOCK, 32, EL), F32),
            pltpu.VMEM((BLOCK, EL), F32),
            pltpu.VMEM((LEVELS, ROWS, width), F32),
            pltpu.VMEM((BLOCK, EL), F32),
            pltpu.VMEM((ROWS, EL), jnp.int32),
            pltpu.VMEM((2, GROUPS, 8, EL), F32),
            pltpu.VMEM((2, GROUPS, 8, EL), F32),
            pltpu.VMEM((LEVELS, GROUPS, 8, EL), F32),
            pltpu.VMEM((LEVELS, GROUPS, 8, EL), F32),
            pltpu.SemaphoreType.DMA((9,)),
            pltpu.SemaphoreType.DMA((2, GROUPS)),
            pltpu.SemaphoreType.DMA((2, GROUPS)),
            pltpu.SemaphoreType.DMA((GROUPS,)),
            pltpu.SemaphoreType.DMA((GROUPS,)),
        ],
        compiler_params=pltpu.CompilerParams(
            collective_id=0, has_side_effects=True, vmem_limit_bytes=60 << 20
        ),
    )(
        start_state,
        right_side,
        block_inverse,
        lifted_flux_jacobian.swapaxes(1, 2),
        face_weight,
        dep_level.reshape(1, EL),
        face_link,
        send_list,
        recv_list,
    )
    return pl.pallas_call(
        hand_on,
        out_shape=(out, out),
        in_specs=[vmem, vmem],
        out_specs=(hbm, hbm),
        scratch_shapes=[pltpu.SemaphoreType.DMA((2,))],
    )(first, second)


def solution(mesh):
    return jax.shard_map(
        body,
        mesh=mesh,
        in_specs=(
            P(None, ("curve", "slab")),
            P(None, ("curve", "slab")),
            P(None, None, ("curve", "slab")),
            P(),
            P(None, ("curve", "slab")),
            P(("curve", "slab")),
            P(None, ("curve", "slab")),
            P(None, ("curve", "slab")),
            P(None, ("curve", "slab")),
        ),
        out_specs=(P(None, ("curve", "slab")), P(None, ("curve", "slab"))),
        check_vma=False,
    )
```

```python
import functools

import jax
import jax.numpy as jnp
from jax import lax
from jax.experimental import pallas as pl
from jax.experimental.pallas import tpu as pltpu
from jax.sharding import PartitionSpec as P

VARS = 5
TRACE = 45
BLOCK = 135
EL = 128
LEVELS = 8
CAP = 4
PAD = 64
GROUPS = 12
ROWS = 8 * GROUPS
FAR, OWN, PAIR = range(3)
LATE = ((FAR, 2), (FAR, 1), (FAR, 3), (FAR, 0), (OWN, 2), (PAIR, 2))
EARLY = ((OWN, 1), (OWN, 3), (PAIR, 1), (PAIR, 3), (PAIR, 0), (OWN, 0))
PLACES = {key: at for at, key in enumerate(LATE + EARLY)}
HALF = 8 * len(LATE)
STACK = 144
MESH = pl.DeviceIdType.MESH
F32 = jnp.float32
BF16 = jnp.bfloat16


def split(x):
    hi = x.astype(BF16)
    lo = (x - hi.astype(F32)).astype(BF16)
    return hi, lo


def dot(a, b):
    return lax.dot_general(a, b, (((1,), (0,)), ((), ())), preferred_element_type=F32)


def dot_t(a, b):
    return lax.dot_general(a, b, (((1,), (1,)), ((), ())), preferred_element_type=F32)


def kernel(
    start_hbm,
    right_hbm,
    inverse_hbm,
    jac_hbm,
    weight_hbm,
    level_hbm,
    link_hbm,
    send_hbm,
    recv_hbm,
    forward_ref,
    swept_ref,
    right_ref,
    jac_ref,
    weight_ref,
    level_ref,
    link_ref,
    send_ref,
    recv_ref,
    inverse,
    state,
    table,
    solve_in,
    update,
    jac,
    jac2,
    jac3,
    links,
    picks,
    drops,
    late_drops,
    late_lane,
    early_flow,
    late_spread,
    late_chosen,
    late_part,
    factors,
    total,
    index,
    out_buf,
    in_buf,
    first_out,
    first_in,
    input_sems,
    send_sem,
    recv_sem,
    first_send_sem,
    first_recv_sem,
):
    curves = lax.axis_size("curve")
    slabs = lax.axis_size("slab")
    my_curve = lax.axis_index("curve")
    my_slab = lax.axis_index("slab")
    odd = lax.rem(my_curve, 2)
    far_curve = my_curve + 2 * odd - 1
    pair_curve = my_curve + 1 - 2 * odd
    has_far = jnp.logical_and(far_curve >= 0, far_curve < curves)
    kind_curve = (far_curve, my_curve, pair_curve)
    here = PLACES[OWN, 0]

    pulls = [
        pltpu.make_async_copy(source, target, input_sems.at[at])
        for at, (source, target) in enumerate(
            (
                (start_hbm, state),
                (send_hbm, send_ref),
                (recv_hbm, recv_ref),
                (jac_hbm, jac_ref),
                (weight_hbm, weight_ref),
                (link_hbm, link_ref),
                (right_hbm, right_ref),
                (level_hbm, level_ref),
                (inverse_hbm, inverse),
            )
        )
    ]
    for pull in pulls:
        pull.start()

    @pl.when(jnp.logical_not(has_far))
    def _():
        in_buf[:, :4] = jnp.zeros((2, 4, 8, EL), F32)
        first_in[:, :4] = jnp.zeros((LEVELS, 4, 8, EL), F32)

    def each_late(act):
        @pl.when(has_far)
        def _():
            for kind, shift in LATE[:4]:
                act(kind, shift)

        for kind, shift in LATE[4:]:
            act(kind, shift)

    def each_early(act):
        for kind, shift in EARLY[:-1]:
            act(kind, shift)

    def each_peer(act):
        each_late(act)
        each_early(act)

    def device(kind, shift):
        return (kind_curve[kind], lax.rem(my_slab + shift, slabs))

    barrier = pltpu.get_barrier_semaphore()
    each_peer(
        lambda kind, shift: pl.semaphore_signal(
            barrier, inc=1, device_id=device(kind, shift), device_id_type=MESH
        )
    )

    lane = lax.broadcasted_iota(jnp.int32, (ROWS, EL), 1)

    def to_rows(list_ref):
        shift = lax.rem((curves + 1 - my_curve) * (slabs * CAP), curves * slabs * CAP)
        near = pltpu.roll(list_ref[...], shift, 1)[:, :EL]
        tall = jnp.concatenate([near] * 16, axis=0).T
        step = slabs * CAP
        low, mid, high = (tall[step * k : step * (k + 1), :] for k in range(3))
        ordered = (jnp.where(odd == 1, high, low), mid, jnp.where(odd == 1, low, high))
        for kind in range(3):
            block = ordered[kind]
            turned = block
            for z in range(1, slabs):
                other = jnp.concatenate([block[CAP * z :], block[: CAP * z]], axis=0)
                turned = jnp.where(my_slab == z, other, turned)
            for shift in range(slabs):
                group = PLACES[kind, shift]
                four = turned[CAP * shift : CAP * (shift + 1), :]
                index[8 * group : 8 * group + CAP, :] = four
                index[8 * group + CAP : 8 * group + 8, :] = four

    table[...] = jnp.zeros_like(table)

    def fill_table():
        for side in range(2):
            for q in range(9):
                table[side, pl.ds(q, VARS, stride=9), :] = state[
                    pl.ds(18 * side + q, VARS, stride=27), :
                ]
            for q in range(3):
                table[2 + side, pl.ds(q, 15, stride=3), :] = state[
                    pl.ds(6 * side + q, 15, stride=9), :
                ]
            table[4 + side, :TRACE, :] = state[pl.ds(2 * side, TRACE, stride=3), :]

    for pull in pulls[:2]:
        pull.wait()
    fill_table()
    to_rows(send_ref)
    for level in range(LEVELS):
        column = index[:, level : level + 1]
        for face in range(6):
            picks[level, :, EL * face : EL * (face + 1)] = (
                jnp.where(column == lane + EL * face, 1.0, 0.0).astype(BF16)
            )

    def packed(level):
        hi, lo = split(jnp.concatenate([table[face] for face in range(6)], axis=1))
        halves = dot_t(picks[level], jnp.concatenate([hi, lo], axis=0))
        return halves + pltpu.roll(halves, PAD, 1)

    for level in range(LEVELS):
        first_out[level] = packed(level).reshape(GROUPS, 8, EL)

    @pl.when(has_far)
    def _():
        pl.semaphore_wait(barrier, 3 * slabs - 1)

    @pl.when(jnp.logical_not(has_far))
    def _():
        pl.semaphore_wait(barrier, 2 * slabs - 1)

    def first_copy(kind, shift):
        source = PLACES[kind, shift]
        target = PLACES[kind, (4 - shift) % 4]
        return pltpu.make_async_remote_copy(
            src_ref=first_out.at[:, source],
            dst_ref=first_in.at[:, target],
            send_sem=first_send_sem.at[source],
            recv_sem=first_recv_sem.at[target],
            device_id=device(kind, shift),
            device_id_type=MESH,
        )

    def first_arrival(kind, shift):
        place = PLACES[kind, shift]
        return pltpu.make_async_remote_copy(
            src_ref=first_out.at[:, place],
            dst_ref=first_in.at[:, place],
            send_sem=first_send_sem.at[place],
            recv_sem=first_recv_sem.at[place],
            device_id=device(kind, shift),
            device_id_type=MESH,
        )

    def copy(slot, kind, shift):
        source = PLACES[kind, shift]
        target = PLACES[kind, (4 - shift) % 4]
        return pltpu.make_async_remote_copy(
            src_ref=out_buf.at[slot, source],
            dst_ref=in_buf.at[slot, target],
            send_sem=send_sem.at[slot, source],
            recv_sem=recv_sem.at[slot, target],
            device_id=device(kind, shift),
            device_id_type=MESH,
        )

    def arrival(slot, kind, shift):
        place = PLACES[kind, shift]
        return pltpu.make_async_remote_copy(
            src_ref=out_buf.at[slot, place],
            dst_ref=in_buf.at[slot, place],
            send_sem=send_sem.at[slot, place],
            recv_sem=recv_sem.at[slot, place],
            device_id=device(kind, shift),
            device_id_type=MESH,
        )

    each_peer(lambda kind, shift: first_copy(kind, shift).start())
    first_in[:, here] = first_out[:, here]

    for pull in pulls[2:8]:
        pull.wait()
    jac[...] = jnp.zeros_like(jac)
    for face in range(6):
        jac[PAD * face : PAD * face + TRACE, :BLOCK] = jac_ref[face]
    width = 6 * PAD
    jac_hi, jac_lo = split(jac[...].T[:BLOCK])
    jac2[:BLOCK] = jac_hi
    jac2[BLOCK:STACK] = jnp.zeros((STACK - BLOCK, width), BF16)
    jac2[STACK : STACK + BLOCK] = jac_lo
    jac2[STACK + BLOCK :] = jnp.zeros((STACK - BLOCK, width), BF16)
    jac3[:, :width] = jac_hi
    jac3[:, width : 2 * width] = jac_lo
    jac3[:, 2 * width :] = jac_hi

    row = lax.broadcasted_iota(jnp.int32, (EL, EL), 0)
    for face in range(6):
        one = jnp.where(link_ref[face : face + 1, :] == row, 1.0, 0.0).astype(BF16)
        links[face, :EL, :] = one
        links[face, EL:, :] = one

    def tiled(rows):
        low = lax.broadcasted_iota(jnp.int32, (8, rows.shape[1]), 0) < CAP
        mixed = [
            jnp.where(low, rows[16 * k : 16 * k + 8], rows[16 * k + 8 : 16 * k + 16])
            for k in range(3)
        ]
        return jnp.concatenate([rows, rows, *mixed, jnp.zeros_like(mixed[0])], axis=0)

    to_rows(recv_ref)
    face_lane = lax.broadcasted_iota(jnp.int32, (ROWS, width), 1) // PAD
    first_half = lax.broadcasted_iota(jnp.int32, (ROWS, EL), 0) % 8 < CAP
    for level in range(LEVELS):
        column = index[:, level : level + 1]
        hit = jnp.zeros((ROWS, EL), F32)
        gain = jnp.zeros((ROWS, EL), F32)
        for face in range(6):
            mine = column == lane + EL * face
            hit = jnp.where(mine, 1.0, hit)
            gain = jnp.where(mine, weight_ref[face : face + 1, :], gain)
        drops[level] = jnp.where(first_half, hit, 0.0).astype(BF16)
        late_drops[level] = tiled(hit[:HALF]).astype(BF16)
        scale = jnp.sum(gain, axis=1, keepdims=True)
        factors[level] = jnp.where(column // EL == face_lane, scale, 0.0)
    late_lane[...] = (tiled(index[:HALF, :]).T)[:8] % EL

    def local_flow():
        parts_hi = []
        parts_lo = []
        for face in range(6):
            other = face + 1 - 2 * (face % 2)
            hi, lo = split(table[other])
            moved = dot(jnp.concatenate([hi, lo], axis=1), links[face])
            hi, lo = split(moved * weight_ref[face : face + 1, :])
            parts_hi.append(hi)
            parts_lo.append(lo)
        hi = jnp.concatenate(parts_hi, axis=0)
        lo = jnp.concatenate(parts_lo, axis=0)
        return dot(jac3[...], jnp.concatenate([hi, hi, lo], axis=0))

    def scattered(values, where_to):
        hi, lo = split(values)
        return dot(
            jnp.concatenate([hi, lo], axis=1), jnp.concatenate([where_to, where_to], axis=0)
        )

    def spread(block, factor, tile=lambda rows: rows):
        hi, lo = split(tile(jnp.concatenate([block] * 3, axis=1) * factor))
        both = dot_t(jac2[...], hi)
        return both[:BLOCK] + both[STACK : STACK + BLOCK] + dot_t(jac2[:BLOCK], lo)

    def first_flow(low, high):
        count = LEVELS * (high - low) * 8
        block = first_in[:, low:high].reshape(count, EL)
        values = spread(block, factors[:, 8 * low : 8 * high].reshape(count, width))
        return scattered(values, drops[:, 8 * low : 8 * high].reshape(count, EL))

    known = right_ref[...] - local_flow()
    each_early(lambda kind, shift: first_arrival(kind, shift).wait_recv())
    ghost = first_flow(len(LATE), GROUPS)
    each_late(lambda kind, shift: first_arrival(kind, shift).wait_recv())
    ghost = ghost + first_flow(0, len(LATE))
    total[...] = ghost
    solve_in[...] = known - ghost
    each_peer(lambda kind, shift: first_arrival(kind, shift).wait_send())
    pulls[8].wait()

    chunk = 45

    lanes8 = lax.broadcasted_iota(jnp.int32, (8, EL), 1)
    tile_at = lanes8 // 8
    second = (lanes8 // 4) % 2
    place_of = jnp.where(tile_at < 12, 2 * (tile_at // 6) + second, jnp.where(tile_at < 15, 4, 7))
    def merged(pieces, place):
        got = pieces[0]
        for part in range(1, len(pieces)):
            got = jnp.where(place == part, pieces[part], got)
        return got

    def tail_of(values):
        return jnp.concatenate([values, jnp.zeros((136 - BLOCK, EL), F32)], axis=0)

    def choose(level):
        where_from = jnp.broadcast_to(late_lane[pl.ds(level, 1), :], (8, EL))

        def moved(values):
            return jnp.take_along_axis(values, where_from, axis=1)

        def rows(at, carry):
            for k in range(chunk):
                i = at * chunk + k
                for m in range(3):
                    late_chosen[level, i, 8 * m : 8 * m + 8, :] = merged(
                        [
                            moved(inverse[i, 8 * b : 8 * b + 8, :])
                            for b in range(5 * m, 5 * m + 5)
                        ],
                        place_of,
                    )
                late_chosen[level, i, 24:32, :] = merged(
                    [moved(inverse[i, 120:128, :]), moved(tail_of(inverse[i, 128:BLOCK, :]))],
                    place_of,
                )
            return carry

        lax.fori_loop(0, BLOCK // chunk, rows, 0)

    def fold(values):
        pieces = [
            merged([values[8 * b : 8 * b + 8] for b in range(5 * m, 5 * m + 5)], place_of)
            for m in range(3)
        ]
        last = merged([values[120:128], tail_of(values[128:BLOCK])], place_of)
        pieces.append(jnp.where(place_of < 2, last, 0.0))
        return jnp.concatenate(pieces, axis=0)

    at8 = lax.broadcasted_iota(jnp.int32, (8, EL), 0)

    def gathered_sums(parts):
        top = at8 < 4
        fours = [
            jnp.where(top, parts[k], parts[k + 4])
            + pltpu.roll(jnp.where(top, parts[k + 4], parts[k]), 4, 0)
            for k in range(4)
        ]
        top = at8 % 4 < 2
        twos = [
            jnp.where(
                top,
                fours[k] + pltpu.roll(fours[k], 6, 0),
                fours[k + 2] + pltpu.roll(fours[k + 2], 2, 0),
            )
            for k in range(2)
        ]
        return jnp.where(
            at8 % 2 < 1, twos[0] + pltpu.roll(twos[0], 7, 0), twos[1] + pltpu.roll(twos[1], 1, 0)
        )

    def products(matrix, i, tiles):
        got = None
        for m, tile in enumerate(tiles):
            one = matrix[i, 8 * m : 8 * m + 8, :] * tile
            got = one if got is None else got + one
        return got

    def part_multiply(matrix, vector, target):
        tiles = [vector[8 * m : 8 * m + 8] for m in range(4)]

        def rows(at, carry):
            for k in range(8):
                g = at * 8 + k
                target[pl.ds(pl.multiple_of(8 * g, 8), 8), :] = gathered_sums(
                    [products(matrix, 8 * g + r, tiles) for r in range(8)]
                )
            return carry

        lax.fori_loop(0, 16 // 8, rows, 0)
        last = [products(matrix, 128 + r, tiles) for r in range(BLOCK - 128)]
        target[128:BLOCK, :] = gathered_sums(last + [jnp.zeros((8, EL), F32)])[: BLOCK - 128]

    def multiply():
        vector = solve_in[...]
        tiles = [vector[8 * m : 8 * m + 8] for m in range(16)]
        last_tile = tail_of(vector[128:BLOCK])

        def sums(i):
            last = tail_of(inverse[i, 128:BLOCK, :]) * last_tile
            return products(inverse, i, tiles) + last

        def rows(at, carry):
            for k in range(4):
                g = at * 4 + k
                update[pl.ds(pl.multiple_of(8 * g, 8), 8), :] = gathered_sums(
                    [sums(8 * g + r) for r in range(8)]
                )
            return carry

        lax.fori_loop(0, 4, rows, 0)
        last = [sums(128 + r) for r in range(BLOCK - 128)]
        update[128:BLOCK, :] = gathered_sums(last + [jnp.zeros((8, EL), F32)])[: BLOCK - 128]

    def level_of(step):
        return jnp.where(step < LEVELS, step, 2 * LEVELS - 1 - step)

    multiply()
    state[...] = jnp.where(level_ref[...] == 0, update[...], state[...])

    def level_step(step, carry):
        level = level_of(step)
        slot = lax.rem(step, 2)

        @pl.when(step >= 2)
        def _():
            each_peer(lambda kind, shift: arrival(slot, kind, shift).wait_send())

        fill_table()
        fresh = packed(level).reshape(GROUPS, 8, EL)
        out_buf[slot] = fresh - first_out[level]
        each_peer(lambda kind, shift: copy(slot, kind, shift).start())
        first_out[level] = fresh
        in_buf[slot, here] = out_buf[slot, here]

        @pl.when(step == LEVELS - 1)
        def _():
            forward_ref[...] = state[...]

        @pl.when(step > 0)
        def _():
            before = level_of(step - 1)
            once = jnp.where(place_of[:1] == 0, late_spread[...], 0.0)
            total[...] = total[...] + early_flow[...] + scattered(once, late_drops[before])

        solve_in[...] = right_ref[...] - local_flow() - total[...]
        @pl.when(step < LEVELS)
        def _():
            choose(level)

        each_early(lambda kind, shift: arrival(slot, kind, shift).wait_recv())
        block = in_buf[slot, len(LATE) :].reshape(HALF, EL)
        flow = scattered(spread(block, factors[level, HALF:]), drops[level, HALF:])
        early_flow[...] = flow
        solve_in[...] = solve_in[...] - flow
        multiply()
        each_late(lambda kind, shift: arrival(slot, kind, shift).wait_recv())
        block = in_buf[slot, : len(LATE)].reshape(HALF, EL)
        values = spread(block, factors[level, :HALF], tiled)
        late_spread[...] = values
        part_multiply(late_chosen.at[level], fold(values), late_part)
        fresh = update[...] - scattered(late_part[...], late_drops[level])
        state[...] = jnp.where(level_ref[...] == level_of(step + 1), fresh, state[...])
        return carry

    lax.fori_loop(0, 2 * LEVELS - 1, level_step, 0)
    swept_ref[...] = state[...]
    for slot in range(2):
        each_peer(lambda kind, shift: arrival(slot, kind, shift).wait_send())


def hand_on(first_ref, second_ref, first_out, second_out, sems):
    copies = (
        pltpu.make_async_copy(first_ref, first_out, sems.at[0]),
        pltpu.make_async_copy(second_ref, second_out, sems.at[1]),
    )
    for one in copies:
        one.start()
    for one in copies:
        one.wait()


def body(
    start_state,
    right_side,
    block_inverse,
    lifted_flux_jacobian,
    face_weight,
    dep_level,
    face_link,
    send_list,
    recv_list,
):
    vmem = pl.BlockSpec(memory_space=pltpu.VMEM)
    out = jax.ShapeDtypeStruct((BLOCK, EL), F32)
    width = 6 * PAD
    lists = send_list.shape[1]
    hbm = pl.BlockSpec(memory_space=pl.ANY)
    first, second = pl.pallas_call(
        kernel,
        out_shape=(out, out),
        in_specs=[hbm] * 9,
        out_specs=(vmem, vmem),
        scratch_shapes=[
            pltpu.VMEM((BLOCK, EL), F32),
            pltpu.VMEM((6, TRACE, BLOCK), F32),
            pltpu.VMEM((6, EL), F32),
            pltpu.VMEM((1, EL), jnp.int32),
            pltpu.VMEM((6, EL), jnp.int32),
            pltpu.VMEM((LEVELS, lists), jnp.int32),
            pltpu.VMEM((LEVELS, lists), jnp.int32),
            pltpu.VMEM((BLOCK, BLOCK, EL), F32),
            pltpu.VMEM((BLOCK, EL), F32),
            pltpu.VMEM((6, PAD, EL), F32),
            pltpu.VMEM((BLOCK, EL), F32),
            pltpu.VMEM((BLOCK, EL), F32),
            pltpu.VMEM((width, 256), F32),
            pltpu.VMEM((2 * STACK, width), BF16),
            pltpu.VMEM((BLOCK, 3 * width), BF16),
            pltpu.VMEM((6, 2 * EL, EL), BF16),
            pltpu.VMEM((LEVELS, ROWS, 6 * EL), BF16),
            pltpu.VMEM((LEVELS, ROWS, EL), BF16),
            pltpu.VMEM((LEVELS, EL, EL), BF16),
            pltpu.VMEM((8, EL), jnp.int32),
            pltpu.VMEM((BLOCK, EL), F32),
            pltpu.VMEM((BLOCK, EL), F32),
            pltpu.VMEM((LEVELS, BLOCK, 32, EL), F32),
            pltpu.VMEM((BLOCK, EL), F32),
            pltpu.VMEM((LEVELS, ROWS, width), F32),
            pltpu.VMEM((BLOCK, EL), F32),
            pltpu.VMEM((ROWS, EL), jnp.int32),
            pltpu.VMEM((2, GROUPS, 8, EL), F32),
            pltpu.VMEM((2, GROUPS, 8, EL), F32),
            pltpu.VMEM((LEVELS, GROUPS, 8, EL), F32),
            pltpu.VMEM((LEVELS, GROUPS, 8, EL), F32),
            pltpu.SemaphoreType.DMA((9,)),
            pltpu.SemaphoreType.DMA((2, GROUPS)),
            pltpu.SemaphoreType.DMA((2, GROUPS)),
            pltpu.SemaphoreType.DMA((GROUPS,)),
            pltpu.SemaphoreType.DMA((GROUPS,)),
        ],
        compiler_params=pltpu.CompilerParams(
            collective_id=0, has_side_effects=True, vmem_limit_bytes=60 << 20
        ),
    )(
        start_state,
        right_side,
        block_inverse,
        lifted_flux_jacobian.swapaxes(1, 2),
        face_weight,
        dep_level.reshape(1, EL),
        face_link,
        send_list,
        recv_list,
    )
    return pl.pallas_call(
        hand_on,
        out_shape=(out, out),
        in_specs=[vmem, vmem],
        out_specs=(hbm, hbm),
        scratch_shapes=[pltpu.SemaphoreType.DMA((2,))],
    )(first, second)


def solution(mesh):
    return jax.shard_map(
        body,
        mesh=mesh,
        in_specs=(
            P(None, ("curve", "slab")),
            P(None, ("curve", "slab")),
            P(None, None, ("curve", "slab")),
            P(),
            P(None, ("curve", "slab")),
            P(("curve", "slab")),
            P(None, ("curve", "slab")),
            P(None, ("curve", "slab")),
            P(None, ("curve", "slab")),
        ),
        out_specs=(P(None, ("curve", "slab")), P(None, ("curve", "slab"))),
        check_vma=False,
    )
```

```python
import functools

import jax
import jax.numpy as jnp
from jax import lax
from jax.experimental import pallas as pl
from jax.experimental.pallas import tpu as pltpu
from jax.sharding import PartitionSpec as P

VARS = 5
TRACE = 45
BLOCK = 135
EL = 128
LEVELS = 8
CAP = 4
PAD = 64
GROUPS = 12
ROWS = 8 * GROUPS
FAR, OWN, PAIR = range(3)
LATE = ((FAR, 2), (FAR, 1), (FAR, 3), (FAR, 0), (OWN, 2), (PAIR, 2))
EARLY = ((OWN, 1), (OWN, 3), (PAIR, 1), (PAIR, 3), (PAIR, 0), (OWN, 0))
PLACES = {key: at for at, key in enumerate(LATE + EARLY)}
HALF = 8 * len(LATE)
STACK = 144
MESH = pl.DeviceIdType.MESH
F32 = jnp.float32
BF16 = jnp.bfloat16


def split(x):
    hi = x.astype(BF16)
    lo = (x - hi.astype(F32)).astype(BF16)
    return hi, lo


def dot(a, b):
    return lax.dot_general(a, b, (((1,), (0,)), ((), ())), preferred_element_type=F32)


def dot_t(a, b):
    return lax.dot_general(a, b, (((1,), (1,)), ((), ())), preferred_element_type=F32)


def kernel(
    start_hbm,
    right_hbm,
    inverse_hbm,
    jac_hbm,
    weight_hbm,
    level_hbm,
    link_hbm,
    send_hbm,
    recv_hbm,
    forward_ref,
    swept_ref,
    right_ref,
    jac_ref,
    weight_ref,
    level_ref,
    link_ref,
    send_ref,
    recv_ref,
    inverse,
    state,
    table,
    solve_in,
    update,
    jac,
    jac2,
    jac3,
    links,
    picks,
    drops,
    late_drops,
    late_lane,
    early_flow,
    late_spread,
    late_chosen,
    late_part,
    factors,
    total,
    index,
    out_buf,
    in_buf,
    first_out,
    first_in,
    input_sems,
    send_sem,
    recv_sem,
    first_send_sem,
    first_recv_sem,
):
    curves = lax.axis_size("curve")
    slabs = lax.axis_size("slab")
    my_curve = lax.axis_index("curve")
    my_slab = lax.axis_index("slab")
    odd = lax.rem(my_curve, 2)
    far_curve = my_curve + 2 * odd - 1
    pair_curve = my_curve + 1 - 2 * odd
    has_far = jnp.logical_and(far_curve >= 0, far_curve < curves)
    kind_curve = (far_curve, my_curve, pair_curve)
    here = PLACES[OWN, 0]

    pulls = [
        pltpu.make_async_copy(source, target, input_sems.at[at])
        for at, (source, target) in enumerate(
            (
                (start_hbm, state),
                (send_hbm, send_ref),
                (recv_hbm, recv_ref),
                (jac_hbm, jac_ref),
                (weight_hbm, weight_ref),
                (link_hbm, link_ref),
                (right_hbm, right_ref),
                (level_hbm, level_ref),
                (inverse_hbm, inverse),
            )
        )
    ]
    for pull in pulls:
        pull.start()

    @pl.when(jnp.logical_not(has_far))
    def _():
        in_buf[:, :4] = jnp.zeros((2, 4, 8, EL), F32)
        first_in[:, :4] = jnp.zeros((LEVELS, 4, 8, EL), F32)

    def each_late(act):
        @pl.when(has_far)
        def _():
            for kind, shift in LATE[:4]:
                act(kind, shift)

        for kind, shift in LATE[4:]:
            act(kind, shift)

    def each_early(act):
        for kind, shift in EARLY[:-1]:
            act(kind, shift)

    def each_peer(act):
        each_late(act)
        each_early(act)

    def device(kind, shift):
        return (kind_curve[kind], lax.rem(my_slab + shift, slabs))

    barrier = pltpu.get_barrier_semaphore()
    each_peer(
        lambda kind, shift: pl.semaphore_signal(
            barrier, inc=1, device_id=device(kind, shift), device_id_type=MESH
        )
    )

    lane = lax.broadcasted_iota(jnp.int32, (ROWS, EL), 1)

    def to_rows(list_ref):
        shift = lax.rem((curves + 1 - my_curve) * (slabs * CAP), curves * slabs * CAP)
        near = pltpu.roll(list_ref[...], shift, 1)[:, :EL]
        tall = jnp.concatenate([near] * 16, axis=0).T
        step = slabs * CAP
        low, mid, high = (tall[step * k : step * (k + 1), :] for k in range(3))
        ordered = (jnp.where(odd == 1, high, low), mid, jnp.where(odd == 1, low, high))
        for kind in range(3):
            block = ordered[kind]
            turned = block
            for z in range(1, slabs):
                other = jnp.concatenate([block[CAP * z :], block[: CAP * z]], axis=0)
                turned = jnp.where(my_slab == z, other, turned)
            for shift in range(slabs):
                group = PLACES[kind, shift]
                four = turned[CAP * shift : CAP * (shift + 1), :]
                index[8 * group : 8 * group + CAP, :] = four
                index[8 * group + CAP : 8 * group + 8, :] = four

    table[...] = jnp.zeros_like(table)

    def fill_table():
        for side in range(2):
            for q in range(9):
                table[side, pl.ds(q, VARS, stride=9), :] = state[
                    pl.ds(18 * side + q, VARS, stride=27), :
                ]
            for q in range(3):
                table[2 + side, pl.ds(q, 15, stride=3), :] = state[
                    pl.ds(6 * side + q, 15, stride=9), :
                ]
            table[4 + side, :TRACE, :] = state[pl.ds(2 * side, TRACE, stride=3), :]

    for pull in pulls[:2]:
        pull.wait()
    fill_table()
    to_rows(send_ref)
    for level in range(LEVELS):
        column = index[:, level : level + 1]
        for face in range(6):
            picks[level, :, EL * face : EL * (face + 1)] = (
                jnp.where(column == lane + EL * face, 1.0, 0.0).astype(BF16)
            )

    def packed(level):
        hi, lo = split(jnp.concatenate([table[face] for face in range(6)], axis=1))
        halves = dot_t(picks[level], jnp.concatenate([hi, lo], axis=0))
        return halves + pltpu.roll(halves, PAD, 1)

    for level in range(LEVELS):
        first_out[level] = packed(level).reshape(GROUPS, 8, EL)

    @pl.when(has_far)
    def _():
        pl.semaphore_wait(barrier, 3 * slabs - 1)

    @pl.when(jnp.logical_not(has_far))
    def _():
        pl.semaphore_wait(barrier, 2 * slabs - 1)

    def first_copy(kind, shift):
        source = PLACES[kind, shift]
        target = PLACES[kind, (4 - shift) % 4]
        return pltpu.make_async_remote_copy(
            src_ref=first_out.at[:, source],
            dst_ref=first_in.at[:, target],
            send_sem=first_send_sem.at[source],
            recv_sem=first_recv_sem.at[target],
            device_id=device(kind, shift),
            device_id_type=MESH,
        )

    def first_arrival(kind, shift):
        place = PLACES[kind, shift]
        return pltpu.make_async_remote_copy(
            src_ref=first_out.at[:, place],
            dst_ref=first_in.at[:, place],
            send_sem=first_send_sem.at[place],
            recv_sem=first_recv_sem.at[place],
            device_id=device(kind, shift),
            device_id_type=MESH,
        )

    def copy(slot, kind, shift):
        source = PLACES[kind, shift]
        target = PLACES[kind, (4 - shift) % 4]
        return pltpu.make_async_remote_copy(
            src_ref=out_buf.at[slot, source],
            dst_ref=in_buf.at[slot, target],
            send_sem=send_sem.at[slot, source],
            recv_sem=recv_sem.at[slot, target],
            device_id=device(kind, shift),
            device_id_type=MESH,
        )

    def arrival(slot, kind, shift):
        place = PLACES[kind, shift]
        return pltpu.make_async_remote_copy(
            src_ref=out_buf.at[slot, place],
            dst_ref=in_buf.at[slot, place],
            send_sem=send_sem.at[slot, place],
            recv_sem=recv_sem.at[slot, place],
            device_id=device(kind, shift),
            device_id_type=MESH,
        )

    each_peer(lambda kind, shift: first_copy(kind, shift).start())
    first_in[:, here] = first_out[:, here]

    for pull in pulls[2:8]:
        pull.wait()
    jac[...] = jnp.zeros_like(jac)
    for face in range(6):
        jac[PAD * face : PAD * face + TRACE, :BLOCK] = jac_ref[face]
    width = 6 * PAD
    jac_hi, jac_lo = split(jac[...].T[:BLOCK])
    jac2[:BLOCK] = jac_hi
    jac2[BLOCK:STACK] = jnp.zeros((STACK - BLOCK, width), BF16)
    jac2[STACK : STACK + BLOCK] = jac_lo
    jac2[STACK + BLOCK :] = jnp.zeros((STACK - BLOCK, width), BF16)
    jac3[:, :width] = jac_hi
    jac3[:, width : 2 * width] = jac_lo
    jac3[:, 2 * width :] = jac_hi

    row = lax.broadcasted_iota(jnp.int32, (EL, EL), 0)
    for face in range(6):
        one = jnp.where(link_ref[face : face + 1, :] == row, 1.0, 0.0).astype(BF16)
        links[face, :EL, :] = one
        links[face, EL:, :] = one

    def tiled(rows):
        low = lax.broadcasted_iota(jnp.int32, (8, rows.shape[1]), 0) < CAP
        mixed = [
            jnp.where(low, rows[16 * k : 16 * k + 8], rows[16 * k + 8 : 16 * k + 16])
            for k in range(3)
        ]
        return jnp.concatenate([rows, rows, *mixed, jnp.zeros_like(mixed[0])], axis=0)

    to_rows(recv_ref)
    face_lane = lax.broadcasted_iota(jnp.int32, (ROWS, width), 1) // PAD
    first_half = lax.broadcasted_iota(jnp.int32, (ROWS, EL), 0) % 8 < CAP
    for level in range(LEVELS):
        column = index[:, level : level + 1]
        hit = jnp.zeros((ROWS, EL), F32)
        gain = jnp.zeros((ROWS, EL), F32)
        for face in range(6):
            mine = column == lane + EL * face
            hit = jnp.where(mine, 1.0, hit)
            gain = jnp.where(mine, weight_ref[face : face + 1, :], gain)
        drops[level] = jnp.where(first_half, hit, 0.0).astype(BF16)
        late_drops[level] = tiled(hit[:HALF]).astype(BF16)
        scale = jnp.sum(gain, axis=1, keepdims=True)
        factors[level] = jnp.where(column // EL == face_lane, scale, 0.0)
    late_lane[...] = (tiled(index[:HALF, :]).T)[:8] % EL

    def local_flow():
        parts_hi = []
        parts_lo = []
        for face in range(6):
            other = face + 1 - 2 * (face % 2)
            hi, lo = split(table[other])
            moved = dot(jnp.concatenate([hi, lo], axis=1), links[face])
            hi, lo = split(moved * weight_ref[face : face + 1, :])
            parts_hi.append(hi)
            parts_lo.append(lo)
        hi = jnp.concatenate(parts_hi, axis=0)
        lo = jnp.concatenate(parts_lo, axis=0)
        return dot(jac3[...], jnp.concatenate([hi, hi, lo], axis=0))

    def scattered(values, where_to):
        hi, lo = split(values)
        return dot(
            jnp.concatenate([hi, lo], axis=1), jnp.concatenate([where_to, where_to], axis=0)
        )

    def spread(block, factor, tile=lambda rows: rows):
        hi, lo = split(tile(jnp.concatenate([block] * 3, axis=1) * factor))
        both = dot_t(jac2[...], hi)
        return both[:BLOCK] + both[STACK : STACK + BLOCK] + dot_t(jac2[:BLOCK], lo)

    def first_flow(low, high):
        count = LEVELS * (high - low) * 8
        block = first_in[:, low:high].reshape(count, EL)
        values = spread(block, factors[:, 8 * low : 8 * high].reshape(count, width))
        return scattered(values, drops[:, 8 * low : 8 * high].reshape(count, EL))

    known = right_ref[...] - local_flow()
    each_early(lambda kind, shift: first_arrival(kind, shift).wait_recv())
    ghost = first_flow(len(LATE), GROUPS)
    each_late(lambda kind, shift: first_arrival(kind, shift).wait_recv())
    ghost = ghost + first_flow(0, len(LATE))
    total[...] = ghost
    solve_in[...] = known - ghost
    each_peer(lambda kind, shift: first_arrival(kind, shift).wait_send())
    pulls[8].wait()

    chunk = 45

    lanes8 = lax.broadcasted_iota(jnp.int32, (8, EL), 1)
    tile_at = lanes8 // 8
    second = (lanes8 // 4) % 2
    place_of = jnp.where(tile_at < 12, 2 * (tile_at // 6) + second, jnp.where(tile_at < 15, 4, 7))
    def merged(pieces, place):
        got = pieces[0]
        for part in range(1, len(pieces)):
            got = jnp.where(place == part, pieces[part], got)
        return got

    def tail_of(values):
        return jnp.concatenate([values, jnp.zeros((136 - BLOCK, EL), F32)], axis=0)

    def choose(level):
        where_from = jnp.broadcast_to(late_lane[pl.ds(level, 1), :], (8, EL))

        def moved(values):
            return jnp.take_along_axis(values, where_from, axis=1)

        def rows(at, carry):
            for k in range(chunk):
                i = at * chunk + k
                for m in range(3):
                    late_chosen[level, i, 8 * m : 8 * m + 8, :] = merged(
                        [
                            moved(inverse[i, 8 * b : 8 * b + 8, :])
                            for b in range(5 * m, 5 * m + 5)
                        ],
                        place_of,
                    )
                late_chosen[level, i, 24:32, :] = merged(
                    [moved(inverse[i, 120:128, :]), moved(tail_of(inverse[i, 128:BLOCK, :]))],
                    place_of,
                )
            return carry

        lax.fori_loop(0, BLOCK // chunk, rows, 0)

    def fold(values):
        pieces = [
            merged([values[8 * b : 8 * b + 8] for b in range(5 * m, 5 * m + 5)], place_of)
            for m in range(3)
        ]
        last = merged([values[120:128], tail_of(values[128:BLOCK])], place_of)
        pieces.append(jnp.where(place_of < 2, last, 0.0))
        return jnp.concatenate(pieces, axis=0)

    at8 = lax.broadcasted_iota(jnp.int32, (8, EL), 0)

    def gathered_sums(parts):
        top = at8 < 4
        fours = [
            jnp.where(top, parts[k], parts[k + 4])
            + pltpu.roll(jnp.where(top, parts[k + 4], parts[k]), 4, 0)
            for k in range(4)
        ]
        top = at8 % 4 < 2
        twos = [
            jnp.where(
                top,
                fours[k] + pltpu.roll(fours[k], 6, 0),
                fours[k + 2] + pltpu.roll(fours[k + 2], 2, 0),
            )
            for k in range(2)
        ]
        return jnp.where(
            at8 % 2 < 1, twos[0] + pltpu.roll(twos[0], 7, 0), twos[1] + pltpu.roll(twos[1], 1, 0)
        )

    def products(matrix, i, tiles):
        got = None
        for m, tile in enumerate(tiles):
            one = matrix[i, 8 * m : 8 * m + 8, :] * tile
            got = one if got is None else got + one
        return got

    def part_multiply(matrix, vector, target):
        tiles = [vector[8 * m : 8 * m + 8] for m in range(4)]

        def rows(at, carry):
            for k in range(16):
                g = at * 16 + k
                target[pl.ds(pl.multiple_of(8 * g, 8), 8), :] = gathered_sums(
                    [products(matrix, 8 * g + r, tiles) for r in range(8)]
                )
            return carry

        rows(0, 0)
        last = [products(matrix, 128 + r, tiles) for r in range(BLOCK - 128)]
        target[128:BLOCK, :] = gathered_sums(last + [jnp.zeros((8, EL), F32)])[: BLOCK - 128]

    def multiply():
        vector = solve_in[...]
        tiles = [vector[8 * m : 8 * m + 8] for m in range(16)]
        last_tile = tail_of(vector[128:BLOCK])

        def sums(i):
            last = tail_of(inverse[i, 128:BLOCK, :]) * last_tile
            return products(inverse, i, tiles) + last

        def rows(at, carry):
            for k in range(4):
                g = at * 4 + k
                update[pl.ds(pl.multiple_of(8 * g, 8), 8), :] = gathered_sums(
                    [sums(8 * g + r) for r in range(8)]
                )
            return carry

        lax.fori_loop(0, 4, rows, 0)
        last = [sums(128 + r) for r in range(BLOCK - 128)]
        update[128:BLOCK, :] = gathered_sums(last + [jnp.zeros((8, EL), F32)])[: BLOCK - 128]

    def level_of(step):
        return jnp.where(step < LEVELS, step, 2 * LEVELS - 1 - step)

    multiply()
    state[...] = jnp.where(level_ref[...] == 0, update[...], state[...])

    def level_step(step, carry):
        level = level_of(step)
        slot = lax.rem(step, 2)

        fill_table()
        fresh = packed(level).reshape(GROUPS, 8, EL)
        out_buf[slot] = fresh - first_out[level]
        each_peer(lambda kind, shift: copy(slot, kind, shift).start())
        first_out[level] = fresh
        in_buf[slot, here] = out_buf[slot, here]

        @pl.when(step >= 1)
        def _():
            each_peer(lambda kind, shift: arrival(1 - slot, kind, shift).wait_send())

        @pl.when(step == LEVELS - 1)
        def _():
            forward_ref[...] = state[...]

        @pl.when(step > 0)
        def _():
            before = level_of(step - 1)
            once = jnp.where(place_of[:1] == 0, late_spread[...], 0.0)
            total[...] = total[...] + early_flow[...] + scattered(once, late_drops[before])

        solve_in[...] = right_ref[...] - local_flow() - total[...]
        @pl.when(step < LEVELS)
        def _():
            choose(level)

        each_early(lambda kind, shift: arrival(slot, kind, shift).wait_recv())
        block = in_buf[slot, len(LATE) :].reshape(HALF, EL)
        flow = scattered(spread(block, factors[level, HALF:]), drops[level, HALF:])
        early_flow[...] = flow
        solve_in[...] = solve_in[...] - flow
        multiply()
        each_late(lambda kind, shift: arrival(slot, kind, shift).wait_recv())
        block = in_buf[slot, : len(LATE)].reshape(HALF, EL)
        values = spread(block, factors[level, :HALF], tiled)
        late_spread[...] = values
        part_multiply(late_chosen.at[level], fold(values), late_part)
        fresh = update[...] - scattered(late_part[...], late_drops[level])
        state[...] = jnp.where(level_ref[...] == level_of(step + 1), fresh, state[...])
        return carry

    lax.fori_loop(0, 2 * LEVELS - 1, level_step, 0)
    swept_ref[...] = state[...]
    each_peer(lambda kind, shift: arrival(0, kind, shift).wait_send())


def hand_on(first_ref, second_ref, first_out, second_out, sems):
    copies = (
        pltpu.make_async_copy(first_ref, first_out, sems.at[0]),
        pltpu.make_async_copy(second_ref, second_out, sems.at[1]),
    )
    for one in copies:
        one.start()
    for one in copies:
        one.wait()


def body(
    start_state,
    right_side,
    block_inverse,
    lifted_flux_jacobian,
    face_weight,
    dep_level,
    face_link,
    send_list,
    recv_list,
):
    vmem = pl.BlockSpec(memory_space=pltpu.VMEM)
    out = jax.ShapeDtypeStruct((BLOCK, EL), F32)
    width = 6 * PAD
    lists = send_list.shape[1]
    hbm = pl.BlockSpec(memory_space=pl.ANY)
    first, second = pl.pallas_call(
        kernel,
        out_shape=(out, out),
        in_specs=[hbm] * 9,
        out_specs=(vmem, vmem),
        scratch_shapes=[
            pltpu.VMEM((BLOCK, EL), F32),
            pltpu.VMEM((6, TRACE, BLOCK), F32),
            pltpu.VMEM((6, EL), F32),
            pltpu.VMEM((1, EL), jnp.int32),
            pltpu.VMEM((6, EL), jnp.int32),
            pltpu.VMEM((LEVELS, lists), jnp.int32),
            pltpu.VMEM((LEVELS, lists), jnp.int32),
            pltpu.VMEM((BLOCK, BLOCK, EL), F32),
            pltpu.VMEM((BLOCK, EL), F32),
            pltpu.VMEM((6, PAD, EL), F32),
            pltpu.VMEM((BLOCK, EL), F32),
            pltpu.VMEM((BLOCK, EL), F32),
            pltpu.VMEM((width, 256), F32),
            pltpu.VMEM((2 * STACK, width), BF16),
            pltpu.VMEM((BLOCK, 3 * width), BF16),
            pltpu.VMEM((6, 2 * EL, EL), BF16),
            pltpu.VMEM((LEVELS, ROWS, 6 * EL), BF16),
            pltpu.VMEM((LEVELS, ROWS, EL), BF16),
            pltpu.VMEM((LEVELS, EL, EL), BF16),
            pltpu.VMEM((8, EL), jnp.int32),
            pltpu.VMEM((BLOCK, EL), F32),
            pltpu.VMEM((BLOCK, EL), F32),
            pltpu.VMEM((LEVELS, BLOCK, 32, EL), F32),
            pltpu.VMEM((BLOCK, EL), F32),
            pltpu.VMEM((LEVELS, ROWS, width), F32),
            pltpu.VMEM((BLOCK, EL), F32),
            pltpu.VMEM((ROWS, EL), jnp.int32),
            pltpu.VMEM((2, GROUPS, 8, EL), F32),
            pltpu.VMEM((2, GROUPS, 8, EL), F32),
            pltpu.VMEM((LEVELS, GROUPS, 8, EL), F32),
            pltpu.VMEM((LEVELS, GROUPS, 8, EL), F32),
            pltpu.SemaphoreType.DMA((9,)),
            pltpu.SemaphoreType.DMA((2, GROUPS)),
            pltpu.SemaphoreType.DMA((2, GROUPS)),
            pltpu.SemaphoreType.DMA((GROUPS,)),
            pltpu.SemaphoreType.DMA((GROUPS,)),
        ],
        compiler_params=pltpu.CompilerParams(
            collective_id=0, has_side_effects=True, vmem_limit_bytes=60 << 20
        ),
    )(
        start_state,
        right_side,
        block_inverse,
        lifted_flux_jacobian.swapaxes(1, 2),
        face_weight,
        dep_level.reshape(1, EL),
        face_link,
        send_list,
        recv_list,
    )
    return pl.pallas_call(
        hand_on,
        out_shape=(out, out),
        in_specs=[vmem, vmem],
        out_specs=(hbm, hbm),
        scratch_shapes=[pltpu.SemaphoreType.DMA((2,))],
    )(first, second)


def solution(mesh):
    return jax.shard_map(
        body,
        mesh=mesh,
        in_specs=(
            P(None, ("curve", "slab")),
            P(None, ("curve", "slab")),
            P(None, None, ("curve", "slab")),
            P(),
            P(None, ("curve", "slab")),
            P(("curve", "slab")),
            P(None, ("curve", "slab")),
            P(None, ("curve", "slab")),
            P(None, ("curve", "slab")),
        ),
        out_specs=(P(None, ("curve", "slab")), P(None, ("curve", "slab"))),
        check_vma=False,
    )
```

```python
import functools

import jax
import jax.numpy as jnp
from jax import lax
from jax.experimental import pallas as pl
from jax.experimental.pallas import tpu as pltpu
from jax.sharding import PartitionSpec as P

VARS = 5
TRACE = 45
BLOCK = 135
EL = 128
LEVELS = 8
CAP = 4
PAD = 64
GROUPS = 12
ROWS = 8 * GROUPS
FAR, OWN, PAIR = range(3)
LATE = ((FAR, 2), (FAR, 1), (FAR, 3), (FAR, 0), (OWN, 2), (PAIR, 2))
EARLY = ((OWN, 1), (OWN, 3), (PAIR, 1), (PAIR, 3), (PAIR, 0), (OWN, 0))
PLACES = {key: at for at, key in enumerate(LATE + EARLY)}
HALF = 8 * len(LATE)
STACK = 144
MESH = pl.DeviceIdType.MESH
F32 = jnp.float32
BF16 = jnp.bfloat16


def split(x):
    hi = x.astype(BF16)
    lo = (x - hi.astype(F32)).astype(BF16)
    return hi, lo


def dot(a, b):
    return lax.dot_general(a, b, (((1,), (0,)), ((), ())), preferred_element_type=F32)


def dot_t(a, b):
    return lax.dot_general(a, b, (((1,), (1,)), ((), ())), preferred_element_type=F32)


def kernel(
    start_hbm,
    right_hbm,
    inverse_hbm,
    jac_hbm,
    weight_hbm,
    level_hbm,
    link_hbm,
    send_hbm,
    recv_hbm,
    forward_ref,
    swept_ref,
    right_ref,
    jac_ref,
    weight_ref,
    level_ref,
    link_ref,
    send_ref,
    recv_ref,
    inverse,
    state,
    table,
    solve_in,
    update,
    jac,
    jac2,
    jac3,
    links,
    picks,
    drops,
    late_drops,
    late_lane,
    early_flow,
    late_spread,
    late_chosen,
    late_part,
    factors,
    total,
    index,
    out_buf,
    in_buf,
    sent,
    first_out,
    first_in,
    first_drops,
    first_factors,
    input_sems,
    send_sem,
    recv_sem,
    first_send_sem,
    first_recv_sem,
):
    curves = lax.axis_size("curve")
    slabs = lax.axis_size("slab")
    my_curve = lax.axis_index("curve")
    my_slab = lax.axis_index("slab")
    odd = lax.rem(my_curve, 2)
    far_curve = my_curve + 2 * odd - 1
    pair_curve = my_curve + 1 - 2 * odd
    has_far = jnp.logical_and(far_curve >= 0, far_curve < curves)
    kind_curve = (far_curve, my_curve, pair_curve)
    here = PLACES[OWN, 0]

    pulls = [
        pltpu.make_async_copy(source, target, input_sems.at[at])
        for at, (source, target) in enumerate(
            (
                (start_hbm, state),
                (send_hbm, send_ref),
                (recv_hbm, recv_ref),
                (jac_hbm, jac_ref),
                (weight_hbm, weight_ref),
                (link_hbm, link_ref),
                (right_hbm, right_ref),
                (level_hbm, level_ref),
                (inverse_hbm, inverse),
            )
        )
    ]
    for pull in pulls:
        pull.start()

    @pl.when(jnp.logical_not(has_far))
    def _():
        in_buf[:, :4] = jnp.zeros((2, 4, 8, EL), F32)
        first_in[:, :4] = jnp.zeros((LEVELS // 2, 4, 8, EL), F32)

    def each_late(act):
        @pl.when(has_far)
        def _():
            for kind, shift in LATE[:4]:
                act(kind, shift)

        for kind, shift in LATE[4:]:
            act(kind, shift)

    def each_early(act):
        for kind, shift in EARLY[:-1]:
            act(kind, shift)

    def each_peer(act):
        each_late(act)
        each_early(act)

    def device(kind, shift):
        return (kind_curve[kind], lax.rem(my_slab + shift, slabs))

    barrier = pltpu.get_barrier_semaphore()
    each_peer(
        lambda kind, shift: pl.semaphore_signal(
            barrier, inc=1, device_id=device(kind, shift), device_id_type=MESH
        )
    )

    lane = lax.broadcasted_iota(jnp.int32, (ROWS, EL), 1)

    def to_rows(list_ref):
        shift = lax.rem((curves + 1 - my_curve) * (slabs * CAP), curves * slabs * CAP)
        near = pltpu.roll(list_ref[...], shift, 1)[:, :EL]
        tall = jnp.concatenate([near] * 16, axis=0).T
        step = slabs * CAP
        low, mid, high = (tall[step * k : step * (k + 1), :] for k in range(3))
        ordered = (jnp.where(odd == 1, high, low), mid, jnp.where(odd == 1, low, high))
        for kind in range(3):
            block = ordered[kind]
            turned = block
            for z in range(1, slabs):
                other = jnp.concatenate([block[CAP * z :], block[: CAP * z]], axis=0)
                turned = jnp.where(my_slab == z, other, turned)
            for shift in range(slabs):
                group = PLACES[kind, shift]
                four = turned[CAP * shift : CAP * (shift + 1), :]
                index[8 * group : 8 * group + CAP, :] = four
                index[8 * group + CAP : 8 * group + 8, :] = four

    table[...] = jnp.zeros_like(table)

    def fill_table():
        for side in range(2):
            for q in range(9):
                table[side, pl.ds(q, VARS, stride=9), :] = state[
                    pl.ds(18 * side + q, VARS, stride=27), :
                ]
            for q in range(3):
                table[2 + side, pl.ds(q, 15, stride=3), :] = state[
                    pl.ds(6 * side + q, 15, stride=9), :
                ]
            table[4 + side, :TRACE, :] = state[pl.ds(2 * side, TRACE, stride=3), :]

    for pull in pulls[:2]:
        pull.wait()
    fill_table()
    to_rows(send_ref)
    for level in range(LEVELS):
        column = index[:, level : level + 1]
        for face in range(6):
            picks[level, :, EL * face : EL * (face + 1)] = (
                jnp.where(column == lane + EL * face, 1.0, 0.0).astype(BF16)
            )

    def packed(level):
        hi, lo = split(jnp.concatenate([table[face] for face in range(6)], axis=1))
        halves = dot_t(picks[level], jnp.concatenate([hi, lo], axis=0))
        return halves + pltpu.roll(halves, PAD, 1)

    first_half = lax.broadcasted_iota(jnp.int32, (ROWS, EL), 0) % 8 < CAP
    for duo in range(LEVELS // 2):
        even, after = packed(2 * duo), packed(2 * duo + 1)
        sent[2 * duo] = even.reshape(GROUPS, 8, EL)
        sent[2 * duo + 1] = after.reshape(GROUPS, 8, EL)
        first_out[duo] = jnp.where(first_half, even, after).reshape(GROUPS, 8, EL)

    @pl.when(has_far)
    def _():
        pl.semaphore_wait(barrier, 3 * slabs - 1)

    @pl.when(jnp.logical_not(has_far))
    def _():
        pl.semaphore_wait(barrier, 2 * slabs - 1)

    def first_copy(kind, shift):
        source = PLACES[kind, shift]
        target = PLACES[kind, (4 - shift) % 4]
        return pltpu.make_async_remote_copy(
            src_ref=first_out.at[:, source],
            dst_ref=first_in.at[:, target],
            send_sem=first_send_sem.at[source],
            recv_sem=first_recv_sem.at[target],
            device_id=device(kind, shift),
            device_id_type=MESH,
        )

    def first_arrival(kind, shift):
        place = PLACES[kind, shift]
        return pltpu.make_async_remote_copy(
            src_ref=first_out.at[:, place],
            dst_ref=first_in.at[:, place],
            send_sem=first_send_sem.at[place],
            recv_sem=first_recv_sem.at[place],
            device_id=device(kind, shift),
            device_id_type=MESH,
        )

    def copy(slot, kind, shift):
        source = PLACES[kind, shift]
        target = PLACES[kind, (4 - shift) % 4]
        return pltpu.make_async_remote_copy(
            src_ref=out_buf.at[slot, source],
            dst_ref=in_buf.at[slot, target],
            send_sem=send_sem.at[slot, source],
            recv_sem=recv_sem.at[slot, target],
            device_id=device(kind, shift),
            device_id_type=MESH,
        )

    def arrival(slot, kind, shift):
        place = PLACES[kind, shift]
        return pltpu.make_async_remote_copy(
            src_ref=out_buf.at[slot, place],
            dst_ref=in_buf.at[slot, place],
            send_sem=send_sem.at[slot, place],
            recv_sem=recv_sem.at[slot, place],
            device_id=device(kind, shift),
            device_id_type=MESH,
        )

    each_peer(lambda kind, shift: first_copy(kind, shift).start())
    first_in[:, here] = first_out[:, here]

    for pull in pulls[2:8]:
        pull.wait()
    jac[...] = jnp.zeros_like(jac)
    for face in range(6):
        jac[PAD * face : PAD * face + TRACE, :BLOCK] = jac_ref[face]
    width = 6 * PAD
    jac_hi, jac_lo = split(jac[...].T[:BLOCK])
    jac2[:BLOCK] = jac_hi
    jac2[BLOCK:STACK] = jnp.zeros((STACK - BLOCK, width), BF16)
    jac2[STACK : STACK + BLOCK] = jac_lo
    jac2[STACK + BLOCK :] = jnp.zeros((STACK - BLOCK, width), BF16)
    jac3[:, :width] = jac_hi
    jac3[:, width : 2 * width] = jac_lo
    jac3[:, 2 * width :] = jac_hi

    row = lax.broadcasted_iota(jnp.int32, (EL, EL), 0)
    for face in range(6):
        one = jnp.where(link_ref[face : face + 1, :] == row, 1.0, 0.0).astype(BF16)
        links[face, :EL, :] = one
        links[face, EL:, :] = one

    def tiled(rows):
        low = lax.broadcasted_iota(jnp.int32, (8, rows.shape[1]), 0) < CAP
        mixed = [
            jnp.where(low, rows[16 * k : 16 * k + 8], rows[16 * k + 8 : 16 * k + 16])
            for k in range(3)
        ]
        return jnp.concatenate([rows, rows, *mixed, jnp.zeros_like(mixed[0])], axis=0)

    to_rows(recv_ref)
    face_lane = lax.broadcasted_iota(jnp.int32, (ROWS, width), 1) // PAD
    wide_half = lax.broadcasted_iota(jnp.int32, (ROWS, width), 0) % 8 < CAP
    for level in range(LEVELS):
        column = index[:, level : level + 1]
        hit = jnp.zeros((ROWS, EL), F32)
        gain = jnp.zeros((ROWS, EL), F32)
        for face in range(6):
            mine = column == lane + EL * face
            hit = jnp.where(mine, 1.0, hit)
            gain = jnp.where(mine, weight_ref[face : face + 1, :], gain)
        drops[level] = jnp.where(first_half, hit, 0.0).astype(BF16)
        late_drops[level] = tiled(hit[:HALF]).astype(BF16)
        scale = jnp.sum(gain, axis=1, keepdims=True)
        factor = jnp.where(column // EL == face_lane, scale, 0.0)
        factors[level] = factor
        if level % 2 == 1:
            first_drops[level // 2] = jnp.where(first_half, even_hit, hit).astype(BF16)
            first_factors[level // 2] = jnp.where(wide_half, even_factor, factor)
        even_hit, even_factor = hit, factor
    late_lane[...] = (tiled(index[:HALF, :]).T)[:8] % EL

    def local_flow():
        parts_hi = []
        parts_lo = []
        for face in range(6):
            other = face + 1 - 2 * (face % 2)
            hi, lo = split(table[other])
            moved = dot(jnp.concatenate([hi, lo], axis=1), links[face])
            hi, lo = split(moved * weight_ref[face : face + 1, :])
            parts_hi.append(hi)
            parts_lo.append(lo)
        hi = jnp.concatenate(parts_hi, axis=0)
        lo = jnp.concatenate(parts_lo, axis=0)
        return dot(jac3[...], jnp.concatenate([hi, hi, lo], axis=0))

    def scattered(values, where_to):
        hi, lo = split(values)
        return dot(
            jnp.concatenate([hi, lo], axis=1), jnp.concatenate([where_to, where_to], axis=0)
        )

    def spread(block, factor, tile=lambda rows: rows):
        hi, lo = split(tile(jnp.concatenate([block] * 3, axis=1) * factor))
        both = dot_t(jac2[...], hi)
        return both[:BLOCK] + both[STACK : STACK + BLOCK] + dot_t(jac2[:BLOCK], lo)

    def first_flow(low, high):
        count = LEVELS // 2 * (high - low) * 8
        block = first_in[:, low:high].reshape(count, EL)
        values = spread(block, first_factors[:, 8 * low : 8 * high].reshape(count, width))
        return scattered(values, first_drops[:, 8 * low : 8 * high].reshape(count, EL))

    known = right_ref[...] - local_flow()
    each_early(lambda kind, shift: first_arrival(kind, shift).wait_recv())
    ghost = first_flow(len(LATE), GROUPS)
    each_late(lambda kind, shift: first_arrival(kind, shift).wait_recv())
    ghost = ghost + first_flow(0, len(LATE))
    total[...] = ghost
    solve_in[...] = known - ghost
    each_peer(lambda kind, shift: first_arrival(kind, shift).wait_send())
    pulls[8].wait()

    chunk = 45

    lanes8 = lax.broadcasted_iota(jnp.int32, (8, EL), 1)
    tile_at = lanes8 // 8
    second = (lanes8 // 4) % 2
    place_of = jnp.where(tile_at < 12, 2 * (tile_at // 6) + second, jnp.where(tile_at < 15, 4, 7))
    def merged(pieces, place):
        got = pieces[0]
        for part in range(1, len(pieces)):
            got = jnp.where(place == part, pieces[part], got)
        return got

    def tail_of(values):
        return jnp.concatenate([values, jnp.zeros((136 - BLOCK, EL), F32)], axis=0)

    def choose(level):
        where_from = jnp.broadcast_to(late_lane[pl.ds(level, 1), :], (8, EL))

        def moved(values):
            return jnp.take_along_axis(values, where_from, axis=1)

        def rows(at, carry):
            for k in range(chunk):
                i = at * chunk + k
                for m in range(3):
                    late_chosen[level, i, 8 * m : 8 * m + 8, :] = merged(
                        [
                            moved(inverse[i, 8 * b : 8 * b + 8, :])
                            for b in range(5 * m, 5 * m + 5)
                        ],
                        place_of,
                    )
                late_chosen[level, i, 24:32, :] = merged(
                    [moved(inverse[i, 120:128, :]), moved(tail_of(inverse[i, 128:BLOCK, :]))],
                    place_of,
                )
            return carry

        lax.fori_loop(0, BLOCK // chunk, rows, 0)

    def fold(values):
        pieces = [
            merged([values[8 * b : 8 * b + 8] for b in range(5 * m, 5 * m + 5)], place_of)
            for m in range(3)
        ]
        last = merged([values[120:128], tail_of(values[128:BLOCK])], place_of)
        pieces.append(jnp.where(place_of < 2, last, 0.0))
        return jnp.concatenate(pieces, axis=0)

    at8 = lax.broadcasted_iota(jnp.int32, (8, EL), 0)

    def gathered_sums(parts):
        top = at8 < 4
        fours = [
            jnp.where(top, parts[k], parts[k + 4])
            + pltpu.roll(jnp.where(top, parts[k + 4], parts[k]), 4, 0)
            for k in range(4)
        ]
        top = at8 % 4 < 2
        twos = [
            jnp.where(
                top,
                fours[k] + pltpu.roll(fours[k], 6, 0),
                fours[k + 2] + pltpu.roll(fours[k + 2], 2, 0),
            )
            for k in range(2)
        ]
        return jnp.where(
            at8 % 2 < 1, twos[0] + pltpu.roll(twos[0], 7, 0), twos[1] + pltpu.roll(twos[1], 1, 0)
        )

    def products(matrix, i, tiles):
        got = None
        for m, tile in enumerate(tiles):
            one = matrix[i, 8 * m : 8 * m + 8, :] * tile
            got = one if got is None else got + one
        return got

    def part_multiply(matrix, vector, target):
        tiles = [vector[8 * m : 8 * m + 8] for m in range(4)]

        def rows(at, carry):
            for k in range(16):
                g = at * 16 + k
                target[pl.ds(pl.multiple_of(8 * g, 8), 8), :] = gathered_sums(
                    [products(matrix, 8 * g + r, tiles) for r in range(8)]
                )
            return carry

        rows(0, 0)
        last = [products(matrix, 128 + r, tiles) for r in range(BLOCK - 128)]
        target[128:BLOCK, :] = gathered_sums(last + [jnp.zeros((8, EL), F32)])[: BLOCK - 128]

    def multiply():
        vector = solve_in[...]
        tiles = [vector[8 * m : 8 * m + 8] for m in range(16)]
        last_tile = tail_of(vector[128:BLOCK])

        def sums(i):
            last = tail_of(inverse[i, 128:BLOCK, :]) * last_tile
            return products(inverse, i, tiles) + last

        def rows(at, carry):
            for k in range(4):
                g = at * 4 + k
                update[pl.ds(pl.multiple_of(8 * g, 8), 8), :] = gathered_sums(
                    [sums(8 * g + r) for r in range(8)]
                )
            return carry

        lax.fori_loop(0, 4, rows, 0)
        last = [sums(128 + r) for r in range(BLOCK - 128)]
        update[128:BLOCK, :] = gathered_sums(last + [jnp.zeros((8, EL), F32)])[: BLOCK - 128]

    def level_of(step):
        return jnp.where(step < LEVELS, step, 2 * LEVELS - 1 - step)

    multiply()
    state[...] = jnp.where(level_ref[...] == 0, update[...], state[...])

    def level_step(step, carry):
        level = level_of(step)
        slot = lax.rem(step, 2)

        fill_table()
        fresh = packed(level).reshape(GROUPS, 8, EL)
        out_buf[slot] = fresh - sent[level]
        each_peer(lambda kind, shift: copy(slot, kind, shift).start())
        sent[level] = fresh
        in_buf[slot, here] = out_buf[slot, here]

        @pl.when(step >= 1)
        def _():
            each_peer(lambda kind, shift: arrival(1 - slot, kind, shift).wait_send())

        @pl.when(step == LEVELS - 1)
        def _():
            forward_ref[...] = state[...]

        @pl.when(step > 0)
        def _():
            before = level_of(step - 1)
            once = jnp.where(place_of[:1] == 0, late_spread[...], 0.0)
            total[...] = total[...] + early_flow[...] + scattered(once, late_drops[before])

        solve_in[...] = right_ref[...] - local_flow() - total[...]
        @pl.when(step < LEVELS)
        def _():
            choose(level)

        each_early(lambda kind, shift: arrival(slot, kind, shift).wait_recv())
        block = in_buf[slot, len(LATE) :].reshape(HALF, EL)
        flow = scattered(spread(block, factors[level, HALF:]), drops[level, HALF:])
        early_flow[...] = flow
        solve_in[...] = solve_in[...] - flow
        multiply()
        each_late(lambda kind, shift: arrival(slot, kind, shift).wait_recv())
        block = in_buf[slot, : len(LATE)].reshape(HALF, EL)
        values = spread(block, factors[level, :HALF], tiled)
        late_spread[...] = values
        part_multiply(late_chosen.at[level], fold(values), late_part)
        fresh = update[...] - scattered(late_part[...], late_drops[level])
        state[...] = jnp.where(level_ref[...] == level_of(step + 1), fresh, state[...])
        return carry

    lax.fori_loop(0, 2 * LEVELS - 1, level_step, 0)
    swept_ref[...] = state[...]
    each_peer(lambda kind, shift: arrival(0, kind, shift).wait_send())


def hand_on(first_ref, second_ref, first_out, second_out, sems):
    copies = (
        pltpu.make_async_copy(first_ref, first_out, sems.at[0]),
        pltpu.make_async_copy(second_ref, second_out, sems.at[1]),
    )
    for one in copies:
        one.start()
    for one in copies:
        one.wait()


def body(
    start_state,
    right_side,
    block_inverse,
    lifted_flux_jacobian,
    face_weight,
    dep_level,
    face_link,
    send_list,
    recv_list,
):
    vmem = pl.BlockSpec(memory_space=pltpu.VMEM)
    out = jax.ShapeDtypeStruct((BLOCK, EL), F32)
    width = 6 * PAD
    lists = send_list.shape[1]
    hbm = pl.BlockSpec(memory_space=pl.ANY)
    first, second = pl.pallas_call(
        kernel,
        out_shape=(out, out),
        in_specs=[hbm] * 9,
        out_specs=(vmem, vmem),
        scratch_shapes=[
            pltpu.VMEM((BLOCK, EL), F32),
            pltpu.VMEM((6, TRACE, BLOCK), F32),
            pltpu.VMEM((6, EL), F32),
            pltpu.VMEM((1, EL), jnp.int32),
            pltpu.VMEM((6, EL), jnp.int32),
            pltpu.VMEM((LEVELS, lists), jnp.int32),
            pltpu.VMEM((LEVELS, lists), jnp.int32),
            pltpu.VMEM((BLOCK, BLOCK, EL), F32),
            pltpu.VMEM((BLOCK, EL), F32),
            pltpu.VMEM((6, PAD, EL), F32),
            pltpu.VMEM((BLOCK, EL), F32),
            pltpu.VMEM((BLOCK, EL), F32),
            pltpu.VMEM((width, 256), F32),
            pltpu.VMEM((2 * STACK, width), BF16),
            pltpu.VMEM((BLOCK, 3 * width), BF16),
            pltpu.VMEM((6, 2 * EL, EL), BF16),
            pltpu.VMEM((LEVELS, ROWS, 6 * EL), BF16),
            pltpu.VMEM((LEVELS, ROWS, EL), BF16),
            pltpu.VMEM((LEVELS, EL, EL), BF16),
            pltpu.VMEM((8, EL), jnp.int32),
            pltpu.VMEM((BLOCK, EL), F32),
            pltpu.VMEM((BLOCK, EL), F32),
            pltpu.VMEM((LEVELS, BLOCK, 32, EL), F32),
            pltpu.VMEM((BLOCK, EL), F32),
            pltpu.VMEM((LEVELS, ROWS, width), F32),
            pltpu.VMEM((BLOCK, EL), F32),
            pltpu.VMEM((ROWS, EL), jnp.int32),
            pltpu.VMEM((2, GROUPS, 8, EL), F32),
            pltpu.VMEM((2, GROUPS, 8, EL), F32),
            pltpu.VMEM((LEVELS, GROUPS, 8, EL), F32),
            pltpu.VMEM((LEVELS // 2, GROUPS, 8, EL), F32),
            pltpu.VMEM((LEVELS // 2, GROUPS, 8, EL), F32),
            pltpu.VMEM((LEVELS // 2, ROWS, EL), BF16),
            pltpu.VMEM((LEVELS // 2, ROWS, width), F32),
            pltpu.SemaphoreType.DMA((9,)),
            pltpu.SemaphoreType.DMA((2, GROUPS)),
            pltpu.SemaphoreType.DMA((2, GROUPS)),
            pltpu.SemaphoreType.DMA((GROUPS,)),
            pltpu.SemaphoreType.DMA((GROUPS,)),
        ],
        compiler_params=pltpu.CompilerParams(
            collective_id=0, has_side_effects=True, vmem_limit_bytes=60 << 20
        ),
    )(
        start_state,
        right_side,
        block_inverse,
        lifted_flux_jacobian.swapaxes(1, 2),
        face_weight,
        dep_level.reshape(1, EL),
        face_link,
        send_list,
        recv_list,
    )
    return pl.pallas_call(
        hand_on,
        out_shape=(out, out),
        in_specs=[vmem, vmem],
        out_specs=(hbm, hbm),
        scratch_shapes=[pltpu.SemaphoreType.DMA((2,))],
    )(first, second)


def solution(mesh):
    return jax.shard_map(
        body,
        mesh=mesh,
        in_specs=(
            P(None, ("curve", "slab")),
            P(None, ("curve", "slab")),
            P(None, None, ("curve", "slab")),
            P(),
            P(None, ("curve", "slab")),
            P(("curve", "slab")),
            P(None, ("curve", "slab")),
            P(None, ("curve", "slab")),
            P(None, ("curve", "slab")),
        ),
        out_specs=(P(None, ("curve", "slab")), P(None, ("curve", "slab"))),
        check_vma=False,
    )
```

```python
import functools

import jax
import jax.numpy as jnp
from jax import lax
from jax.experimental import pallas as pl
from jax.experimental.pallas import tpu as pltpu
from jax.sharding import PartitionSpec as P

VARS = 5
TRACE = 45
BLOCK = 135
EL = 128
LEVELS = 8
CAP = 4
PAD = 64
GROUPS = 12
ROWS = 8 * GROUPS
FAR, OWN, PAIR = range(3)
LATE = ((FAR, 2), (FAR, 1), (FAR, 3), (FAR, 0), (OWN, 2), (PAIR, 2))
EARLY = ((OWN, 1), (OWN, 3), (PAIR, 1), (PAIR, 3), (PAIR, 0), (OWN, 0))
PLACES = {key: at for at, key in enumerate(LATE + EARLY)}
HALF = 8 * len(LATE)
STACK = 144
MESH = pl.DeviceIdType.MESH
F32 = jnp.float32
BF16 = jnp.bfloat16


def split(x):
    hi = x.astype(BF16)
    lo = (x - hi.astype(F32)).astype(BF16)
    return hi, lo


def dot(a, b):
    return lax.dot_general(a, b, (((1,), (0,)), ((), ())), preferred_element_type=F32)


def dot_t(a, b):
    return lax.dot_general(a, b, (((1,), (1,)), ((), ())), preferred_element_type=F32)


def kernel(
    start_hbm,
    right_hbm,
    inverse_hbm,
    jac_hbm,
    weight_hbm,
    level_hbm,
    link_hbm,
    send_hbm,
    recv_hbm,
    forward_ref,
    swept_ref,
    right_ref,
    jac_ref,
    weight_ref,
    level_ref,
    link_ref,
    send_ref,
    recv_ref,
    inverse,
    state,
    table,
    solve_in,
    update,
    jac,
    jac2,
    jac3,
    links,
    picks,
    drops,
    late_drops,
    late_lane,
    early_flow,
    late_spread,
    late_chosen,
    late_part,
    factors,
    total,
    index,
    out_buf,
    in_buf,
    sent,
    first_out,
    first_in,
    first_drops,
    first_factors,
    input_sems,
    send_sem,
    recv_sem,
    first_send_sem,
    first_recv_sem,
):
    curves = lax.axis_size("curve")
    slabs = lax.axis_size("slab")
    my_curve = lax.axis_index("curve")
    my_slab = lax.axis_index("slab")
    odd = lax.rem(my_curve, 2)
    far_curve = my_curve + 2 * odd - 1
    pair_curve = my_curve + 1 - 2 * odd
    has_far = jnp.logical_and(far_curve >= 0, far_curve < curves)
    kind_curve = (far_curve, my_curve, pair_curve)
    here = PLACES[OWN, 0]

    pulls = [
        pltpu.make_async_copy(source, target, input_sems.at[at])
        for at, (source, target) in enumerate(
            (
                (start_hbm, state),
                (send_hbm, send_ref),
                (recv_hbm, recv_ref),
                (jac_hbm, jac_ref),
                (weight_hbm, weight_ref),
                (link_hbm, link_ref),
                (right_hbm, right_ref),
                (level_hbm, level_ref),
                (inverse_hbm, inverse),
            )
        )
    ]
    for pull in pulls:
        pull.start()

    @pl.when(jnp.logical_not(has_far))
    def _():
        in_buf[:, :4] = jnp.zeros((2, 4, 8, EL), F32)
        first_in[:, :4] = jnp.zeros((LEVELS // 2, 4, 8, EL), F32)

    def each_late(act):
        @pl.when(has_far)
        def _():
            for kind, shift in LATE[:4]:
                act(kind, shift)

        for kind, shift in LATE[4:]:
            act(kind, shift)

    def each_early(act):
        for kind, shift in EARLY[:-1]:
            act(kind, shift)

    def each_peer(act):
        each_late(act)
        each_early(act)

    def device(kind, shift):
        return (kind_curve[kind], lax.rem(my_slab + shift, slabs))

    barrier = pltpu.get_barrier_semaphore()
    each_peer(
        lambda kind, shift: pl.semaphore_signal(
            barrier, inc=1, device_id=device(kind, shift), device_id_type=MESH
        )
    )

    lane = lax.broadcasted_iota(jnp.int32, (ROWS, EL), 1)

    def to_rows(list_ref):
        shift = lax.rem((curves + 1 - my_curve) * (slabs * CAP), curves * slabs * CAP)
        near = pltpu.roll(list_ref[...], shift, 1)[:, :EL]
        tall = jnp.concatenate([near] * 16, axis=0).T
        step = slabs * CAP
        low, mid, high = (tall[step * k : step * (k + 1), :] for k in range(3))
        ordered = (jnp.where(odd == 1, high, low), mid, jnp.where(odd == 1, low, high))
        for kind in range(3):
            block = ordered[kind]
            turned = block
            for z in range(1, slabs):
                other = jnp.concatenate([block[CAP * z :], block[: CAP * z]], axis=0)
                turned = jnp.where(my_slab == z, other, turned)
            for shift in range(slabs):
                group = PLACES[kind, shift]
                four = turned[CAP * shift : CAP * (shift + 1), :]
                index[8 * group : 8 * group + CAP, :] = four
                index[8 * group + CAP : 8 * group + 8, :] = four

    table[...] = jnp.zeros_like(table)

    def fill_table():
        for side in range(2):
            for q in range(9):
                table[side, pl.ds(q, VARS, stride=9), :] = state[
                    pl.ds(18 * side + q, VARS, stride=27), :
                ]
            for q in range(3):
                table[2 + side, pl.ds(q, 15, stride=3), :] = state[
                    pl.ds(6 * side + q, 15, stride=9), :
                ]
            table[4 + side, :TRACE, :] = state[pl.ds(2 * side, TRACE, stride=3), :]

    for pull in pulls[:2]:
        pull.wait()
    fill_table()
    to_rows(send_ref)
    for level in range(LEVELS):
        column = index[:, level : level + 1]
        for face in range(6):
            picks[level, :, EL * face : EL * (face + 1)] = (
                jnp.where(column == lane + EL * face, 1.0, 0.0).astype(BF16)
            )

    def packed(level):
        hi, lo = split(jnp.concatenate([table[face] for face in range(6)], axis=1))
        halves = dot_t(picks[level], jnp.concatenate([hi, lo], axis=0))
        return halves + pltpu.roll(halves, PAD, 1)

    first_half = lax.broadcasted_iota(jnp.int32, (ROWS, EL), 0) % 8 < CAP
    for duo in range(LEVELS // 2):
        even, after = packed(2 * duo), packed(2 * duo + 1)
        sent[2 * duo] = even.reshape(GROUPS, 8, EL)
        sent[2 * duo + 1] = after.reshape(GROUPS, 8, EL)
        first_out[duo] = jnp.where(first_half, even, after).reshape(GROUPS, 8, EL)

    @pl.when(has_far)
    def _():
        pl.semaphore_wait(barrier, 3 * slabs - 1)

    @pl.when(jnp.logical_not(has_far))
    def _():
        pl.semaphore_wait(barrier, 2 * slabs - 1)

    def first_copy(kind, shift):
        source = PLACES[kind, shift]
        target = PLACES[kind, (4 - shift) % 4]
        return pltpu.make_async_remote_copy(
            src_ref=first_out.at[:, source],
            dst_ref=first_in.at[:, target],
            send_sem=first_send_sem.at[source],
            recv_sem=first_recv_sem.at[target],
            device_id=device(kind, shift),
            device_id_type=MESH,
        )

    def first_arrival(kind, shift):
        place = PLACES[kind, shift]
        return pltpu.make_async_remote_copy(
            src_ref=first_out.at[:, place],
            dst_ref=first_in.at[:, place],
            send_sem=first_send_sem.at[place],
            recv_sem=first_recv_sem.at[place],
            device_id=device(kind, shift),
            device_id_type=MESH,
        )

    def copy(slot, kind, shift):
        source = PLACES[kind, shift]
        target = PLACES[kind, (4 - shift) % 4]
        return pltpu.make_async_remote_copy(
            src_ref=out_buf.at[slot, source],
            dst_ref=in_buf.at[slot, target],
            send_sem=send_sem.at[slot, source],
            recv_sem=recv_sem.at[slot, target],
            device_id=device(kind, shift),
            device_id_type=MESH,
        )

    def arrival(slot, kind, shift):
        place = PLACES[kind, shift]
        return pltpu.make_async_remote_copy(
            src_ref=out_buf.at[slot, place],
            dst_ref=in_buf.at[slot, place],
            send_sem=send_sem.at[slot, place],
            recv_sem=recv_sem.at[slot, place],
            device_id=device(kind, shift),
            device_id_type=MESH,
        )

    each_peer(lambda kind, shift: first_copy(kind, shift).start())
    first_in[:, here] = first_out[:, here]

    for pull in pulls[2:8]:
        pull.wait()
    jac[...] = jnp.zeros_like(jac)
    for face in range(6):
        jac[PAD * face : PAD * face + TRACE, :BLOCK] = jac_ref[face]
    width = 6 * PAD
    jac_hi, jac_lo = split(jac[...].T[:BLOCK])
    jac2[:BLOCK] = jac_hi
    jac2[BLOCK:STACK] = jnp.zeros((STACK - BLOCK, width), BF16)
    jac2[STACK : STACK + BLOCK] = jac_lo
    jac2[STACK + BLOCK :] = jnp.zeros((STACK - BLOCK, width), BF16)
    jac3[:, :width] = jac_hi
    jac3[:, width : 2 * width] = jac_lo
    jac3[:, 2 * width :] = jac_hi

    row = lax.broadcasted_iota(jnp.int32, (EL, EL), 0)
    for face in range(6):
        one = jnp.where(link_ref[face : face + 1, :] == row, 1.0, 0.0).astype(BF16)
        links[face, :EL, :] = one
        links[face, EL:, :] = one

    def tiled(rows):
        low = lax.broadcasted_iota(jnp.int32, (8, rows.shape[1]), 0) < CAP
        mixed = [
            jnp.where(low, rows[16 * k : 16 * k + 8], rows[16 * k + 8 : 16 * k + 16])
            for k in range(3)
        ]
        return jnp.concatenate([rows, rows, *mixed, jnp.zeros_like(mixed[0])], axis=0)

    to_rows(recv_ref)
    face_lane = lax.broadcasted_iota(jnp.int32, (ROWS, width), 1) // PAD
    wide_half = lax.broadcasted_iota(jnp.int32, (ROWS, width), 0) % 8 < CAP
    for level in range(LEVELS):
        column = index[:, level : level + 1]
        hit = jnp.zeros((ROWS, EL), F32)
        gain = jnp.zeros((ROWS, EL), F32)
        for face in range(6):
            mine = column == lane + EL * face
            hit = jnp.where(mine, 1.0, hit)
            gain = jnp.where(mine, weight_ref[face : face + 1, :], gain)
        drops[level] = jnp.where(first_half, hit, 0.0).astype(BF16)
        late_drops[level] = tiled(hit[:HALF]).astype(BF16)
        scale = jnp.sum(gain, axis=1, keepdims=True)
        factor = jnp.where(column // EL == face_lane, scale, 0.0)
        factors[level] = factor
        if level % 2 == 1:
            first_drops[level // 2] = jnp.where(first_half, even_hit, hit).astype(BF16)
            first_factors[level // 2] = jnp.where(wide_half, even_factor, factor)
        even_hit, even_factor = hit, factor
    late_lane[...] = (tiled(index[:HALF, :]).T)[:8] % EL

    def local_flow():
        parts_hi = []
        parts_lo = []
        for face in range(6):
            other = face + 1 - 2 * (face % 2)
            hi, lo = split(table[other])
            moved = dot(jnp.concatenate([hi, lo], axis=1), links[face])
            hi, lo = split(moved * weight_ref[face : face + 1, :])
            parts_hi.append(hi)
            parts_lo.append(lo)
        hi = jnp.concatenate(parts_hi, axis=0)
        lo = jnp.concatenate(parts_lo, axis=0)
        return dot(jac3[...], jnp.concatenate([hi, hi, lo], axis=0))

    def scattered(values, where_to):
        hi, lo = split(values)
        return dot(
            jnp.concatenate([hi, lo], axis=1), jnp.concatenate([where_to, where_to], axis=0)
        )

    def spread(block, factor, tile=lambda rows: rows):
        hi, lo = split(tile(jnp.concatenate([block] * 3, axis=1) * factor))
        both = dot_t(jac2[...], hi)
        return both[:BLOCK] + both[STACK : STACK + BLOCK] + dot_t(jac2[:BLOCK], lo)

    def first_flow(low, high):
        count = LEVELS // 2 * (high - low) * 8
        block = first_in[:, low:high].reshape(count, EL)
        values = spread(block, first_factors[:, 8 * low : 8 * high].reshape(count, width))
        return scattered(values, first_drops[:, 8 * low : 8 * high].reshape(count, EL))

    known = right_ref[...] - local_flow()

    chunk = 135

    lanes8 = lax.broadcasted_iota(jnp.int32, (8, EL), 1)
    tile_at = lanes8 // 8
    second = (lanes8 // 4) % 2
    place_of = jnp.where(tile_at < 12, 2 * (tile_at // 6) + second, jnp.where(tile_at < 15, 4, 7))
    def merged(pieces, place):
        got = pieces[0]
        for part in range(1, len(pieces)):
            got = jnp.where(place == part, pieces[part], got)
        return got

    def tail_of(values):
        return jnp.concatenate([values, jnp.zeros((136 - BLOCK, EL), F32)], axis=0)

    def choose(level):
        where_from = jnp.broadcast_to(late_lane[pl.ds(level, 1), :], (8, EL))

        def moved(values):
            return jnp.take_along_axis(values, where_from, axis=1)

        def rows(at, carry):
            for k in range(chunk):
                i = at * chunk + k
                for m in range(3):
                    late_chosen[level, i, 8 * m : 8 * m + 8, :] = merged(
                        [
                            moved(inverse[i, 8 * b : 8 * b + 8, :])
                            for b in range(5 * m, 5 * m + 5)
                        ],
                        place_of,
                    )
                late_chosen[level, i, 24:32, :] = merged(
                    [moved(inverse[i, 120:128, :]), moved(tail_of(inverse[i, 128:BLOCK, :]))],
                    place_of,
                )
            return carry

        lax.fori_loop(0, BLOCK // chunk, rows, 0)

    def fold(values):
        pieces = [
            merged([values[8 * b : 8 * b + 8] for b in range(5 * m, 5 * m + 5)], place_of)
            for m in range(3)
        ]
        last = merged([values[120:128], tail_of(values[128:BLOCK])], place_of)
        pieces.append(jnp.where(place_of < 2, last, 0.0))
        return jnp.concatenate(pieces, axis=0)

    at8 = lax.broadcasted_iota(jnp.int32, (8, EL), 0)

    def gathered_sums(parts):
        top = at8 < 4
        fours = [
            jnp.where(top, parts[k], parts[k + 4])
            + pltpu.roll(jnp.where(top, parts[k + 4], parts[k]), 4, 0)
            for k in range(4)
        ]
        top = at8 % 4 < 2
        twos = [
            jnp.where(
                top,
                fours[k] + pltpu.roll(fours[k], 6, 0),
                fours[k + 2] + pltpu.roll(fours[k + 2], 2, 0),
            )
            for k in range(2)
        ]
        return jnp.where(
            at8 % 2 < 1, twos[0] + pltpu.roll(twos[0], 7, 0), twos[1] + pltpu.roll(twos[1], 1, 0)
        )

    def products(matrix, i, tiles):
        got = None
        for m, tile in enumerate(tiles):
            one = matrix[i, 8 * m : 8 * m + 8, :] * tile
            got = one if got is None else got + one
        return got

    def part_multiply(matrix, vector, target):
        tiles = [vector[8 * m : 8 * m + 8] for m in range(4)]

        def rows(at, carry):
            for k in range(16):
                g = at * 16 + k
                target[pl.ds(pl.multiple_of(8 * g, 8), 8), :] = gathered_sums(
                    [products(matrix, 8 * g + r, tiles) for r in range(8)]
                )
            return carry

        rows(0, 0)
        last = [products(matrix, 128 + r, tiles) for r in range(BLOCK - 128)]
        target[128:BLOCK, :] = gathered_sums(last + [jnp.zeros((8, EL), F32)])[: BLOCK - 128]

    def multiply():
        vector = solve_in[...]
        tiles = [vector[8 * m : 8 * m + 8] for m in range(16)]
        last_tile = tail_of(vector[128:BLOCK])

        def sums(i):
            last = tail_of(inverse[i, 128:BLOCK, :]) * last_tile
            return products(inverse, i, tiles) + last

        def rows(at, carry):
            for k in range(8):
                g = at * 8 + k
                update[pl.ds(pl.multiple_of(8 * g, 8), 8), :] = gathered_sums(
                    [sums(8 * g + r) for r in range(8)]
                )
            return carry

        lax.fori_loop(0, 2, rows, 0)
        last = [sums(128 + r) for r in range(BLOCK - 128)]
        update[128:BLOCK, :] = gathered_sums(last + [jnp.zeros((8, EL), F32)])[: BLOCK - 128]

    def level_of(step):
        return jnp.where(step < LEVELS, step, 2 * LEVELS - 1 - step)

    pulls[8].wait()
    choose(0)
    each_early(lambda kind, shift: first_arrival(kind, shift).wait_recv())
    ghost = first_flow(len(LATE), GROUPS)
    each_late(lambda kind, shift: first_arrival(kind, shift).wait_recv())
    ghost = ghost + first_flow(0, len(LATE))
    total[...] = ghost
    solve_in[...] = known - ghost
    each_peer(lambda kind, shift: first_arrival(kind, shift).wait_send())
    multiply()
    state[...] = jnp.where(level_ref[...] == 0, update[...], state[...])

    def level_step(step, carry):
        level = level_of(step)
        slot = lax.rem(step, 2)

        fill_table()
        fresh = packed(level).reshape(GROUPS, 8, EL)
        out_buf[slot] = fresh - sent[level]
        each_peer(lambda kind, shift: copy(slot, kind, shift).start())
        sent[level] = fresh
        in_buf[slot, here] = out_buf[slot, here]

        @pl.when(step >= 1)
        def _():
            each_peer(lambda kind, shift: arrival(1 - slot, kind, shift).wait_send())

        @pl.when(step == LEVELS - 1)
        def _():
            forward_ref[...] = state[...]

        @pl.when(step > 0)
        def _():
            before = level_of(step - 1)
            once = jnp.where(place_of[:1] == 0, late_spread[...], 0.0)
            total[...] = total[...] + early_flow[...] + scattered(once, late_drops[before])

        solve_in[...] = right_ref[...] - local_flow() - total[...]
        @pl.when(step < LEVELS - 1)
        def _():
            choose(level + 1)

        each_early(lambda kind, shift: arrival(slot, kind, shift).wait_recv())
        block = in_buf[slot, len(LATE) :].reshape(HALF, EL)
        flow = scattered(spread(block, factors[level, HALF:]), drops[level, HALF:])
        early_flow[...] = flow
        solve_in[...] = solve_in[...] - flow
        multiply()
        each_late(lambda kind, shift: arrival(slot, kind, shift).wait_recv())
        block = in_buf[slot, : len(LATE)].reshape(HALF, EL)
        values = spread(block, factors[level, :HALF], tiled)
        late_spread[...] = values
        part_multiply(late_chosen.at[level], fold(values), late_part)
        fresh = update[...] - scattered(late_part[...], late_drops[level])
        state[...] = jnp.where(level_ref[...] == level_of(step + 1), fresh, state[...])
        return carry

    lax.fori_loop(0, 2 * LEVELS - 1, level_step, 0)
    swept_ref[...] = state[...]
    each_peer(lambda kind, shift: arrival(0, kind, shift).wait_send())


def hand_on(first_ref, second_ref, first_out, second_out, sems):
    copies = (
        pltpu.make_async_copy(first_ref, first_out, sems.at[0]),
        pltpu.make_async_copy(second_ref, second_out, sems.at[1]),
    )
    for one in copies:
        one.start()
    for one in copies:
        one.wait()


def body(
    start_state,
    right_side,
    block_inverse,
    lifted_flux_jacobian,
    face_weight,
    dep_level,
    face_link,
    send_list,
    recv_list,
):
    vmem = pl.BlockSpec(memory_space=pltpu.VMEM)
    out = jax.ShapeDtypeStruct((BLOCK, EL), F32)
    width = 6 * PAD
    lists = send_list.shape[1]
    hbm = pl.BlockSpec(memory_space=pl.ANY)
    first, second = pl.pallas_call(
        kernel,
        out_shape=(out, out),
        in_specs=[hbm] * 9,
        out_specs=(vmem, vmem),
        scratch_shapes=[
            pltpu.VMEM((BLOCK, EL), F32),
            pltpu.VMEM((6, TRACE, BLOCK), F32),
            pltpu.VMEM((6, EL), F32),
            pltpu.VMEM((1, EL), jnp.int32),
            pltpu.VMEM((6, EL), jnp.int32),
            pltpu.VMEM((LEVELS, lists), jnp.int32),
            pltpu.VMEM((LEVELS, lists), jnp.int32),
            pltpu.VMEM((BLOCK, BLOCK, EL), F32),
            pltpu.VMEM((BLOCK, EL), F32),
            pltpu.VMEM((6, PAD, EL), F32),
            pltpu.VMEM((BLOCK, EL), F32),
            pltpu.VMEM((BLOCK, EL), F32),
            pltpu.VMEM((width, 256), F32),
            pltpu.VMEM((2 * STACK, width), BF16),
            pltpu.VMEM((BLOCK, 3 * width), BF16),
            pltpu.VMEM((6, 2 * EL, EL), BF16),
            pltpu.VMEM((LEVELS, ROWS, 6 * EL), BF16),
            pltpu.VMEM((LEVELS, ROWS, EL), BF16),
            pltpu.VMEM((LEVELS, EL, EL), BF16),
            pltpu.VMEM((8, EL), jnp.int32),
            pltpu.VMEM((BLOCK, EL), F32),
            pltpu.VMEM((BLOCK, EL), F32),
            pltpu.VMEM((LEVELS, BLOCK, 32, EL), F32),
            pltpu.VMEM((BLOCK, EL), F32),
            pltpu.VMEM((LEVELS, ROWS, width), F32),
            pltpu.VMEM((BLOCK, EL), F32),
            pltpu.VMEM((ROWS, EL), jnp.int32),
            pltpu.VMEM((2, GROUPS, 8, EL), F32),
            pltpu.VMEM((2, GROUPS, 8, EL), F32),
            pltpu.VMEM((LEVELS, GROUPS, 8, EL), F32),
            pltpu.VMEM((LEVELS // 2, GROUPS, 8, EL), F32),
            pltpu.VMEM((LEVELS // 2, GROUPS, 8, EL), F32),
            pltpu.VMEM((LEVELS // 2, ROWS, EL), BF16),
            pltpu.VMEM((LEVELS // 2, ROWS, width), F32),
            pltpu.SemaphoreType.DMA((9,)),
            pltpu.SemaphoreType.DMA((2, GROUPS)),
            pltpu.SemaphoreType.DMA((2, GROUPS)),
            pltpu.SemaphoreType.DMA((GROUPS,)),
            pltpu.SemaphoreType.DMA((GROUPS,)),
        ],
        compiler_params=pltpu.CompilerParams(
            collective_id=0, has_side_effects=True, vmem_limit_bytes=60 << 20
        ),
    )(
        start_state,
        right_side,
        block_inverse,
        lifted_flux_jacobian.swapaxes(1, 2),
        face_weight,
        dep_level.reshape(1, EL),
        face_link,
        send_list,
        recv_list,
    )
    return pl.pallas_call(
        hand_on,
        out_shape=(out, out),
        in_specs=[vmem, vmem],
        out_specs=(hbm, hbm),
        scratch_shapes=[pltpu.SemaphoreType.DMA((2,))],
    )(first, second)


def solution(mesh):
    return jax.shard_map(
        body,
        mesh=mesh,
        in_specs=(
            P(None, ("curve", "slab")),
            P(None, ("curve", "slab")),
            P(None, None, ("curve", "slab")),
            P(),
            P(None, ("curve", "slab")),
            P(("curve", "slab")),
            P(None, ("curve", "slab")),
            P(None, ("curve", "slab")),
            P(None, ("curve", "slab")),
        ),
        out_specs=(P(None, ("curve", "slab")), P(None, ("curve", "slab"))),
        check_vma=False,
    )
```

```python
import functools

import jax
import jax.numpy as jnp
from jax import lax
from jax.experimental import pallas as pl
from jax.experimental.pallas import tpu as pltpu
from jax.sharding import PartitionSpec as P

VARS = 5
TRACE = 45
BLOCK = 135
EL = 128
LEVELS = 8
CAP = 4
PAD = 64
GROUPS = 12
ROWS = 8 * GROUPS
FAR, OWN, PAIR = range(3)
LATE = ((FAR, 2), (FAR, 1), (FAR, 3), (FAR, 0), (OWN, 2), (PAIR, 2))
EARLY = ((OWN, 1), (OWN, 3), (PAIR, 1), (PAIR, 3), (PAIR, 0), (OWN, 0))
PLACES = {key: at for at, key in enumerate(LATE + EARLY)}
HALF = 8 * len(LATE)
STACK = 144
MESH = pl.DeviceIdType.MESH
F32 = jnp.float32
BF16 = jnp.bfloat16


def split(x):
    hi = x.astype(BF16)
    lo = (x - hi.astype(F32)).astype(BF16)
    return hi, lo


def dot(a, b):
    return lax.dot_general(a, b, (((1,), (0,)), ((), ())), preferred_element_type=F32)


def dot_t(a, b):
    return lax.dot_general(a, b, (((1,), (1,)), ((), ())), preferred_element_type=F32)


def kernel(
    start_hbm,
    right_hbm,
    inverse_hbm,
    jac_hbm,
    weight_hbm,
    level_hbm,
    link_hbm,
    send_hbm,
    recv_hbm,
    forward_ref,
    swept_ref,
    right_ref,
    jac_ref,
    weight_ref,
    level_ref,
    link_ref,
    send_ref,
    recv_ref,
    inverse,
    state,
    table,
    solve_in,
    update,
    jac,
    jac2,
    jac3,
    links,
    picks,
    drops,
    late_drops,
    late_lane,
    early_flow,
    late_spread,
    late_chosen,
    late_part,
    factors,
    total,
    index,
    out_buf,
    in_buf,
    sent,
    first_out,
    first_in,
    first_drops,
    first_factors,
    input_sems,
    send_sem,
    recv_sem,
):
    curves = lax.axis_size("curve")
    slabs = lax.axis_size("slab")
    my_curve = lax.axis_index("curve")
    my_slab = lax.axis_index("slab")
    odd = lax.rem(my_curve, 2)
    far_curve = my_curve + 2 * odd - 1
    pair_curve = my_curve + 1 - 2 * odd
    has_far = jnp.logical_and(far_curve >= 0, far_curve < curves)
    kind_curve = (far_curve, my_curve, pair_curve)
    here = PLACES[OWN, 0]

    pulls = [
        pltpu.make_async_copy(source, target, input_sems.at[at])
        for at, (source, target) in enumerate(
            (
                (start_hbm, state),
                (send_hbm, send_ref),
                (recv_hbm, recv_ref),
                (jac_hbm, jac_ref),
                (weight_hbm, weight_ref),
                (link_hbm, link_ref),
                (right_hbm, right_ref),
                (level_hbm, level_ref),
                (inverse_hbm, inverse),
            )
        )
    ]
    for pull in pulls:
        pull.start()

    @pl.when(jnp.logical_not(has_far))
    def _():
        in_buf[:, :4] = jnp.zeros((2, 4, 8, EL), F32)
        first_in[:, :4] = jnp.zeros((LEVELS // 2, 4, 8, EL), F32)

    def each_late(act):
        @pl.when(has_far)
        def _():
            for kind, shift in LATE[:4]:
                act(kind, shift)

        for kind, shift in LATE[4:]:
            act(kind, shift)

    def each_early(act):
        for kind, shift in EARLY[:-1]:
            act(kind, shift)

    def each_peer(act):
        each_late(act)
        each_early(act)

    def device(kind, shift):
        return (kind_curve[kind], lax.rem(my_slab + shift, slabs))

    barrier = pltpu.get_barrier_semaphore()
    each_peer(
        lambda kind, shift: pl.semaphore_signal(
            barrier, inc=1, device_id=device(kind, shift), device_id_type=MESH
        )
    )

    lane = lax.broadcasted_iota(jnp.int32, (ROWS, EL), 1)

    def to_rows(list_ref):
        shift = lax.rem((curves + 1 - my_curve) * (slabs * CAP), curves * slabs * CAP)
        near = pltpu.roll(list_ref[...], shift, 1)[:, :EL]
        tall = jnp.concatenate([near] * 16, axis=0).T
        step = slabs * CAP
        low, mid, high = (tall[step * k : step * (k + 1), :] for k in range(3))
        ordered = (jnp.where(odd == 1, high, low), mid, jnp.where(odd == 1, low, high))
        for kind in range(3):
            block = ordered[kind]
            turned = block
            for z in range(1, slabs):
                other = jnp.concatenate([block[CAP * z :], block[: CAP * z]], axis=0)
                turned = jnp.where(my_slab == z, other, turned)
            for shift in range(slabs):
                group = PLACES[kind, shift]
                four = turned[CAP * shift : CAP * (shift + 1), :]
                index[8 * group : 8 * group + CAP, :] = four
                index[8 * group + CAP : 8 * group + 8, :] = four

    table[...] = jnp.zeros_like(table)

    def fill_table():
        for side in range(2):
            for q in range(9):
                table[side, pl.ds(q, VARS, stride=9), :] = state[
                    pl.ds(18 * side + q, VARS, stride=27), :
                ]
            for q in range(3):
                table[2 + side, pl.ds(q, 15, stride=3), :] = state[
                    pl.ds(6 * side + q, 15, stride=9), :
                ]
            table[4 + side, :TRACE, :] = state[pl.ds(2 * side, TRACE, stride=3), :]

    for pull in pulls[:2]:
        pull.wait()
    fill_table()
    to_rows(send_ref)
    for level in range(LEVELS):
        column = index[:, level : level + 1]
        for face in range(6):
            picks[level, :, EL * face : EL * (face + 1)] = (
                jnp.where(column == lane + EL * face, 1.0, 0.0).astype(BF16)
            )

    def packed(level):
        hi, lo = split(jnp.concatenate([table[face] for face in range(6)], axis=1))
        halves = dot_t(picks[level], jnp.concatenate([hi, lo], axis=0))
        return halves + pltpu.roll(halves, PAD, 1)

    first_half = lax.broadcasted_iota(jnp.int32, (ROWS, EL), 0) % 8 < CAP
    for duo in range(LEVELS // 2):
        even, after = packed(2 * duo), packed(2 * duo + 1)
        sent[2 * duo] = even.reshape(GROUPS, 8, EL)
        sent[2 * duo + 1] = after.reshape(GROUPS, 8, EL)
        first_out[duo] = jnp.where(first_half, even, after).reshape(GROUPS, 8, EL)

    @pl.when(has_far)
    def _():
        pl.semaphore_wait(barrier, 3 * slabs - 1)

    @pl.when(jnp.logical_not(has_far))
    def _():
        pl.semaphore_wait(barrier, 2 * slabs - 1)

    def first_copy(kind, shift):
        source = PLACES[kind, shift]
        target = PLACES[kind, (4 - shift) % 4]
        return pltpu.make_async_remote_copy(
            src_ref=first_out.at[:, source],
            dst_ref=first_in.at[:, target],
            send_sem=send_sem.at[1, source],
            recv_sem=recv_sem.at[1, target],
            device_id=device(kind, shift),
            device_id_type=MESH,
        )

    def first_arrival(kind, shift):
        place = PLACES[kind, shift]
        return pltpu.make_async_remote_copy(
            src_ref=first_out.at[:, place],
            dst_ref=first_in.at[:, place],
            send_sem=send_sem.at[1, place],
            recv_sem=recv_sem.at[1, place],
            device_id=device(kind, shift),
            device_id_type=MESH,
        )

    def copy(slot, kind, shift):
        source = PLACES[kind, shift]
        target = PLACES[kind, (4 - shift) % 4]
        return pltpu.make_async_remote_copy(
            src_ref=out_buf.at[slot, source],
            dst_ref=in_buf.at[slot, target],
            send_sem=send_sem.at[slot, source],
            recv_sem=recv_sem.at[slot, target],
            device_id=device(kind, shift),
            device_id_type=MESH,
        )

    def arrival(slot, kind, shift):
        place = PLACES[kind, shift]
        return pltpu.make_async_remote_copy(
            src_ref=out_buf.at[slot, place],
            dst_ref=in_buf.at[slot, place],
            send_sem=send_sem.at[slot, place],
            recv_sem=recv_sem.at[slot, place],
            device_id=device(kind, shift),
            device_id_type=MESH,
        )

    each_peer(lambda kind, shift: first_copy(kind, shift).start())
    first_in[:, here] = first_out[:, here]

    for pull in pulls[2:8]:
        pull.wait()
    jac[...] = jnp.zeros_like(jac)
    for face in range(6):
        jac[PAD * face : PAD * face + TRACE, :BLOCK] = jac_ref[face]
    width = 6 * PAD
    jac_hi, jac_lo = split(jac[...].T[:BLOCK])
    jac2[:BLOCK] = jac_hi
    jac2[BLOCK:STACK] = jnp.zeros((STACK - BLOCK, width), BF16)
    jac2[STACK : STACK + BLOCK] = jac_lo
    jac2[STACK + BLOCK :] = jnp.zeros((STACK - BLOCK, width), BF16)
    jac3[:, :width] = jac_hi
    jac3[:, width : 2 * width] = jac_lo
    jac3[:, 2 * width :] = jac_hi

    row = lax.broadcasted_iota(jnp.int32, (EL, EL), 0)
    for face in range(6):
        one = jnp.where(link_ref[face : face + 1, :] == row, 1.0, 0.0).astype(BF16)
        links[face, :EL, :] = one
        links[face, EL:, :] = one

    def tiled(rows):
        low = lax.broadcasted_iota(jnp.int32, (8, rows.shape[1]), 0) < CAP
        mixed = [
            jnp.where(low, rows[16 * k : 16 * k + 8], rows[16 * k + 8 : 16 * k + 16])
            for k in range(3)
        ]
        return jnp.concatenate([rows, rows, *mixed, jnp.zeros_like(mixed[0])], axis=0)

    to_rows(recv_ref)
    face_lane = lax.broadcasted_iota(jnp.int32, (ROWS, width), 1) // PAD
    wide_half = lax.broadcasted_iota(jnp.int32, (ROWS, width), 0) % 8 < CAP
    for level in range(LEVELS):
        column = index[:, level : level + 1]
        hit = jnp.zeros((ROWS, EL), F32)
        gain = jnp.zeros((ROWS, EL), F32)
        for face in range(6):
            mine = column == lane + EL * face
            hit = jnp.where(mine, 1.0, hit)
            gain = jnp.where(mine, weight_ref[face : face + 1, :], gain)
        drops[level] = jnp.where(first_half, hit, 0.0).astype(BF16)
        late_drops[level] = tiled(hit[:HALF]).astype(BF16)
        scale = jnp.sum(gain, axis=1, keepdims=True)
        factor = jnp.where(column // EL == face_lane, scale, 0.0)
        factors[level] = factor
        if level % 2 == 1:
            first_drops[level // 2] = jnp.where(first_half, even_hit, hit).astype(BF16)
            first_factors[level // 2] = jnp.where(wide_half, even_factor, factor)
        even_hit, even_factor = hit, factor
    late_lane[...] = (tiled(index[:HALF, :]).T)[:8] % EL

    def local_flow():
        parts_hi = []
        parts_lo = []
        for face in range(6):
            other = face + 1 - 2 * (face % 2)
            hi, lo = split(table[other])
            moved = dot(jnp.concatenate([hi, lo], axis=1), links[face])
            hi, lo = split(moved * weight_ref[face : face + 1, :])
            parts_hi.append(hi)
            parts_lo.append(lo)
        hi = jnp.concatenate(parts_hi, axis=0)
        lo = jnp.concatenate(parts_lo, axis=0)
        return dot(jac3[...], jnp.concatenate([hi, hi, lo], axis=0))

    def scattered(values, where_to):
        hi, lo = split(values)
        return dot(
            jnp.concatenate([hi, lo], axis=1), jnp.concatenate([where_to, where_to], axis=0)
        )

    def spread(block, factor, tile=lambda rows: rows):
        hi, lo = split(tile(jnp.concatenate([block] * 3, axis=1) * factor))
        both = dot_t(jac2[...], hi)
        return both[:BLOCK] + both[STACK : STACK + BLOCK] + dot_t(jac2[:BLOCK], lo)

    def first_flow(low, high):
        count = LEVELS // 2 * (high - low) * 8
        block = first_in[:, low:high].reshape(count, EL)
        values = spread(block, first_factors[:, 8 * low : 8 * high].reshape(count, width))
        return scattered(values, first_drops[:, 8 * low : 8 * high].reshape(count, EL))

    known = right_ref[...] - local_flow()

    chunk = 135

    lanes8 = lax.broadcasted_iota(jnp.int32, (8, EL), 1)
    tile_at = lanes8 // 8
    second = (lanes8 // 4) % 2
    place_of = jnp.where(tile_at < 12, 2 * (tile_at // 6) + second, jnp.where(tile_at < 15, 4, 7))
    def merged(pieces, place):
        got = pieces[0]
        for part in range(1, len(pieces)):
            got = jnp.where(place == part, pieces[part], got)
        return got

    def tail_of(values):
        return jnp.concatenate([values, jnp.zeros((136 - BLOCK, EL), F32)], axis=0)

    def choose(level):
        where_from = jnp.broadcast_to(late_lane[pl.ds(level, 1), :], (8, EL))

        def moved(values):
            return jnp.take_along_axis(values, where_from, axis=1)

        def rows(at, carry):
            for k in range(chunk):
                i = at * chunk + k
                for m in range(3):
                    late_chosen[level, i, 8 * m : 8 * m + 8, :] = merged(
                        [
                            moved(inverse[i, 8 * b : 8 * b + 8, :])
                            for b in range(5 * m, 5 * m + 5)
                        ],
                        place_of,
                    )
                late_chosen[level, i, 24:32, :] = merged(
                    [moved(inverse[i, 120:128, :]), moved(tail_of(inverse[i, 128:BLOCK, :]))],
                    place_of,
                )
            return carry

        lax.fori_loop(0, BLOCK // chunk, rows, 0)

    def fold(values):
        pieces = [
            merged([values[8 * b : 8 * b + 8] for b in range(5 * m, 5 * m + 5)], place_of)
            for m in range(3)
        ]
        last = merged([values[120:128], tail_of(values[128:BLOCK])], place_of)
        pieces.append(jnp.where(place_of < 2, last, 0.0))
        return jnp.concatenate(pieces, axis=0)

    at8 = lax.broadcasted_iota(jnp.int32, (8, EL), 0)

    def gathered_sums(parts):
        top = at8 < 4
        fours = [
            jnp.where(top, parts[k], parts[k + 4])
            + pltpu.roll(jnp.where(top, parts[k + 4], parts[k]), 4, 0)
            for k in range(4)
        ]
        top = at8 % 4 < 2
        twos = [
            jnp.where(
                top,
                fours[k] + pltpu.roll(fours[k], 6, 0),
                fours[k + 2] + pltpu.roll(fours[k + 2], 2, 0),
            )
            for k in range(2)
        ]
        return jnp.where(
            at8 % 2 < 1, twos[0] + pltpu.roll(twos[0], 7, 0), twos[1] + pltpu.roll(twos[1], 1, 0)
        )

    def products(matrix, i, tiles):
        got = None
        for m, tile in enumerate(tiles):
            one = matrix[i, 8 * m : 8 * m + 8, :] * tile
            got = one if got is None else got + one
        return got

    def part_multiply(matrix, vector, target):
        tiles = [vector[8 * m : 8 * m + 8] for m in range(4)]

        def rows(at, carry):
            for k in range(16):
                g = at * 16 + k
                target[pl.ds(pl.multiple_of(8 * g, 8), 8), :] = gathered_sums(
                    [products(matrix, 8 * g + r, tiles) for r in range(8)]
                )
            return carry

        rows(0, 0)
        last = [products(matrix, 128 + r, tiles) for r in range(BLOCK - 128)]
        target[128:BLOCK, :] = gathered_sums(last + [jnp.zeros((8, EL), F32)])[: BLOCK - 128]

    def multiply():
        vector = solve_in[...]
        tiles = [vector[8 * m : 8 * m + 8] for m in range(16)]
        last_tile = tail_of(vector[128:BLOCK])

        def sums(i):
            last = tail_of(inverse[i, 128:BLOCK, :]) * last_tile
            return products(inverse, i, tiles) + last

        def rows(at, carry):
            for k in range(8):
                g = at * 8 + k
                update[pl.ds(pl.multiple_of(8 * g, 8), 8), :] = gathered_sums(
                    [sums(8 * g + r) for r in range(8)]
                )
            return carry

        lax.fori_loop(0, 2, rows, 0)
        last = [sums(128 + r) for r in range(BLOCK - 128)]
        update[128:BLOCK, :] = gathered_sums(last + [jnp.zeros((8, EL), F32)])[: BLOCK - 128]

    def level_of(step):
        return jnp.where(step < LEVELS, step, 2 * LEVELS - 1 - step)

    pulls[8].wait()
    choose(0)
    each_early(lambda kind, shift: first_arrival(kind, shift).wait_recv())
    ghost = first_flow(len(LATE), GROUPS)
    each_late(lambda kind, shift: first_arrival(kind, shift).wait_recv())
    ghost = ghost + first_flow(0, len(LATE))
    total[...] = ghost
    solve_in[...] = known - ghost
    each_peer(lambda kind, shift: first_arrival(kind, shift).wait_send())
    multiply()
    state[...] = jnp.where(level_ref[...] == 0, update[...], state[...])

    def level_step(step, carry):
        level = level_of(step)
        slot = lax.rem(step, 2)

        fill_table()
        fresh = packed(level).reshape(GROUPS, 8, EL)
        out_buf[slot] = fresh - sent[level]
        each_peer(lambda kind, shift: copy(slot, kind, shift).start())
        sent[level] = fresh
        in_buf[slot, here] = out_buf[slot, here]

        @pl.when(step >= 1)
        def _():
            each_peer(lambda kind, shift: arrival(1 - slot, kind, shift).wait_send())

        @pl.when(step == LEVELS - 1)
        def _():
            forward_ref[...] = state[...]

        @pl.when(step > 0)
        def _():
            before = level_of(step - 1)
            once = jnp.where(place_of[:1] == 0, late_spread[...], 0.0)
            total[...] = total[...] + early_flow[...] + scattered(once, late_drops[before])

        solve_in[...] = right_ref[...] - local_flow() - total[...]
        @pl.when(step < LEVELS - 1)
        def _():
            choose(level + 1)

        each_early(lambda kind, shift: arrival(slot, kind, shift).wait_recv())
        block = in_buf[slot, len(LATE) :].reshape(HALF, EL)
        flow = scattered(spread(block, factors[level, HALF:]), drops[level, HALF:])
        early_flow[...] = flow
        solve_in[...] = solve_in[...] - flow
        multiply()
        each_late(lambda kind, shift: arrival(slot, kind, shift).wait_recv())
        block = in_buf[slot, : len(LATE)].reshape(HALF, EL)
        values = spread(block, factors[level, :HALF], tiled)
        late_spread[...] = values
        part_multiply(late_chosen.at[level], fold(values), late_part)
        fresh = update[...] - scattered(late_part[...], late_drops[level])
        state[...] = jnp.where(level_ref[...] == level_of(step + 1), fresh, state[...])
        return carry

    lax.fori_loop(0, 2 * LEVELS - 1, level_step, 0)
    swept_ref[...] = state[...]
    each_peer(lambda kind, shift: arrival(0, kind, shift).wait_send())


def hand_on(first_ref, second_ref, first_out, second_out, sems):
    copies = (
        pltpu.make_async_copy(first_ref, first_out, sems.at[0]),
        pltpu.make_async_copy(second_ref, second_out, sems.at[1]),
    )
    for one in copies:
        one.start()
    for one in copies:
        one.wait()


def body(
    start_state,
    right_side,
    block_inverse,
    lifted_flux_jacobian,
    face_weight,
    dep_level,
    face_link,
    send_list,
    recv_list,
):
    vmem = pl.BlockSpec(memory_space=pltpu.VMEM)
    out = jax.ShapeDtypeStruct((BLOCK, EL), F32)
    width = 6 * PAD
    lists = send_list.shape[1]
    hbm = pl.BlockSpec(memory_space=pl.ANY)
    first, second = pl.pallas_call(
        kernel,
        out_shape=(out, out),
        in_specs=[hbm] * 9,
        out_specs=(vmem, vmem),
        scratch_shapes=[
            pltpu.VMEM((BLOCK, EL), F32),
            pltpu.VMEM((6, TRACE, BLOCK), F32),
            pltpu.VMEM((6, EL), F32),
            pltpu.VMEM((1, EL), jnp.int32),
            pltpu.VMEM((6, EL), jnp.int32),
            pltpu.VMEM((LEVELS, lists), jnp.int32),
            pltpu.VMEM((LEVELS, lists), jnp.int32),
            pltpu.VMEM((BLOCK, BLOCK, EL), F32),
            pltpu.VMEM((BLOCK, EL), F32),
            pltpu.VMEM((6, PAD, EL), F32),
            pltpu.VMEM((BLOCK, EL), F32),
            pltpu.VMEM((BLOCK, EL), F32),
            pltpu.VMEM((width, 256), F32),
            pltpu.VMEM((2 * STACK, width), BF16),
            pltpu.VMEM((BLOCK, 3 * width), BF16),
            pltpu.VMEM((6, 2 * EL, EL), BF16),
            pltpu.VMEM((LEVELS, ROWS, 6 * EL), BF16),
            pltpu.VMEM((LEVELS, ROWS, EL), BF16),
            pltpu.VMEM((LEVELS, EL, EL), BF16),
            pltpu.VMEM((8, EL), jnp.int32),
            pltpu.VMEM((BLOCK, EL), F32),
            pltpu.VMEM((BLOCK, EL), F32),
            pltpu.VMEM((LEVELS, BLOCK, 32, EL), F32),
            pltpu.VMEM((BLOCK, EL), F32),
            pltpu.VMEM((LEVELS, ROWS, width), F32),
            pltpu.VMEM((BLOCK, EL), F32),
            pltpu.VMEM((ROWS, EL), jnp.int32),
            pltpu.VMEM((2, GROUPS, 8, EL), F32),
            pltpu.VMEM((2, GROUPS, 8, EL), F32),
            pltpu.VMEM((LEVELS, GROUPS, 8, EL), F32),
            pltpu.VMEM((LEVELS // 2, GROUPS, 8, EL), F32),
            pltpu.VMEM((LEVELS // 2, GROUPS, 8, EL), F32),
            pltpu.VMEM((LEVELS // 2, ROWS, EL), BF16),
            pltpu.VMEM((LEVELS // 2, ROWS, width), F32),
            pltpu.SemaphoreType.DMA((9,)),
            pltpu.SemaphoreType.DMA((2, GROUPS)),
            pltpu.SemaphoreType.DMA((2, GROUPS)),
        ],
        compiler_params=pltpu.CompilerParams(
            collective_id=0, has_side_effects=True, vmem_limit_bytes=60 << 20
        ),
    )(
        start_state,
        right_side,
        block_inverse,
        lifted_flux_jacobian.swapaxes(1, 2),
        face_weight,
        dep_level.reshape(1, EL),
        face_link,
        send_list,
        recv_list,
    )
    return pl.pallas_call(
        hand_on,
        out_shape=(out, out),
        in_specs=[vmem, vmem],
        out_specs=(hbm, hbm),
        scratch_shapes=[pltpu.SemaphoreType.DMA((2,))],
    )(first, second)


def solution(mesh):
    return jax.shard_map(
        body,
        mesh=mesh,
        in_specs=(
            P(None, ("curve", "slab")),
            P(None, ("curve", "slab")),
            P(None, None, ("curve", "slab")),
            P(),
            P(None, ("curve", "slab")),
            P(("curve", "slab")),
            P(None, ("curve", "slab")),
            P(None, ("curve", "slab")),
            P(None, ("curve", "slab")),
        ),
        out_specs=(P(None, ("curve", "slab")), P(None, ("curve", "slab"))),
        check_vma=False,
    )
```
